256 devices in a mesh: dom: 32 (over y, x, core), tp: 8 (over z).
Axes of the slice: x: 4, y: 4, z: 8, core: 2. Of those that a mesh axis runs over, the one named last changes fastest.
Arguments:
- activations: bfloat16 [4, 512, 4096], P(None, 'dom', 'tp'), may hold values from -6 to 6
- norm_gain: float32 [4096], replicated, may hold values from 0.5 to 1.5
- w_query: bfloat16 [4096, 4096], P(None, 'tp'), may hold values from -0.09375 to 0.09375
- w_key: bfloat16 [4096, 1024], P(None, 'tp'), may hold values from -0.09375 to 0.09375
- value_weight: bfloat16 [4096, 1024], P(None, 'tp'), may hold values from -0.5 to 0.5
- w_output: bfloat16 [4096, 4096], P('tp'), may hold values from -0.09375 to 0.09375
- cache_keys: bfloat16 [512, 128, 1024], P('dom', None, 'tp'), may hold values from -740 to 740
- cache_values: bfloat16 [512, 128, 1024], P('dom', None, 'tp'), may hold values from -48 to 48
- tokens: int32 [4, 512], P(None, 'dom'), may hold values from 0 to 128255
- twisting_table: bfloat16 [128256], replicated, may hold values from -6 to 6
- twist_vec: float32 [4096], P('tp'), may hold values from -0.09375 to 0.09375
- previous_log_weights: float32 [512], P('dom'), may hold values from -300 to 0
- copy_counts: int32 [512], P('dom'), may hold values from 0 to 4, as said below
Outputs:
- attn_out: bfloat16 [4, 512, 4096], P(None, 'dom', 'tp')
- new_keys: bfloat16 [512, 132, 1024], P('dom', None, 'tp')
- new_values: bfloat16 [512, 132, 1024], P('dom', None, 'tp')
- out_logw: float32 [512], P('dom')
The draws below stay inside these ranges and needn't reach their ends.
Inputs may be any that keep to these rules, and one draw needn't show every extreme that they name: copy_counts sum to 512; the particles of one index of dom have together at most 64 copies, and one index has exactly that many.
All inputs are finite; a program needn't handle non-finite values.
Results may differ from the reference program's by a relative error of at most 0.012.
The reference program's roundings to bfloat16 on the way (of `normed`, `queries`, `fresh_keys`, `fresh_values`, `key_rows`, `weights` and `context`) count: a program that leaves them out, or rounds other values in their place, can miss the bound.
Values may be sent and summed in bfloat16 or wider, within the bound.
No kernel may reach another device: no remote copies, remote signals or barrier semaphores. Data moves between devices by JAX's collectives and lax.ppermute only.
A program may use at most 64 MiB of HBM per device.

```python
import math
import jax
import jax.numpy as jnp
import numpy as np
from jax import lax

D = 4096
QH = 32
KVH = 8
HD = 128
VOCAB = 128256
STEPS = 4
PART_DEV = 16
L = 128
PARTICLES = 512
N_DOM = 32


def draw_cache_keys(key, part):
    base_key = jax.random.fold_in(jax.random.fold_in(key, 11), 0)
    width = KVH * HD
    result = jnp.clip(jax.random.normal(base_key, (PARTICLES, L, width), jnp.float32), -4.5, 4.5)
    return result.astype(jnp.bfloat16)


def draw_previous_log_weights(key, part):
    result = jax.random.uniform(jax.random.fold_in(key, 23), (PARTICLES,), jnp.float32, -8.0, 0.0)
    return result


def draw_copy_counts(key, part):
    first_key, second_key = jax.random.split(jax.random.fold_in(key, 37), 2)
    devices = PARTICLES // PART_DEV
    slots_all = 4 * PARTICLES
    heavy_device = jax.random.randint(first_key, (), 0, devices)
    shuffle = jax.random.permutation(second_key, slots_all)
    owner_device = jnp.arange(slots_all, dtype=jnp.int32) // (4 * PART_DEV)
    lighter = (owner_device[shuffle] != heavy_device).astype(jnp.int32)
    running = jnp.cumsum(lighter)
    needed = (devices - 4) * PART_DEV
    picked_order = ((lighter == 1) & (running <= needed)).astype(jnp.int32)
    picked = jnp.zeros((slots_all,), jnp.int32).at[shuffle].set(picked_order)
    picked = jnp.maximum(picked, (owner_device == heavy_device).astype(jnp.int32))
    return jnp.sum(picked.reshape(PARTICLES, 4), 1).astype(jnp.int32)


def set_ends(values, stream_key, smallest, top_value):
    dims = values.shape
    place = [jax.random.randint(jax.random.fold_in(stream_key, axis), (), 0, dims[axis]) for axis in range(len(dims))]
    values = values.at[tuple(place)].set(smallest)
    longest = dims.index(max(dims))
    place[longest] = (place[longest] + 1) % dims[longest]
    return values.at[tuple(place)].set(top_value)


def block_levels(key, extent, cuts, smallest, top_value):
    gain = 1.0
    for dim, shards_of in cuts:
        heights = jax.random.uniform(jax.random.fold_in(jax.random.fold_in(key, 6), dim), (shards_of,), jnp.float32, smallest / len(cuts), top_value / len(cuts))
        gain = gain * jnp.repeat(jnp.exp(heights), extent[dim] // shards_of).reshape((-1,) + (1,) * (len(extent) - 1 - dim))
    return gain


def wide_ids(own_key, shape, number_of, lean):
    loads = [min(1 << octave, number_of + 1 - (1 << octave)) * (1 << 20) // math.isqrt((1 << octave) ** lean) + 1 for octave in range((number_of + 1).bit_length()) if 1 << octave <= number_of]
    scale = 1 + sum(loads) // (1 << 30)
    listing = np.cumsum(np.array([max(1, weight // scale) for weight in loads]))
    lot = jax.random.randint(jax.random.fold_in(own_key, 1), shape, 0, int(listing[len(loads) - 1]))
    start = jnp.left_shift(1, jnp.searchsorted(jnp.asarray(listing, jnp.int32), lot, side="right").astype(jnp.int32))
    rank = start - 1 + jax.random.randint(jax.random.fold_in(own_key, 4), shape, 0, 1 << 30) % jnp.minimum(start, number_of + 1 - start)
    return jax.random.permutation(jax.random.fold_in(own_key, 2), number_of)[rank].astype(jnp.int32)


def normal_values(key, shape, scale, reach, cuts=(), kind=jnp.bfloat16):
    values = jax.random.normal(key, shape, jnp.float32) * scale
    if len(cuts) > 0:
        values = block_levels(key, shape, cuts, -0.22, 0.18) * values
    return jnp.clip(values, min=-reach, max=reach).astype(kind)


def setup_inputs(seed: int = 0) -> dict:
    keys = jax.random.split(jax.random.key(seed), 14)
    return {
        "activations": normal_values(keys[0], (STEPS, PARTICLES, D), 1.0, 6.0, ((1, 32), (2, 8))),
        "norm_gain": jnp.clip(1.0 + 0.1 * jax.random.normal(keys[1], (D,), jnp.float32), 0.5, 1.5),
        "w_query": normal_values(keys[2], (D, QH * HD), D ** -0.5, 0.09375, ((1, 8),)),
        "w_key": normal_values(keys[3], (D, KVH * HD), D ** -0.5, 0.09375, ((1, 8),)),
        "value_weight": normal_values(keys[4], (D, KVH * HD), (D // 32) ** -0.5, 0.5, ((1, 8),)),
        "w_output": normal_values(keys[5], (QH * HD, D), (QH * HD) ** -0.5, 0.09375, ((0, 8),)),
        "cache_keys": draw_cache_keys(jax.random.fold_in(keys[13], 71), 0),
        "cache_values": normal_values(keys[7], (PARTICLES, L, KVH * HD), 8.0, 48.0, ((0, 32), (2, 8))),
        "tokens": set_ends(wide_ids(keys[8], (STEPS, PARTICLES), VOCAB, 2), jax.random.fold_in(keys[8], 3), 0, VOCAB - 1).astype(jnp.int32),
        "twisting_table": normal_values(keys[9], (VOCAB,), 1.0, 6.0),
        "twist_vec": normal_values(keys[10], (D,), D ** -0.5, 0.09375, ((0, 8),), jnp.float32),
        "previous_log_weights": draw_previous_log_weights(jax.random.fold_in(keys[13], 71), 0),
        "copy_counts": draw_copy_counts(jax.random.fold_in(keys[13], 71), 0),
    }


def rotate(tensor, positions):
    middle = tensor.shape[-1] // 2
    frequency = 500000.0 ** (-2.0 * jnp.arange(middle, dtype=jnp.float32) / tensor.shape[-1])
    angles = positions[:, None] * frequency[None, :]
    cosine = jnp.cos(angles)[:, None, None, :]
    sine_part = jnp.sin(angles)[:, None, None, :]
    lower_half = tensor[..., :middle]
    upper_half = tensor[..., middle:]
    return jnp.concatenate([lower_half * cosine - upper_half * sine_part, upper_half * cosine + lower_half * sine_part], -1)

def reference(activations, norm_gain, w_query, w_key, value_weight, w_output, cache_keys, cache_values, tokens, twisting_table, twist_vec, previous_log_weights, copy_counts):
    inputs = activations.astype(jnp.float32)
    normed = (inputs * lax.rsqrt(lax.optimization_barrier(jnp.mean(inputs * inputs, -1, keepdims=True)) + 1e-05) * norm_gain).astype(jnp.bfloat16)
    flat_rows = normed.reshape(STEPS * PARTICLES, D)
    positions = (L + jnp.arange(STEPS, dtype=jnp.int32)).astype(jnp.float32)
    queries = jnp.dot(flat_rows, w_query, preferred_element_type=jnp.float32).reshape(STEPS, PARTICLES, QH, HD)
    queries = rotate(queries, positions).astype(jnp.bfloat16)
    fresh_keys = jnp.dot(flat_rows, w_key, preferred_element_type=jnp.float32).reshape(STEPS, PARTICLES, KVH, HD)
    fresh_keys = rotate(fresh_keys, positions).astype(jnp.bfloat16).reshape(STEPS, PARTICLES, KVH * HD)
    fresh_values = jnp.dot(flat_rows, value_weight, preferred_element_type=jnp.float32).astype(jnp.bfloat16).reshape(STEPS, PARTICLES, KVH * HD)
    key_rows = jnp.concatenate([cache_keys, jnp.transpose(fresh_keys, (1, 0, 2))], 1)
    value_rows = jnp.concatenate([cache_values, jnp.transpose(fresh_values, (1, 0, 2))], 1)
    key_span = L + STEPS
    group_size = QH // KVH
    query_heads = queries.reshape(STEPS, PARTICLES, KVH, group_size, HD).astype(jnp.float32)
    key_heads = key_rows.reshape(PARTICLES, key_span, KVH, HD).astype(jnp.float32)
    value_heads = value_rows.reshape(PARTICLES, key_span, KVH, HD).astype(jnp.float32)
    scores = jnp.einsum('snkgd,nlkd->snkgl', query_heads, key_heads) / HD ** 0.5
    allowed = jnp.arange(key_span, dtype=jnp.int32)[None, :] <= (L + jnp.arange(STEPS, dtype=jnp.int32))[:, None]
    allowed = allowed[:, None, None, None, :]
    masked = jnp.where(allowed, scores, -jnp.inf)
    highest = lax.optimization_barrier(jnp.max(masked, -1, keepdims=True))
    exponent = jnp.exp(masked - highest)
    weights = (exponent / lax.optimization_barrier(jnp.sum(exponent, -1, keepdims=True))).astype(jnp.bfloat16)
    context = jnp.einsum('snkgl,nlkd->snkgd', weights.astype(jnp.float32), value_heads).astype(jnp.bfloat16)
    context = context.reshape(STEPS * PARTICLES, QH * HD)
    head_mix = jnp.dot(context, w_output, preferred_element_type=jnp.float32).reshape(STEPS, PARTICLES, D)
    attn_out = head_mix.astype(jnp.bfloat16)
    summed = inputs + head_mix
    twisting_score = lax.optimization_barrier(jnp.sum(summed * twist_vec, -1)) / jnp.sqrt(lax.optimization_barrier(jnp.mean(summed * summed, -1)) + 1e-06)
    token_reward = twisting_table[tokens].astype(jnp.float32)
    particle_log_weight = previous_log_weights + lax.optimization_barrier(jnp.sum(token_reward + twisting_score, 0))
    largest = jnp.max(particle_log_weight)
    out_logw = particle_log_weight - (largest + jnp.log(jnp.sum(jnp.exp(particle_log_weight - largest))))
    copy_ends = jnp.cumsum(copy_counts).astype(jnp.int32)
    new_slot = jnp.arange(PARTICLES, dtype=jnp.int32)
    owner_index = new_slot // PART_DEV
    local_slot = new_slot % PART_DEV
    copy_rank = local_slot * N_DOM + owner_index
    ancestor = lax.optimization_barrier(jnp.sum((copy_ends[None, :] <= copy_rank[:, None]).astype(jnp.int32), 1)).astype(jnp.int32)
    new_keys = key_rows[ancestor]
    new_values = value_rows[ancestor]
    return (attn_out, new_keys, new_values, out_logw)
```

```python
import jax
import jax.numpy as jnp
import numpy as np
from jax import lax
from jax.experimental import pallas as pl
from jax.experimental.pallas import tpu as pltpu
from jax.sharding import PartitionSpec as P

D = 4096
HD = 128
STEPS = 4
NP = 16
ROWS = STEPS * NP
SPAN = 128
TP = 8
DB = D // TP
NDOM = 32
NCHIP = 16
SLOTS = 3
BF = jnp.bfloat16
F32 = jnp.float32
ANY = pl.ANY
VM = pltpu.VMEM
SM = pltpu.SMEM


def spec(space):
    return pl.BlockSpec(memory_space=space)


def nt(a, b):
    return lax.dot_general(a, b, (((1,), (1,)), ((), ())), preferred_element_type=F32)


def mm(a, b):
    return jnp.dot(a, b, preferred_element_type=F32)


def layer_body(blk, *refs):
    acts = refs[:TP]
    gain, wq, wk, wv, wo, kc, vc, table = refs[TP : TP + 8]
    outs = refs[TP + 8 : 2 * TP + 8]
    fresh = refs[2 * TP + 8]
    wq_s, wk_s, wv_s, wo_s, q_s, qa_s, s1_s, ctx_s, kf_s, vf_s, sems = refs[2 * TP + 9 :]

    def loads(s):
        src = pl.multiple_of(blk[s] * DB, DB)
        dst = pl.multiple_of(blk[TP + s] * DB, DB)
        return (
            pltpu.make_async_copy(wq.at[pl.ds(src, DB), :], wq_s.at[s], sems.at[0, s]),
            pltpu.make_async_copy(wk.at[pl.ds(src, DB), :], wk_s.at[s], sems.at[1, s]),
            pltpu.make_async_copy(wv.at[pl.ds(src, DB), :], wv_s.at[s], sems.at[2, s]),
            pltpu.make_async_copy(wo.at[:, pl.ds(dst, DB)], wo_s.at[s], sems.at[3, s]),
        )

    copies = [loads(s) for s in range(TP)]
    for s in range(TP):
        for c in copies[s][:3]:
            c.start()
    for s in range(TP):
        copies[s][3].start()

    square = jnp.zeros((ROWS, 1), F32)
    for s in range(TP):
        x = acts[s][...].astype(F32)
        square = square + jnp.sum(x * x, -1, keepdims=True)
    inv = lax.rsqrt(square / D + 1e-05)
    q = jnp.zeros((ROWS, DB), F32)
    k = jnp.zeros((ROWS, HD), F32)
    v = jnp.zeros((ROWS, HD), F32)
    for s in range(TP):
        x = acts[s][...].astype(F32)
        normed = (x * inv * gain[pl.ds(blk[s], 1), :]).astype(BF)
        for c in copies[s][:3]:
            c.wait()
        q = q + mm(normed, wq_s[s])
        k = k + mm(normed, wk_s[s])
        v = v + mm(normed, wv_s[s])
    cosine = table[0]
    sine = table[1]

    def turned(u):
        return (u * cosine + pltpu.roll(u, HD // 2, 1) * sine).astype(BF)

    heads = DB // HD
    for g in range(heads):
        q_s[g] = turned(q[:, g * HD : (g + 1) * HD]).astype(F32)
    kf = turned(k)
    vf = v.astype(BF)
    kf_s[...] = kf.astype(F32)
    vf_s[...] = vf.astype(F32)
    group = heads * STEPS
    for n in range(NP):
        mine = pl.ds(n, STEPS, stride=NP)
        fresh[n] = jnp.concatenate([kf_s[mine, :], vf_s[mine, :]], 0).astype(BF)
        qn = jnp.concatenate(
            [q_s[g, mine, :] for g in range(heads)], 0
        ).astype(BF)
        qa_s[n * group : (n + 1) * group, :] = qn
        s1_s[n * group : (n + 1) * group, :] = nt(qn, kc[n])
    scale = 1.0 / HD**0.5
    s1 = s1_s[...] * scale
    s2 = nt(qa_s[...], kf) * scale
    row = lax.broadcasted_iota(jnp.int32, (NP * group, ROWS), 0)
    col = lax.broadcasted_iota(jnp.int32, (NP * group, ROWS), 1)
    seen = ((row // group) == (col % NP)) & ((col // NP) <= (row % STEPS))
    s2 = jnp.where(seen, s2, -jnp.inf)
    top = jnp.maximum(jnp.max(s1, -1, keepdims=True), jnp.max(s2, -1, keepdims=True))
    e1 = jnp.exp(s1 - top)
    e2 = jnp.exp(s2 - top)
    total = jnp.sum(e1, -1, keepdims=True) + jnp.sum(e2, -1, keepdims=True)
    w1 = (e1 / total).astype(BF)
    w2 = (e2 / total).astype(BF)
    c2 = mm(w2, vf)
    for n in range(NP):
        span = slice(n * group, (n + 1) * group)
        cn = (mm(w1[span], vc[n]) + c2[span]).astype(BF).astype(F32)
        for g in range(heads):
            ctx_s[g, pl.ds(n, STEPS, stride=NP), :] = cn[
                g * STEPS : (g + 1) * STEPS
            ]
    ctx = jnp.concatenate([ctx_s[g] for g in range(heads)], 1).astype(BF)
    for s in range(TP):
        copies[s][3].wait()
        outs[s][...] = mm(ctx, wo_s[s]).astype(BF)


def layer(blk, acts, gain, wq, wk, wv, wo, kc, vc, table):
    sd = jax.ShapeDtypeStruct
    return pl.pallas_call(
        layer_body,
        in_specs=[spec(SM)] + [spec(VM)] * TP + [spec(VM)] + [spec(ANY)] * 4 + [spec(VM)] * 3,
        out_specs=[spec(VM)] * (TP + 1),
        out_shape=[sd((ROWS, DB), BF)] * TP + [sd((NP, 2 * STEPS, HD), BF)],
        scratch_shapes=[
            VM((TP, DB, DB), BF),
            VM((TP, DB, HD), BF),
            VM((TP, DB, HD), BF),
            VM((TP, DB, DB), BF),
            VM((DB // HD, ROWS, HD), F32),
            VM((NP * 16, HD), BF),
            VM((NP * 16, SPAN), F32),
            VM((DB // HD, ROWS, HD), F32),
            VM((ROWS, HD), F32),
            VM((ROWS, HD), F32),
            pltpu.SemaphoreType.DMA((4, TP)),
        ],
        compiler_params=pltpu.CompilerParams(vmem_limit_bytes=40 * 2**20),
        cost_estimate=pl.CostEstimate(
            flops=2 * ROWS * D * 1280, bytes_accessed=12 * 2**20, transcendentals=NP * 16 * 192
        ),
        name="layer",
    )(blk, *acts, gain, wq, wk, wv, wo, kc, vc, table)


def mix_body(*refs):
    parts = refs[:TP]
    act, twist, attn, sums = refs[TP:]
    mix = parts[0][...].astype(F32)
    for s in range(1, TP):
        mix = mix + parts[s][...].astype(F32)
    attn[...] = mix.astype(BF)
    summed = act[...].astype(F32) + mix
    aligned = jnp.sum(summed * twist[...], -1, keepdims=True)
    energy = jnp.sum(summed * summed, -1, keepdims=True)
    lane = lax.broadcasted_iota(jnp.int32, (ROWS, HD), 1)
    sums[...] = jnp.where(lane == 0, aligned, energy)


def mix(parts, act, twist):
    sd = jax.ShapeDtypeStruct
    return pl.pallas_call(
        mix_body,
        in_specs=[spec(VM)] * (TP + 2),
        out_specs=[spec(VM)] * 2,
        out_shape=[sd((ROWS, DB), BF), sd((ROWS, HD), F32)],
        name="mix",
    )(*parts, act, twist)


def weigh_body(*refs):
    parts = refs[:TP]
    reward, previous, out = refs[TP:]
    sums = parts[0][...]
    for s in range(1, TP):
        sums = sums + parts[s][...]
    score = sums[:, 0:1] / jnp.sqrt(sums[:, 1:2] / D + 1e-06) + reward[...]
    gain = score[0:NP]
    for t in range(1, STEPS):
        gain = gain + score[t * NP : (t + 1) * NP]
    out[...] = jnp.broadcast_to(previous[...] + gain, (NP, HD))


def weigh(parts, reward, previous):
    return pl.pallas_call(
        weigh_body,
        in_specs=[spec(VM)] * (TP + 2),
        out_specs=spec(VM),
        out_shape=jax.ShapeDtypeStruct((NP, HD), F32),
        name="weigh",
    )(*parts, reward, previous)


def plan_body(me_ref, counts_ref, out):
    me = me_ref[0]
    counts = counts_ref[...].astype(F32)
    r16 = lax.broadcasted_iota(jnp.int32, (NP, NP), 0)
    c16 = lax.broadcasted_iota(jnp.int32, (NP, NP), 1)
    within = mm(counts, (r16 <= c16).astype(F32))
    r32 = lax.broadcasted_iota(jnp.int32, (NDOM, NDOM), 0)
    c32 = lax.broadcasted_iota(jnp.int32, (NDOM, NDOM), 1)
    before = jnp.sum(mm((c32 < r32).astype(F32), counts), -1, keepdims=True)
    ends = (within + before).astype(jnp.int32)
    before = before.astype(jnp.int32)
    device = lax.broadcasted_iota(jnp.int32, (NDOM, 1), 0)
    chip_end = jnp.where(device % 2 == 1, ends[:, NP - 1 : NP], -1)
    chip = me // 2
    first = jnp.sum(jnp.where(device == 2 * chip, before, 0))
    lane = lax.broadcasted_iota(jnp.int32, (1, HD), 1)
    dest = 2 * (lane // 4) + me % 2
    sent = first + ((dest - first) & (NDOM - 1)) + NDOM * (lane % 4)
    kept = NDOM * (lane - 64) + me
    found = jnp.zeros((NDOM, HD), jnp.int32)
    for j in range(NP):
        found = found + (ends[:, j : j + 1] <= sent).astype(jnp.int32)
    particle = jnp.sum(found, 0, keepdims=True) - 2 * NP * chip
    particle = jnp.clip(particle, 0, 2 * NP - 1)
    passed = (chip_end >= 0) & (chip_end <= kept)
    source = jnp.sum(passed.astype(jnp.int32), 0, keepdims=True)
    base = jnp.max(jnp.where(passed, chip_end, 0), 0, keepdims=True)
    slot = jnp.clip((kept - base) // NDOM, 0, 3)
    arrived = 4 * jnp.clip(source, 0, NCHIP - 1) + slot
    owned = jnp.sum(counts, -1, keepdims=True).astype(jnp.int32)
    pair = lax.broadcasted_iota(jnp.int32, (NDOM, HD), 1)
    most = jnp.max(jnp.sum(jnp.where(pair == device // 2, owned, 0), 0, keepdims=True))
    line = jnp.where(lane < 64, particle, jnp.where(lane < 80, arrived, most))
    out[...] = jnp.broadcast_to(line, (8, HD))


def plan(me, counts):
    return pl.pallas_call(
        plan_body,
        in_specs=[spec(SM), spec(VM)],
        out_specs=spec(VM),
        out_shape=jax.ShapeDtypeStruct((8, HD), jnp.int32),
        name="plan",
    )(me, counts)


def pack_body(me_ref, idx, *refs):
    half = (len(refs) - 3) // 2
    own, partner = (refs[:half], refs[half : 2 * half])
    out, rows, sems = refs[2 * half :]
    core = me_ref[0] % 2
    loads, at = ([], 0)
    for n in range(half):
        length = own[n].shape[1]
        for side, ref in ((core, own[n]), (1 - core, partner[n])):
            there = rows.at[pl.ds(side * NP, NP), pl.ds(at, length), :]
            loads.append(pltpu.make_async_copy(ref, there, sems.at[len(loads) + 1]))
        at += length
    for c in loads:
        c.start()
    for c in loads:
        c.wait()
    for q in range(NCHIP):
        for s in range(SLOTS):
            pltpu.make_async_copy(rows.at[idx[0, 4 * q + s]], out.at[q, s], sems.at[0]).start()
    pltpu.make_async_copy(out, out, sems.at[0]).wait()


def pack(me, idx, own, partner):
    length = sum(a.shape[1] for a in own)
    return pl.pallas_call(
        pack_body,
        in_specs=[spec(SM), spec(SM)] + [spec(ANY)] * (2 * len(own)),
        out_specs=spec(ANY),
        out_shape=jax.ShapeDtypeStruct((NCHIP, SLOTS, length, HD), BF),
        scratch_shapes=[
            VM((2 * NP, length, HD), BF),
            pltpu.SemaphoreType.DMA((1 + 2 * len(own),)),
        ],
        name="pack",
    )(me, idx, *own, *partner)


def place_body(slots, idx, first, second, keys, values, k_s, v_s, sems):
    copies = []
    for k in range(NP):
        code = idx[0, 64 + k]
        chip = code // 4
        slot = jnp.minimum(code % 4, slots - 1)
        copies.append(pltpu.make_async_copy(first.at[chip, slot], k_s.at[k], sems.at[0, k]))
        copies.append(pltpu.make_async_copy(second.at[chip, slot], v_s.at[k], sems.at[1, k]))
    for c in copies:
        c.start()
    for k in range(NP):
        copies[2 * k].wait()
        copies[2 * k + 1].wait()
        keys[k, 0:SPAN, :] = k_s[k]
        values[k, 0:SPAN, :] = v_s[k, 0:SPAN, :]
        tail = v_s[k, SPAN : SPAN + 2 * STEPS, :].astype(F32)
        keys[k, SPAN : SPAN + STEPS, :] = tail[0:STEPS].astype(BF)
        values[k, SPAN : SPAN + STEPS, :] = tail[STEPS : 2 * STEPS].astype(BF)


def place(idx, first, second):
    out = jax.ShapeDtypeStruct((NP, SPAN + STEPS, HD), BF)
    slots = first.shape[1]
    return pl.pallas_call(
        lambda *refs: place_body(slots, *refs),
        in_specs=[spec(SM), spec(ANY), spec(ANY)],
        out_specs=[spec(VM)] * 2,
        out_shape=[out] * 2,
        scratch_shapes=[
            VM((NP, SPAN, HD), BF),
            VM((NP, SPAN + 2 * STEPS, HD), BF),
            pltpu.SemaphoreType.DMA((2, NP)),
        ],
        name="place",
    )(idx, first, second)


def shifted(value, shift):
    return lax.ppermute(value, "tp", [(i, (i + shift) % TP) for i in range(TP)])


def swapped(value):
    return lax.ppermute(value, "dom", [(i, i ^ 1) for i in range(NDOM)])


SAME_CORE = [list(range(c, NDOM, 2)) for c in range(2)]


def exchanged(rows):
    return lax.all_to_all(rows, "dom", 0, 0, tiled=True, axis_index_groups=SAME_CORE)


def copy_for_each(value):
    sent = jnp.broadcast_to(value[None], (NDOM, *value.shape))
    return lax.all_to_all(sent, "dom", 0, 0, tiled=True)


def rotation_table():
    frequency = np.float32(500000.0) ** (-2.0 * np.arange(HD // 2, dtype=np.float32) / HD)
    angles = (SPAN + np.arange(STEPS, dtype=np.float32))[:, None] * frequency.astype(np.float32)
    cosine = np.concatenate([np.cos(angles), np.cos(angles)], 1)
    sine = np.concatenate([-np.sin(angles), np.sin(angles)], 1)
    return np.stack([np.repeat(cosine, NP, 0), np.repeat(sine, NP, 0)]).astype(np.float32)


def local(
    activations,
    norm_gain,
    w_query,
    w_key,
    value_weight,
    w_output,
    cache_keys,
    cache_values,
    tokens,
    twisting_table,
    twist_vec,
    previous_log_weights,
    copy_counts,
):
    dom = lax.axis_index("dom")
    tp = lax.axis_index("tp")
    me = dom.reshape(1)
    ring = np.arange(TP)
    blk = jnp.concatenate([(tp - ring) % TP, (tp + ring) % TP]).astype(jnp.int32)

    counts = copy_for_each(copy_counts)
    act = activations.reshape(ROWS, DB)
    acts = [act] + [shifted(act, s) for s in range(1, TP)]
    partner_keys = swapped(cache_keys)
    partner_values = swapped(cache_values)

    idx = plan(me, counts)
    first = exchanged(pack(me, idx, [cache_keys], [partner_keys]))

    outs = layer(
        blk,
        acts,
        norm_gain.reshape(TP, DB),
        w_query,
        w_key,
        value_weight,
        w_output,
        cache_keys,
        cache_values,
        rotation_table(),
    )
    partials, fresh = (outs[:TP], outs[TP])
    partner_fresh = swapped(fresh)
    second = exchanged(
        pack(me, idx, [cache_values, fresh], [partner_values, partner_fresh])
    )

    parts = [partials[0]] + [shifted(partials[s], s) for s in range(1, TP)]
    attn, sums = mix(parts, act, twist_vec.reshape(1, DB))
    all_sums = [sums] + [shifted(sums, s) for s in range(1, TP)]
    reward = twisting_table[tokens.reshape(ROWS)].astype(F32).reshape(ROWS, 1)
    logw = weigh(all_sums, reward, previous_log_weights.reshape(NP, 1))[:, 0]
    every = copy_for_each(logw)
    largest = jnp.max(every)
    out_logw = logw - (largest + jnp.log(jnp.sum(jnp.exp(every - largest))))

    def usual(first, second, *_):
        return tuple(place(idx, first, second))

    def crowded(first, second, partner_keys, partner_values, partner_fresh, fresh, idx):
        even = dom % 2 == 0
        mine = jnp.concatenate([cache_keys, cache_values, fresh], 1)
        other = jnp.concatenate([partner_keys, partner_values, partner_fresh], 1)
        chip_rows = jnp.concatenate(
            [jnp.where(even, mine, other), jnp.where(even, other, mine)], 0
        )
        more = exchanged(chip_rows[idx[0, 3:64:4]][:, None])
        return tuple(
            place(
                idx,
                jnp.concatenate([first, more[:, :, :SPAN]], 1),
                jnp.concatenate([second, more[:, :, SPAN:]], 1),
            )
        )

    new_keys, new_values = lax.cond(
        idx[0, 127] > SLOTS * NDOM,
        crowded,
        usual,
        first,
        second,
        partner_keys,
        partner_values,
        partner_fresh,
        fresh,
        idx,
    )
    return (attn.reshape(STEPS, NP, DB), new_keys, new_values, out_logw)


def solution(mesh):
    return jax.shard_map(
        local,
        mesh=mesh,
        in_specs=(
            P(None, "dom", "tp"),
            P(),
            P(None, "tp"),
            P(None, "tp"),
            P(None, "tp"),
            P("tp", None),
            P("dom", None, "tp"),
            P("dom", None, "tp"),
            P(None, "dom"),
            P(),
            P("tp"),
            P("dom"),
            P("dom"),
        ),
        out_specs=(P(None, "dom", "tp"), P("dom", None, "tp"), P("dom", None, "tp"), P("dom")),
        check_vma=False,
    )
```

```python
import jax
import jax.numpy as jnp
import numpy as np
from jax import lax
from jax.experimental import pallas as pl
from jax.experimental.pallas import tpu as pltpu
from jax.sharding import PartitionSpec as P

D = 4096
HD = 128
STEPS = 4
NP = 16
ROWS = STEPS * NP
SPAN = 128
TP = 8
DB = D // TP
HEADS = DB // HD
GROUP = HEADS * STEPS
NDOM = 32
NCHIP = 16
SLOTS = 3
BF = jnp.bfloat16
F32 = jnp.float32
ANY = pl.ANY
VM = pltpu.VMEM
SM = pltpu.SMEM


def spec(space):
    return pl.BlockSpec(memory_space=space)


def limit(mib):
    return pltpu.CompilerParams(vmem_limit_bytes=mib * 2**20)


def nt(a, b):
    return lax.dot_general(a, b, (((1,), (1,)), ((), ())), preferred_element_type=F32)


def mm(a, b):
    return jnp.dot(a, b, preferred_element_type=F32)


def project_body(acts, gain, wq, wk, wv, table, qa, kf, vf, fresh, *scratch):
    wq_s, wk_s, wv_s, q_s, kf_s, vf_s, sems = scratch
    copies = []
    for s in range(TP):
        part = pl.ds(s * DB, DB)
        copies.append(
            [
                pltpu.make_async_copy(w.at[part, :], w_s.at[s], sems.at[n, s])
                for n, (w, w_s) in enumerate(((wq, wq_s), (wk, wk_s), (wv, wv_s)))
            ]
        )
    for group in copies:
        for c in group:
            c.start()
    square = jnp.zeros((ROWS, 1), F32)
    for s in range(TP):
        x = acts[s].astype(F32)
        square = square + jnp.sum(x * x, -1, keepdims=True)
    inv = lax.rsqrt(square / D + 1e-05)
    q = jnp.zeros((ROWS, DB), F32)
    k = jnp.zeros((ROWS, HD), F32)
    v = jnp.zeros((ROWS, HD), F32)
    for s in range(TP):
        x = acts[s].astype(F32)
        normed = (x * inv * gain[s : s + 1, :]).astype(BF)
        for c in copies[s]:
            c.wait()
        q = q + mm(normed, wq_s[s])
        k = k + mm(normed, wk_s[s])
        v = v + mm(normed, wv_s[s])
    cosine = table[0]
    sine = table[1]

    def turned(u):
        return (u * cosine + pltpu.roll(u, HD // 2, 1) * sine).astype(BF)

    for g in range(HEADS):
        q_s[g] = turned(q[:, g * HD : (g + 1) * HD]).astype(F32)
    k = turned(k)
    v = v.astype(BF)
    kf[...] = k
    vf[...] = v
    kf_s[...] = k.astype(F32)
    vf_s[...] = v.astype(F32)
    for n in range(NP):
        mine = pl.ds(n, STEPS, stride=NP)
        fresh[n] = jnp.concatenate([kf_s[mine, :], vf_s[mine, :]], 0).astype(BF)
        qa[n * GROUP : (n + 1) * GROUP, :] = jnp.concatenate(
            [q_s[g, mine, :] for g in range(HEADS)], 0
        ).astype(BF)


def project(acts, gain, wq, wk, wv, table):
    sd = jax.ShapeDtypeStruct
    return pl.pallas_call(
        project_body,
        in_specs=[spec(VM)] * 2 + [spec(ANY)] * 3 + [spec(VM)],
        out_specs=[spec(VM)] * 4,
        out_shape=[
            sd((NP * GROUP, HD), BF),
            sd((ROWS, HD), BF),
            sd((ROWS, HD), BF),
            sd((NP, 2 * STEPS, HD), BF),
        ],
        scratch_shapes=[
            VM((TP, DB, DB), BF),
            VM((TP, DB, HD), BF),
            VM((TP, DB, HD), BF),
            VM((HEADS, ROWS, HD), F32),
            VM((ROWS, HD), F32),
            VM((ROWS, HD), F32),
            pltpu.SemaphoreType.DMA((3, TP)),
        ],
        compiler_params=limit(55),
        cost_estimate=pl.CostEstimate(
            flops=2 * ROWS * D * 768, bytes_accessed=7 * 2**20, transcendentals=0
        ),
        name="project",
    )(acts, gain, wq, wk, wv, table)


def attend_body(blk, qa, kf, vf, kc, vc, wo, *refs):
    outs = refs[:TP]
    s1_s, ctx_s, wo_s, sems = refs[TP:]
    copies = []
    for s in range(TP):
        there = pl.ds(pl.multiple_of(blk[s] * DB, DB), DB)
        copies.append(pltpu.make_async_copy(wo.at[:, there], wo_s.at[s], sems.at[s]))
    for c in copies:
        c.start()
    for n in range(NP):
        span = slice(n * GROUP, (n + 1) * GROUP)
        s1_s[span, :] = nt(qa[span, :], kc[n])
    scale = 1.0 / HD**0.5
    s1 = s1_s[...] * scale
    s2 = nt(qa[...], kf[...]) * scale
    row = lax.broadcasted_iota(jnp.int32, (NP * GROUP, ROWS), 0)
    col = lax.broadcasted_iota(jnp.int32, (NP * GROUP, ROWS), 1)
    seen = ((row // GROUP) == (col % NP)) & ((col // NP) <= (row % STEPS))
    s2 = jnp.where(seen, s2, -jnp.inf)
    top = jnp.maximum(jnp.max(s1, -1, keepdims=True), jnp.max(s2, -1, keepdims=True))
    e1 = jnp.exp(s1 - top)
    e2 = jnp.exp(s2 - top)
    total = jnp.sum(e1, -1, keepdims=True) + jnp.sum(e2, -1, keepdims=True)
    w1 = (e1 / total).astype(BF)
    w2 = (e2 / total).astype(BF)
    c2 = mm(w2, vf[...])
    for n in range(NP):
        span = slice(n * GROUP, (n + 1) * GROUP)
        cn = (mm(w1[span], vc[n]) + c2[span]).astype(BF).astype(F32)
        for g in range(HEADS):
            ctx_s[g, pl.ds(n, STEPS, stride=NP), :] = cn[g * STEPS : (g + 1) * STEPS]
    ctx = jnp.concatenate([ctx_s[g] for g in range(HEADS)], 1).astype(BF)
    for s in range(TP):
        copies[s].wait()
        outs[s][...] = mm(ctx, wo_s[s]).astype(BF)


def attend(blk, qa, kf, vf, kc, vc, wo):
    return pl.pallas_call(
        attend_body,
        in_specs=[spec(SM)] + [spec(VM)] * 5 + [spec(ANY)],
        out_specs=[spec(VM)] * TP,
        out_shape=[jax.ShapeDtypeStruct((ROWS, DB), BF)] * TP,
        scratch_shapes=[
            VM((NP * GROUP, SPAN), F32),
            VM((HEADS, ROWS, HD), F32),
            VM((TP, DB, DB), BF),
            pltpu.SemaphoreType.DMA((TP,)),
        ],
        compiler_params=limit(55),
        cost_estimate=pl.CostEstimate(
            flops=2 * ROWS * D * 640, bytes_accessed=6 * 2**20, transcendentals=NP * 16 * 192
        ),
        name="attend",
    )(blk, qa, kf, vf, kc, vc, wo)


def mix_body(*refs):
    parts = refs[:TP]
    act, twist, attn, sums = refs[TP:]
    mix = parts[0][...].astype(F32)
    for s in range(1, TP):
        mix = mix + parts[s][...].astype(F32)
    attn[...] = mix.astype(BF)
    summed = act[...].astype(F32) + mix
    aligned = jnp.sum(summed * twist[...], -1, keepdims=True)
    energy = jnp.sum(summed * summed, -1, keepdims=True)
    lane = lax.broadcasted_iota(jnp.int32, (ROWS, HD), 1)
    sums[...] = jnp.where(lane == 0, aligned, energy)


def mix(parts, act, twist):
    sd = jax.ShapeDtypeStruct
    return pl.pallas_call(
        mix_body,
        in_specs=[spec(VM)] * (TP + 2),
        out_specs=[spec(VM)] * 2,
        out_shape=[sd((ROWS, DB), BF), sd((ROWS, HD), F32)],
        compiler_params=limit(8),
        name="mix",
    )(*parts, act, twist)


def weigh_body(*refs):
    parts = refs[:TP]
    reward, previous, out = refs[TP:]
    sums = parts[0][...]
    for s in range(1, TP):
        sums = sums + parts[s][...]
    score = sums[:, 0:1] / jnp.sqrt(sums[:, 1:2] / D + 1e-06) + reward[...]
    gain = score[0:NP]
    for t in range(1, STEPS):
        gain = gain + score[t * NP : (t + 1) * NP]
    column = jnp.broadcast_to(previous[...] + gain, (NP, HD))
    row = lax.broadcasted_iota(jnp.int32, (NP, HD), 0)
    lane = lax.broadcasted_iota(jnp.int32, (NP, HD), 1)
    line = jnp.sum(jnp.where(row == lane, column, 0.0), 0, keepdims=True)
    out[...] = jnp.broadcast_to(line[None], (NDOM, 1, HD))


def weigh(parts, reward, previous):
    return pl.pallas_call(
        weigh_body,
        in_specs=[spec(VM)] * (TP + 2),
        out_specs=spec(VM),
        out_shape=jax.ShapeDtypeStruct((NDOM, 1, HD), F32),
        compiler_params=limit(8),
        name="weigh",
    )(*parts, reward, previous)


def finish_body(mine, every, out):
    lane = lax.broadcasted_iota(jnp.int32, (NDOM, HD), 1)
    all_w = jnp.where(lane < NP, every[:, 0, :], -jnp.inf)
    largest = jnp.max(all_w, keepdims=True)
    mass = jnp.sum(jnp.exp(all_w - largest), keepdims=True)
    out[...] = (mine[0] - (largest + jnp.log(mass)))[:, 0:NP]


def finish(mine, every):
    return pl.pallas_call(
        finish_body,
        in_specs=[spec(VM)] * 2,
        out_specs=spec(VM),
        out_shape=jax.ShapeDtypeStruct((1, NP), F32),
        compiler_params=limit(8),
        name="finish",
    )(mine, every)


def plan_body(me_ref, *refs):
    out = refs[-1]
    me = me_ref[0]
    blocks = jnp.concatenate([r[...] for r in refs[:-1]], 0).astype(F32)
    rel = lax.broadcasted_iota(jnp.int32, (NDOM, NDOM), 1)
    back_y = (me // 8 - rel // 8) & 3
    back_x = (me // 2 - rel // 2) & 3
    holder = 8 * back_y + 2 * back_x + ((me + rel) & 1)
    sorted_rows = lax.broadcasted_iota(jnp.int32, (NDOM, NDOM), 0) == holder
    counts = mm(sorted_rows.astype(F32), blocks)
    r16 = lax.broadcasted_iota(jnp.int32, (NP, NP), 0)
    c16 = lax.broadcasted_iota(jnp.int32, (NP, NP), 1)
    within = mm(counts, (r16 <= c16).astype(F32))
    r32 = lax.broadcasted_iota(jnp.int32, (NDOM, NDOM), 0)
    c32 = lax.broadcasted_iota(jnp.int32, (NDOM, NDOM), 1)
    before = jnp.sum(mm((c32 < r32).astype(F32), counts), -1, keepdims=True)
    ends = (within + before).astype(jnp.int32)
    before = before.astype(jnp.int32)
    device = lax.broadcasted_iota(jnp.int32, (NDOM, 1), 0)
    chip_end = jnp.where(device % 2 == 1, ends[:, NP - 1 : NP], -1)
    chip = me // 2
    first = jnp.sum(jnp.where(device == 2 * chip, before, 0))
    lane = lax.broadcasted_iota(jnp.int32, (1, HD), 1)
    dest = 2 * (lane // 4) + me % 2
    sent = first + ((dest - first) & (NDOM - 1)) + NDOM * (lane % 4)
    kept = NDOM * (lane - 64) + me
    found = jnp.zeros((NDOM, HD), jnp.int32)
    for j in range(NP):
        found = found + (ends[:, j : j + 1] <= sent).astype(jnp.int32)
    particle = jnp.sum(found, 0, keepdims=True) - 2 * NP * chip
    particle = jnp.clip(particle, 0, 2 * NP - 1)
    passed = (chip_end >= 0) & (chip_end <= kept)
    source = jnp.sum(passed.astype(jnp.int32), 0, keepdims=True)
    base = jnp.max(jnp.where(passed, chip_end, 0), 0, keepdims=True)
    slot = jnp.clip((kept - base) // NDOM, 0, 3)
    arrived = 4 * jnp.clip(source, 0, NCHIP - 1) + slot
    owned = jnp.sum(counts, -1, keepdims=True).astype(jnp.int32)
    pair = lax.broadcasted_iota(jnp.int32, (NDOM, HD), 1)
    most = jnp.max(jnp.sum(jnp.where(pair == device // 2, owned, 0), 0, keepdims=True))
    line = jnp.where(lane < 64, particle, jnp.where(lane < 80, arrived, most))
    out[...] = jnp.broadcast_to(line, (8, HD))


def plan(me, blocks):
    return pl.pallas_call(
        plan_body,
        in_specs=[spec(SM)] + [spec(VM)] * len(blocks),
        out_specs=spec(VM),
        out_shape=jax.ShapeDtypeStruct((8, HD), jnp.int32),
        compiler_params=limit(8),
        name="plan",
    )(me, *blocks)


def pack_body(me_ref, idx, *refs):
    half = (len(refs) - 3) // 2
    own, partner = (refs[:half], refs[half : 2 * half])
    out, rows, sems = refs[2 * half :]
    core = me_ref[0] % 2
    loads, at = ([], 0)
    for n in range(half):
        length = own[n].shape[1]
        for side, ref in ((core, own[n]), (1 - core, partner[n])):
            there = rows.at[pl.ds(side * NP, NP), pl.ds(at, length), :]
            loads.append(pltpu.make_async_copy(ref, there, sems.at[len(loads) + 1]))
        at += length
    for c in loads:
        c.start()
    for c in loads:
        c.wait()
    for q in range(NCHIP):
        for s in range(SLOTS):
            pltpu.make_async_copy(rows.at[idx[0, 4 * q + s]], out.at[q, s], sems.at[0]).start()
    pltpu.make_async_copy(out, out, sems.at[0]).wait()


def pack(me, idx, own, partner):
    length = sum(a.shape[1] for a in own)
    return pl.pallas_call(
        pack_body,
        in_specs=[spec(SM), spec(SM)] + [spec(ANY)] * (2 * len(own)),
        out_specs=spec(ANY),
        out_shape=jax.ShapeDtypeStruct((NCHIP, SLOTS, length, HD), BF),
        scratch_shapes=[
            VM((2 * NP, length, HD), BF),
            pltpu.SemaphoreType.DMA((1 + 2 * len(own),)),
        ],
        compiler_params=limit(16),
        name="pack",
    )(me, idx, *own, *partner)


def place_body(slots, idx, rows, keys, values, r_s, sems):
    copies = []
    for k in range(NP):
        code = idx[0, 64 + k]
        slot = jnp.minimum(code % 4, slots - 1)
        copies.append(
            pltpu.make_async_copy(rows.at[code // 4, slot], r_s.at[k], sems.at[k])
        )
    for c in copies:
        c.start()
    for k in range(NP):
        copies[k].wait()
        keys[k, 0:SPAN, :] = r_s[k, 0:SPAN, :]
        values[k, 0:SPAN, :] = r_s[k, SPAN : 2 * SPAN, :]
        tail = r_s[k, 2 * SPAN : 2 * SPAN + 2 * STEPS, :].astype(F32)
        keys[k, SPAN : SPAN + STEPS, :] = tail[0:STEPS].astype(BF)
        values[k, SPAN : SPAN + STEPS, :] = tail[STEPS : 2 * STEPS].astype(BF)


def place(idx, rows):
    out = jax.ShapeDtypeStruct((NP, SPAN + STEPS, HD), BF)
    slots = rows.shape[1]
    return pl.pallas_call(
        lambda *refs: place_body(slots, *refs),
        in_specs=[spec(SM), spec(ANY)],
        out_specs=[spec(VM)] * 2,
        out_shape=[out] * 2,
        scratch_shapes=[
            VM((NP, 2 * SPAN + 2 * STEPS, HD), BF),
            pltpu.SemaphoreType.DMA((NP,)),
        ],
        compiler_params=limit(16),
        name="place",
    )(idx, rows)


def shifted(value, shift):
    return lax.ppermute(value, "tp", [(i, (i + shift) % TP) for i in range(TP)])


def swapped(value):
    return lax.ppermute(value, "dom", [(i, i ^ 1) for i in range(NDOM)])


def next_chip(value):
    return lax.ppermute(value, "dom", [(i, (i + 2) % NDOM) for i in range(NDOM)])


SAME_CORE = [list(range(c, NDOM, 2)) for c in range(2)]


def exchanged(rows):
    return lax.all_to_all(rows, "dom", 0, 0, tiled=True, axis_index_groups=SAME_CORE)


def moved(value, axis_stride, shift):
    def to(i):
        at = i // axis_stride % 4
        return i + ((at + shift) % 4 - at) * axis_stride

    return lax.ppermute(value, "dom", [(i, to(i)) for i in range(NDOM)])


def spread_counts(copy_counts):
    own = copy_counts.reshape(1, NP)
    chip = jnp.concatenate([own, swapped(own)], 0)
    row = jnp.concatenate([chip] + [moved(chip, 2, s) for s in range(1, 4)], 0)
    return [row] + [moved(row, 8, s) for s in range(1, 4)]


def rotation_table():
    frequency = np.float32(500000.0) ** (-2.0 * np.arange(HD // 2, dtype=np.float32) / HD)
    angles = (SPAN + np.arange(STEPS, dtype=np.float32))[:, None] * frequency.astype(np.float32)
    cosine = np.concatenate([np.cos(angles), np.cos(angles)], 1)
    sine = np.concatenate([-np.sin(angles), np.sin(angles)], 1)
    return np.stack([np.repeat(cosine, NP, 0), np.repeat(sine, NP, 0)]).astype(np.float32)


def local(
    activations,
    norm_gain,
    w_query,
    w_key,
    value_weight,
    w_output,
    cache_keys,
    cache_values,
    tokens,
    twisting_table,
    twist_vec,
    previous_log_weights,
    copy_counts,
):
    dom = lax.axis_index("dom")
    tp = lax.axis_index("tp")
    me = dom.reshape(1)
    blk = ((tp + np.arange(TP)) % TP).astype(jnp.int32)
    act = activations.reshape(ROWS, DB)

    gathered = lax.all_to_all(
        jnp.broadcast_to(act[None], (TP, ROWS, DB)), "tp", 0, 0, tiled=True
    )
    idx = plan(me, spread_counts(copy_counts))
    partner_keys = swapped(cache_keys)
    partner_values = swapped(cache_values)
    reward = twisting_table[tokens.reshape(ROWS)].astype(F32).reshape(ROWS, 1)

    gathered, idx, partner_keys, partner_values, reward = lax.optimization_barrier(
        (gathered, idx, partner_keys, partner_values, reward)
    )
    qa, kf, vf, fresh = project(
        gathered, norm_gain.reshape(TP, DB), w_query, w_key, value_weight, rotation_table()
    )
    partner_fresh = swapped(fresh)
    packed = pack(
        me,
        idx,
        [cache_keys, cache_values, fresh],
        [partner_keys, partner_values, partner_fresh],
    )
    packed, qa = lax.optimization_barrier((packed, qa))
    rows = exchanged(packed)
    partials = attend(blk, qa, kf, vf, cache_keys, cache_values, w_output)

    parts = [partials[0]] + [shifted(partials[s], s) for s in range(1, TP)]
    attn, sums = mix(parts, act, twist_vec.reshape(1, DB))
    all_sums = [sums] + [shifted(sums, s) for s in range(1, TP)]
    logw = weigh(all_sums, reward, previous_log_weights.reshape(NP, 1))
    logw, rows = lax.optimization_barrier((logw, rows))
    every = lax.all_to_all(logw, "dom", 0, 0, tiled=True)
    out_logw = finish(logw, every).reshape(NP)

    def usual(rows, *_):
        return tuple(place(idx, rows))

    def crowded(rows, partner_keys, partner_values, partner_fresh, fresh, idx):
        even = dom % 2 == 0
        mine = jnp.concatenate([cache_keys, cache_values, fresh], 1)
        other = jnp.concatenate([partner_keys, partner_values, partner_fresh], 1)
        chip_rows = jnp.concatenate(
            [jnp.where(even, mine, other), jnp.where(even, other, mine)], 0
        )
        chosen = chip_rows[idx[0, 3:64:4]]
        chip = dom // 2

        def turn(step, state):
            passing, more = state
            passing = next_chip(passing)
            return passing, more.at[(chip - step) % NCHIP].set(passing[chip])

        start = (chosen, chosen)
        more = lax.fori_loop(1, NCHIP, turn, start)[1].at[chip].set(chosen[chip])
        return tuple(place(idx, jnp.concatenate([rows, more[:, None]], 1)))

    new_keys, new_values = lax.cond(
        idx[0, 127] > SLOTS * NDOM,
        crowded,
        usual,
        rows,
        partner_keys,
        partner_values,
        partner_fresh,
        fresh,
        idx,
    )
    return (attn.reshape(STEPS, NP, DB), new_keys, new_values, out_logw)


def solution(mesh):
    return jax.shard_map(
        local,
        mesh=mesh,
        in_specs=(
            P(None, "dom", "tp"),
            P(),
            P(None, "tp"),
            P(None, "tp"),
            P(None, "tp"),
            P("tp", None),
            P("dom", None, "tp"),
            P("dom", None, "tp"),
            P(None, "dom"),
            P(),
            P("tp"),
            P("dom"),
            P("dom"),
        ),
        out_specs=(P(None, "dom", "tp"), P("dom", None, "tp"), P("dom", None, "tp"), P("dom")),
        check_vma=False,
    )
```

```python
import jax
import jax.numpy as jnp
import numpy as np
from jax import lax
from jax.experimental import pallas as pl
from jax.experimental.pallas import tpu as pltpu
from jax.sharding import PartitionSpec as P

D = 4096
HD = 128
STEPS = 4
NP = 16
ROWS = STEPS * NP
SPAN = 128
TP = 8
DB = D // TP
HEADS = DB // HD
GROUP = HEADS * STEPS
NDOM = 32
NCHIP = 16
SLOTS = 3
BF = jnp.bfloat16
F32 = jnp.float32
ANY = pl.ANY
VM = pltpu.VMEM
SM = pltpu.SMEM


def spec(space):
    return pl.BlockSpec(memory_space=space)


def limit(mib):
    return pltpu.CompilerParams(vmem_limit_bytes=mib * 2**20)


def nt(a, b):
    return lax.dot_general(a, b, (((1,), (1,)), ((), ())), preferred_element_type=F32)


def mm(a, b):
    return jnp.dot(a, b, preferred_element_type=F32)


def project_body(blk, *refs):
    acts = refs[:TP]
    gain, wq, wk, wv, table, qa, kf, vf, fresh = refs[TP : TP + 9]
    wq_s, wk_s, wv_s, q_s, kf_s, vf_s, sems = refs[TP + 9 :]
    copies = []
    for s in range(TP):
        part = pl.ds(pl.multiple_of(blk[s] * DB, DB), DB)
        copies.append(
            [
                pltpu.make_async_copy(w.at[part, :], w_s.at[s], sems.at[n, s])
                for n, (w, w_s) in enumerate(((wq, wq_s), (wk, wk_s), (wv, wv_s)))
            ]
        )
    for group in copies:
        for c in group:
            c.start()
    square = jnp.zeros((ROWS, 1), F32)
    for s in range(TP):
        x = acts[s][...].astype(F32)
        square = square + jnp.sum(x * x, -1, keepdims=True)
    inv = lax.rsqrt(square / D + 1e-05)
    q = jnp.zeros((ROWS, DB), F32)
    k = jnp.zeros((ROWS, HD), F32)
    v = jnp.zeros((ROWS, HD), F32)
    for s in range(TP):
        x = acts[s][...].astype(F32)
        normed = (x * inv * gain[pl.ds(blk[s], 1), :]).astype(BF)
        for c in copies[s]:
            c.wait()
        q = q + mm(normed, wq_s[s])
        k = k + mm(normed, wk_s[s])
        v = v + mm(normed, wv_s[s])
    cosine = table[0]
    sine = table[1]

    def turned(u):
        return (u * cosine + pltpu.roll(u, HD // 2, 1) * sine).astype(BF)

    for g in range(HEADS):
        q_s[g] = turned(q[:, g * HD : (g + 1) * HD]).astype(F32)
    k = turned(k)
    v = v.astype(BF)
    kf[...] = k
    vf[...] = v
    kf_s[...] = k.astype(F32)
    vf_s[...] = v.astype(F32)
    for n in range(NP):
        mine = pl.ds(n, STEPS, stride=NP)
        fresh[n] = jnp.concatenate([kf_s[mine, :], vf_s[mine, :]], 0).astype(BF)
        qa[n * GROUP : (n + 1) * GROUP, :] = jnp.concatenate(
            [q_s[g, mine, :] for g in range(HEADS)], 0
        ).astype(BF)


def project(blk, acts, gain, wq, wk, wv, table):
    sd = jax.ShapeDtypeStruct
    return pl.pallas_call(
        project_body,
        in_specs=[spec(SM)] + [spec(VM)] * (TP + 1) + [spec(ANY)] * 3 + [spec(VM)],
        out_specs=[spec(VM)] * 4,
        out_shape=[
            sd((NP * GROUP, HD), BF),
            sd((ROWS, HD), BF),
            sd((ROWS, HD), BF),
            sd((NP, 2 * STEPS, HD), BF),
        ],
        scratch_shapes=[
            VM((TP, DB, DB), BF),
            VM((TP, DB, HD), BF),
            VM((TP, DB, HD), BF),
            VM((HEADS, ROWS, HD), F32),
            VM((ROWS, HD), F32),
            VM((ROWS, HD), F32),
            pltpu.SemaphoreType.DMA((3, TP)),
        ],
        compiler_params=limit(55),
        cost_estimate=pl.CostEstimate(
            flops=2 * ROWS * D * 768, bytes_accessed=7 * 2**20, transcendentals=0
        ),
        name="project",
    )(blk, *acts, gain, wq, wk, wv, table)


def attend_body(blk, qa, kf, vf, kc, vc, wo, *refs):
    outs = refs[:TP]
    s1_s, ctx_s, wo_s, sems = refs[TP:]
    copies = []
    for s in range(TP):
        there = pl.ds(pl.multiple_of(blk[TP + s] * DB, DB), DB)
        copies.append(pltpu.make_async_copy(wo.at[:, there], wo_s.at[s], sems.at[s]))
    for c in copies:
        c.start()
    for n in range(NP):
        span = slice(n * GROUP, (n + 1) * GROUP)
        s1_s[span, :] = nt(qa[span, :], kc[n])
    scale = 1.0 / HD**0.5
    s1 = s1_s[...] * scale
    s2 = nt(qa[...], kf[...]) * scale
    row = lax.broadcasted_iota(jnp.int32, (NP * GROUP, ROWS), 0)
    col = lax.broadcasted_iota(jnp.int32, (NP * GROUP, ROWS), 1)
    seen = ((row // GROUP) == (col % NP)) & ((col // NP) <= (row % STEPS))
    s2 = jnp.where(seen, s2, -jnp.inf)
    top = jnp.maximum(jnp.max(s1, -1, keepdims=True), jnp.max(s2, -1, keepdims=True))
    e1 = jnp.exp(s1 - top)
    e2 = jnp.exp(s2 - top)
    total = jnp.sum(e1, -1, keepdims=True) + jnp.sum(e2, -1, keepdims=True)
    w1 = (e1 / total).astype(BF)
    w2 = (e2 / total).astype(BF)
    c2 = mm(w2, vf[...])
    for n in range(NP):
        span = slice(n * GROUP, (n + 1) * GROUP)
        cn = (mm(w1[span], vc[n]) + c2[span]).astype(BF).astype(F32)
        for g in range(HEADS):
            ctx_s[g, pl.ds(n, STEPS, stride=NP), :] = cn[g * STEPS : (g + 1) * STEPS]
    ctx = jnp.concatenate([ctx_s[g] for g in range(HEADS)], 1).astype(BF)
    for s in range(TP):
        copies[s].wait()
        outs[s][...] = mm(ctx, wo_s[s]).astype(BF)


def attend(blk, qa, kf, vf, kc, vc, wo):
    return pl.pallas_call(
        attend_body,
        in_specs=[spec(SM)] + [spec(VM)] * 5 + [spec(ANY)],
        out_specs=[spec(VM)] * TP,
        out_shape=[jax.ShapeDtypeStruct((ROWS, DB), BF)] * TP,
        scratch_shapes=[
            VM((NP * GROUP, SPAN), F32),
            VM((HEADS, ROWS, HD), F32),
            VM((TP, DB, DB), BF),
            pltpu.SemaphoreType.DMA((TP,)),
        ],
        compiler_params=limit(55),
        cost_estimate=pl.CostEstimate(
            flops=2 * ROWS * D * 640, bytes_accessed=6 * 2**20, transcendentals=NP * 16 * 192
        ),
        name="attend",
    )(blk, qa, kf, vf, kc, vc, wo)


def mix_body(*refs):
    parts = refs[:TP]
    act, twist, attn, sums = refs[TP:]
    mix = parts[0][...].astype(F32)
    for s in range(1, TP):
        mix = mix + parts[s][...].astype(F32)
    attn[...] = mix.astype(BF)
    summed = act[...].astype(F32) + mix
    aligned = jnp.sum(summed * twist[...], -1, keepdims=True)
    energy = jnp.sum(summed * summed, -1, keepdims=True)
    row = lax.broadcasted_iota(jnp.int32, (ROWS, HD), 0)
    lane = lax.broadcasted_iota(jnp.int32, (ROWS, HD), 1)
    both = jnp.where(lane == row, aligned, 0.0) + jnp.where(lane == row + ROWS, energy, 0.0)
    sums[...] = jnp.broadcast_to(jnp.sum(both, 0, keepdims=True)[None], (TP, 1, HD))


def mix(parts, act, twist):
    sd = jax.ShapeDtypeStruct
    return pl.pallas_call(
        mix_body,
        in_specs=[spec(VM)] * (TP + 2),
        out_specs=[spec(VM)] * 2,
        out_shape=[sd((ROWS, DB), BF), sd((TP, 1, HD), F32)],
        compiler_params=limit(8),
        name="mix",
    )(*parts, act, twist)


def weigh_body(idx, sums, reward, previous, fresh, line, sent):
    total = sums[0]
    for t in range(1, TP):
        total = total + sums[t]
    energy = pltpu.roll(total, ROWS, 1)
    score = total / jnp.sqrt(energy / D + 1e-06) + reward[...]
    gain = score
    for t in range(1, STEPS):
        gain = gain + pltpu.roll(score, HD - NP * t, 1)
    logw = previous[...] + gain
    line[...] = logw
    high = logw.astype(BF).astype(F32)
    middle = (logw - high).astype(BF).astype(F32)
    low = logw - high - middle
    row = lax.broadcasted_iota(jnp.int32, (8, HD), 0)
    parts = jnp.where(row == 0, high, jnp.where(row == 1, middle, jnp.where(row == 2, low, 0.0)))
    parts = parts.astype(BF)
    for d in range(NDOM):
        sent[d, 0] = fresh[idx[1, 2 * d]]
        sent[d, 1] = fresh[idx[1, 2 * d + 1]]
        sent[d, 2] = parts


def weigh(idx, sums, reward, previous, fresh):
    sd = jax.ShapeDtypeStruct
    return pl.pallas_call(
        weigh_body,
        in_specs=[spec(SM)] + [spec(VM)] * 4,
        out_specs=[spec(VM)] * 2,
        out_shape=[sd((1, HD), F32), sd((NDOM, 3, 8, HD), BF)],
        compiler_params=limit(8),
        name="weigh",
    )(idx, sums, reward, previous, fresh)


def finish_body(idx, line, got, keys_in, values_in, logw, keys, values, all_s, f_s, k_s, v_s, sems):
    for k in range(NP):
        code = idx[1, 64 + k]
        f_s[pl.ds(k, 2 * STEPS, stride=NP), :] = got[code // 2, code % 2].astype(F32)
    half = STEPS * NP
    k_s[...] = f_s[0:half, :].reshape(STEPS, NP, HD).astype(BF)
    v_s[...] = f_s[half : 2 * half, :].reshape(STEPS, NP, HD).astype(BF)
    tail = pl.ds(SPAN, STEPS)
    copies = [
        pltpu.make_async_copy(k_s, keys.at[tail], sems.at[0]),
        pltpu.make_async_copy(v_s, values.at[tail], sems.at[1]),
    ]
    for c in copies:
        c.start()
    for d in range(NDOM):
        all_s[d : d + 1, :] = jnp.sum(got[d, 2].astype(F32), 0, keepdims=True)
    lane = lax.broadcasted_iota(jnp.int32, (NDOM, HD), 1)
    all_w = jnp.where(lane < NP, all_s[...], -jnp.inf)
    largest = jnp.max(all_w, keepdims=True)
    mass = jnp.sum(jnp.exp(all_w - largest), keepdims=True)
    logw[...] = (line[...] - (largest + jnp.log(mass)))[:, 0:NP]
    for c in copies:
        c.wait()


def finish(idx, line, got, keys, values):
    sd = jax.ShapeDtypeStruct
    return pl.pallas_call(
        finish_body,
        in_specs=[spec(SM)] + [spec(VM)] * 2 + [spec(ANY)] * 2,
        out_specs=[spec(VM)] + [spec(ANY)] * 2,
        out_shape=[sd((1, NP), F32), sd(keys.shape, BF), sd(values.shape, BF)],
        scratch_shapes=[
            VM((NDOM, HD), F32),
            VM((2 * STEPS * NP, HD), F32),
            VM((STEPS, NP, HD), BF),
            VM((STEPS, NP, HD), BF),
            pltpu.SemaphoreType.DMA((2,)),
        ],
        input_output_aliases={3: 1, 4: 2},
        compiler_params=limit(8),
        name="finish",
    )(idx, line, got, keys, values)


def plan_body(me_ref, counts_ref, out):
    me = me_ref[0]
    counts = counts_ref[:, 0, 0:NP].astype(F32)
    r16 = lax.broadcasted_iota(jnp.int32, (NP, NP), 0)
    c16 = lax.broadcasted_iota(jnp.int32, (NP, NP), 1)
    within = mm(counts, (r16 <= c16).astype(F32))
    r32 = lax.broadcasted_iota(jnp.int32, (NDOM, NDOM), 0)
    c32 = lax.broadcasted_iota(jnp.int32, (NDOM, NDOM), 1)
    before = jnp.sum(mm((c32 < r32).astype(F32), counts), -1, keepdims=True)
    ends = (within + before).astype(jnp.int32)
    before = before.astype(jnp.int32)
    device = lax.broadcasted_iota(jnp.int32, (NDOM, 1), 0)
    chip_end = jnp.where(device % 2 == 1, ends[:, NP - 1 : NP], -1)
    chip = me // 2
    first = jnp.sum(jnp.where(device == 2 * chip, before, 0))
    lane = lax.broadcasted_iota(jnp.int32, (1, HD), 1)
    dest = 2 * (lane // 4) + me % 2
    sent = first + ((dest - first) & (NDOM - 1)) + NDOM * (lane % 4)
    kept = NDOM * (lane - 64) + me
    found = jnp.zeros((NDOM, HD), jnp.int32)
    for j in range(NP):
        found = found + (ends[:, j : j + 1] <= sent).astype(jnp.int32)
    particle = jnp.sum(found, 0, keepdims=True) - 2 * NP * chip
    particle = jnp.clip(particle, 0, 2 * NP - 1)
    passed = (chip_end >= 0) & (chip_end <= kept)
    source = jnp.sum(passed.astype(jnp.int32), 0, keepdims=True)
    base = jnp.max(jnp.where(passed, chip_end, 0), 0, keepdims=True)
    slot = jnp.clip((kept - base) // NDOM, 0, 3)
    arrived = 4 * jnp.clip(source, 0, NCHIP - 1) + slot
    owned = jnp.sum(counts, -1, keepdims=True).astype(jnp.int32)
    pair = lax.broadcasted_iota(jnp.int32, (NDOM, HD), 1)
    most = jnp.max(jnp.sum(jnp.where(pair == device // 2, owned, 0), 0, keepdims=True))
    line = jnp.where(lane < 64, particle, jnp.where(lane < 80, arrived, most))

    own = jnp.sum(jnp.where(device == me, before, 0))
    sent = own + ((lane // 2 - own) & (NDOM - 1)) + NDOM * (lane % 2)
    found = jnp.zeros((NDOM, HD), jnp.int32)
    for j in range(NP):
        found = found + (ends[:, j : j + 1] <= sent).astype(jnp.int32)
    particle = jnp.sum(found, 0, keepdims=True) - NP * me
    particle = jnp.clip(particle, 0, NP - 1)
    passed = ends[:, NP - 1 : NP] <= kept
    source = jnp.sum(passed.astype(jnp.int32), 0, keepdims=True)
    base = jnp.max(jnp.where(passed, ends[:, NP - 1 : NP], 0), 0, keepdims=True)
    slot = jnp.clip((kept - base) // NDOM, 0, 1)
    arrived = 2 * jnp.clip(source, 0, NDOM - 1) + slot
    second = jnp.where(lane < 64, particle, arrived)
    row = lax.broadcasted_iota(jnp.int32, (8, HD), 0)
    out[...] = jnp.where(row == 0, line, second)


def plan(me, counts):
    return pl.pallas_call(
        plan_body,
        in_specs=[spec(SM), spec(VM)],
        out_specs=spec(VM),
        out_shape=jax.ShapeDtypeStruct((8, HD), jnp.int32),
        compiler_params=limit(8),
        name="plan",
    )(me, counts)


def pack_body(me_ref, idx, *refs):
    half = (len(refs) - 3) // 2
    own, partner = (refs[:half], refs[half : 2 * half])
    out, rows, sems = refs[2 * half :]
    core = me_ref[0] % 2
    loads, at = ([], 0)
    for n in range(half):
        length = own[n].shape[1]
        for side, ref in ((core, own[n]), (1 - core, partner[n])):
            there = rows.at[pl.ds(side * NP, NP), pl.ds(at, length), :]
            loads.append(pltpu.make_async_copy(ref, there, sems.at[len(loads) + 1]))
        at += length
    for c in loads:
        c.start()
    for c in loads:
        c.wait()
    for q in range(NCHIP):
        for s in range(SLOTS):
            pltpu.make_async_copy(rows.at[idx[0, 4 * q + s]], out.at[q, s], sems.at[0]).start()
    pltpu.make_async_copy(out, out, sems.at[0]).wait()


def pack(me, idx, own, partner):
    length = sum(a.shape[1] for a in own)
    return pl.pallas_call(
        pack_body,
        in_specs=[spec(SM), spec(SM)] + [spec(ANY)] * (2 * len(own)),
        out_specs=spec(ANY),
        out_shape=jax.ShapeDtypeStruct((NCHIP, SLOTS, length, HD), BF),
        scratch_shapes=[
            VM((2 * NP, length, HD), BF),
            pltpu.SemaphoreType.DMA((1 + 2 * len(own),)),
        ],
        compiler_params=limit(16),
        name="pack",
    )(me, idx, *own, *partner)


def place_body(slots, idx, rows, keys, values, sems):
    copies = []
    for k in range(NP):
        code = idx[0, 64 + k]
        slot = jnp.minimum(code % 4, slots - 1)
        for n, out in enumerate((keys, values)):
            part = rows.at[code // 4, slot, pl.ds(n * SPAN, SPAN), :]
            copies.append(pltpu.make_async_copy(part, out.at[k], sems.at[n, k]))
    for c in copies:
        c.start()
    for c in copies:
        c.wait()


def place(idx, rows):
    slots = rows.shape[1]
    return pl.pallas_call(
        lambda *refs: place_body(slots, *refs),
        in_specs=[spec(SM), spec(ANY)],
        out_specs=[spec(VM)] * 2,
        out_shape=[jax.ShapeDtypeStruct((NP, SPAN, HD), BF)] * 2,
        scratch_shapes=[pltpu.SemaphoreType.DMA((2, NP))],
        compiler_params=limit(16),
        name="place",
    )(idx, rows)


def shifted(value, shift):
    return lax.ppermute(value, "tp", [(i, (i + shift) % TP) for i in range(TP)])


def swapped(value):
    return lax.ppermute(value, "dom", [(i, i ^ 1) for i in range(NDOM)])


def next_chip(value):
    return lax.ppermute(value, "dom", [(i, (i + 2) % NDOM) for i in range(NDOM)])


SAME_CORE = [list(range(c, NDOM, 2)) for c in range(2)]


def exchanged(rows):
    return lax.all_to_all(rows, "dom", 0, 0, tiled=True, axis_index_groups=SAME_CORE)


def counts_of_all(counts):
    line = jnp.pad(counts, (0, HD - NP))
    sent = jnp.broadcast_to(line[None, None], (NDOM, 8, HD))
    return lax.all_to_all(sent, "dom", 0, 0, tiled=True)


def rotation_table():
    frequency = np.float32(500000.0) ** (-2.0 * np.arange(HD // 2, dtype=np.float32) / HD)
    angles = (SPAN + np.arange(STEPS, dtype=np.float32))[:, None] * frequency.astype(np.float32)
    cosine = np.concatenate([np.cos(angles), np.cos(angles)], 1)
    sine = np.concatenate([-np.sin(angles), np.sin(angles)], 1)
    return np.stack([np.repeat(cosine, NP, 0), np.repeat(sine, NP, 0)]).astype(np.float32)


def local(
    activations,
    norm_gain,
    w_query,
    w_key,
    value_weight,
    w_output,
    cache_keys,
    cache_values,
    tokens,
    twisting_table,
    twist_vec,
    previous_log_weights,
    copy_counts,
):
    dom = lax.axis_index("dom")
    tp = lax.axis_index("tp")
    me = dom.reshape(1)
    ring = np.arange(TP)
    blk = (jnp.concatenate([tp - ring, tp + ring]) % TP).astype(jnp.int32)
    act = activations.reshape(ROWS, DB)

    counts = counts_of_all(copy_counts)
    acts = [act] + [shifted(act, s) for s in range(1, TP)]
    counts, *acts[2:6] = lax.optimization_barrier((counts, *acts[2:6]))
    partner_keys = swapped(cache_keys)
    partner_values = swapped(cache_values)
    idx = plan(me, counts)
    packed = pack(me, idx, [cache_keys, cache_values], [partner_keys, partner_values])
    rows = exchanged(packed)
    reward = twisting_table[tokens.reshape(ROWS)].astype(F32)
    reward = jnp.pad(reward, (0, HD - ROWS)).reshape(1, HD)
    previous = jnp.pad(previous_log_weights, (0, HD - NP)).reshape(1, HD)

    packed, *acts = lax.optimization_barrier((packed, *acts))
    qa, kf, vf, fresh = project(
        blk, acts, norm_gain.reshape(TP, DB), w_query, w_key, value_weight, rotation_table()
    )
    partials = attend(blk, qa, kf, vf, cache_keys, cache_values, w_output)
    parts = [partials[0]] + [shifted(partials[s], s) for s in range(1, TP)]
    attn, sums = mix(parts, act, twist_vec.reshape(1, DB))
    sums, rows, reward, previous = lax.optimization_barrier((sums, rows, reward, previous))
    sums = lax.all_to_all(sums, "tp", 0, 0, tiled=True)
    line, sent = weigh(idx, sums, reward, previous, fresh)
    got = lax.all_to_all(sent, "dom", 0, 0, tiled=True)

    def usual(rows, *_):
        return tuple(place(idx, rows))

    def crowded(rows, partner_keys, partner_values, idx):
        even = dom % 2 == 0
        mine = jnp.concatenate([cache_keys, cache_values], 1)
        other = jnp.concatenate([partner_keys, partner_values], 1)
        chip_rows = jnp.concatenate(
            [jnp.where(even, mine, other), jnp.where(even, other, mine)], 0
        )
        chosen = chip_rows[idx[0, 3:64:4]]
        chip = dom // 2

        def turn(step, state):
            passing, more = state
            passing = next_chip(passing)
            return passing, more.at[(chip - step) % NCHIP].set(passing[chip])

        start = (chosen, chosen)
        more = lax.fori_loop(1, NCHIP, turn, start)[1].at[chip].set(chosen[chip])
        return tuple(place(idx, jnp.concatenate([rows, more[:, None]], 1)))

    old_keys, old_values = lax.cond(
        idx[0, 127] > SLOTS * NDOM,
        crowded,
        usual,
        rows,
        partner_keys,
        partner_values,
        idx,
    )

    def by_position(old):
        return jnp.pad(jnp.transpose(old, (1, 0, 2)), ((0, STEPS), (0, 0), (0, 0)))

    out_logw, new_keys, new_values = finish(
        idx, line, got, by_position(old_keys), by_position(old_values)
    )
    return (
        attn.reshape(STEPS, NP, DB),
        jnp.transpose(new_keys, (1, 0, 2)),
        jnp.transpose(new_values, (1, 0, 2)),
        out_logw.reshape(NP),
    )


def solution(mesh):
    return jax.shard_map(
        local,
        mesh=mesh,
        in_specs=(
            P(None, "dom", "tp"),
            P(),
            P(None, "tp"),
            P(None, "tp"),
            P(None, "tp"),
            P("tp", None),
            P("dom", None, "tp"),
            P("dom", None, "tp"),
            P(None, "dom"),
            P(),
            P("tp"),
            P("dom"),
            P("dom"),
        ),
        out_specs=(P(None, "dom", "tp"), P("dom", None, "tp"), P("dom", None, "tp"), P("dom")),
        check_vma=False,
    )
```

```python
import jax
import jax.numpy as jnp
import numpy as np
from jax import lax
from jax.experimental import pallas as pl
from jax.experimental.pallas import tpu as pltpu
from jax.sharding import PartitionSpec as P

D = 4096
HD = 128
STEPS = 4
NP = 16
ROWS = STEPS * NP
SPAN = 128
TP = 8
DB = D // TP
HEADS = DB // HD
GROUP = HEADS * STEPS
NDOM = 32
NCHIP = 16
SLOTS = 3
BF = jnp.bfloat16
F32 = jnp.float32
ANY = pl.ANY
VM = pltpu.VMEM
SM = pltpu.SMEM


def spec(space):
    return pl.BlockSpec(memory_space=space)


def limit(mib):
    return pltpu.CompilerParams(vmem_limit_bytes=mib * 2**20)


def nt(a, b):
    return lax.dot_general(a, b, (((1,), (1,)), ((), ())), preferred_element_type=F32)


def mm(a, b):
    return jnp.dot(a, b, preferred_element_type=F32)


def project_body(acts, gain, wq, wk, wv, table, qa, kf, vf, fresh, *scratch):
    wq_s, wk_s, wv_s, q_s, kf_s, vf_s, sems = scratch
    copies = []
    for s in range(TP):
        part = pl.ds(s * DB, DB)
        copies.append(
            [
                pltpu.make_async_copy(w.at[part, :], w_s.at[s], sems.at[n, s])
                for n, (w, w_s) in enumerate(((wq, wq_s), (wk, wk_s), (wv, wv_s)))
            ]
        )
    for group in copies:
        for c in group:
            c.start()
    square = jnp.zeros((ROWS, 1), F32)
    for s in range(TP):
        x = acts[s].astype(F32)
        square = square + jnp.sum(x * x, -1, keepdims=True)
    inv = lax.rsqrt(square / D + 1e-05)
    q = jnp.zeros((ROWS, DB), F32)
    k = jnp.zeros((ROWS, HD), F32)
    v = jnp.zeros((ROWS, HD), F32)
    for s in range(TP):
        x = acts[s].astype(F32)
        normed = (x * inv * gain[s : s + 1, :]).astype(BF)
        for c in copies[s]:
            c.wait()
        q = q + mm(normed, wq_s[s])
        k = k + mm(normed, wk_s[s])
        v = v + mm(normed, wv_s[s])
    cosine = table[0]
    sine = table[1]

    def turned(u):
        return (u * cosine + pltpu.roll(u, HD // 2, 1) * sine).astype(BF)

    for g in range(HEADS):
        q_s[g] = turned(q[:, g * HD : (g + 1) * HD]).astype(F32)
    k = turned(k)
    v = v.astype(BF)
    kf[...] = k
    vf[...] = v
    kf_s[...] = k.astype(F32)
    vf_s[...] = v.astype(F32)
    for n in range(NP):
        mine = pl.ds(n, STEPS, stride=NP)
        fresh[n] = jnp.concatenate([kf_s[mine, :], vf_s[mine, :]], 0).astype(BF)
        qa[n * GROUP : (n + 1) * GROUP, :] = jnp.concatenate(
            [q_s[g, mine, :] for g in range(HEADS)], 0
        ).astype(BF)


def project(acts, gain, wq, wk, wv, table):
    sd = jax.ShapeDtypeStruct
    return pl.pallas_call(
        project_body,
        in_specs=[spec(VM)] * 2 + [spec(ANY)] * 3 + [spec(VM)],
        out_specs=[spec(VM)] * 4,
        out_shape=[
            sd((NP * GROUP, HD), BF),
            sd((ROWS, HD), BF),
            sd((ROWS, HD), BF),
            sd((NP, 2 * STEPS, HD), BF),
        ],
        scratch_shapes=[
            VM((TP, DB, DB), BF),
            VM((TP, DB, HD), BF),
            VM((TP, DB, HD), BF),
            VM((HEADS, ROWS, HD), F32),
            VM((ROWS, HD), F32),
            VM((ROWS, HD), F32),
            pltpu.SemaphoreType.DMA((3, TP)),
        ],
        compiler_params=limit(55),
        cost_estimate=pl.CostEstimate(
            flops=2 * ROWS * D * 768, bytes_accessed=7 * 2**20, transcendentals=0
        ),
        name="project",
    )(acts, gain, wq, wk, wv, table)


def attend_body(blk, qa, kf, vf, kc, vc, wo, *refs):
    outs = refs[:TP]
    s1_s, ctx_s, wo_s, sems = refs[TP:]
    copies = []
    for s in range(TP):
        there = pl.ds(pl.multiple_of(blk[s] * DB, DB), DB)
        copies.append(pltpu.make_async_copy(wo.at[:, there], wo_s.at[s], sems.at[s]))
    for c in copies:
        c.start()
    for n in range(NP):
        span = slice(n * GROUP, (n + 1) * GROUP)
        s1_s[span, :] = nt(qa[span, :], kc[n])
    scale = 1.0 / HD**0.5
    s1 = s1_s[...] * scale
    s2 = nt(qa[...], kf[...]) * scale
    row = lax.broadcasted_iota(jnp.int32, (NP * GROUP, ROWS), 0)
    col = lax.broadcasted_iota(jnp.int32, (NP * GROUP, ROWS), 1)
    seen = ((row // GROUP) == (col % NP)) & ((col // NP) <= (row % STEPS))
    s2 = jnp.where(seen, s2, -jnp.inf)
    top = jnp.maximum(jnp.max(s1, -1, keepdims=True), jnp.max(s2, -1, keepdims=True))
    e1 = jnp.exp(s1 - top)
    e2 = jnp.exp(s2 - top)
    total = jnp.sum(e1, -1, keepdims=True) + jnp.sum(e2, -1, keepdims=True)
    w1 = (e1 / total).astype(BF)
    w2 = (e2 / total).astype(BF)
    c2 = mm(w2, vf[...])
    for n in range(NP):
        span = slice(n * GROUP, (n + 1) * GROUP)
        cn = (mm(w1[span], vc[n]) + c2[span]).astype(BF).astype(F32)
        for g in range(HEADS):
            ctx_s[g, pl.ds(n, STEPS, stride=NP), :] = cn[g * STEPS : (g + 1) * STEPS]
    ctx = jnp.concatenate([ctx_s[g] for g in range(HEADS)], 1).astype(BF)
    for s in range(TP):
        copies[s].wait()
        outs[s][...] = mm(ctx, wo_s[s]).astype(BF)


def attend(blk, qa, kf, vf, kc, vc, wo):
    return pl.pallas_call(
        attend_body,
        in_specs=[spec(SM)] + [spec(VM)] * 5 + [spec(ANY)],
        out_specs=[spec(VM)] * TP,
        out_shape=[jax.ShapeDtypeStruct((ROWS, DB), BF)] * TP,
        scratch_shapes=[
            VM((NP * GROUP, SPAN), F32),
            VM((HEADS, ROWS, HD), F32),
            VM((TP, DB, DB), BF),
            pltpu.SemaphoreType.DMA((TP,)),
        ],
        compiler_params=limit(55),
        cost_estimate=pl.CostEstimate(
            flops=2 * ROWS * D * 640, bytes_accessed=6 * 2**20, transcendentals=NP * 16 * 192
        ),
        name="attend",
    )(blk, qa, kf, vf, kc, vc, wo)


def mix_body(*refs):
    parts = refs[:TP]
    act, twist, base, attn, message = refs[TP:]
    mix = parts[0][...].astype(F32)
    for s in range(1, TP):
        mix = mix + parts[s][...].astype(F32)
    attn[...] = mix.astype(BF)
    summed = act[...].astype(F32) + mix
    aligned = jnp.sum(summed * twist[...], -1, keepdims=True)
    energy = jnp.sum(summed * summed, -1, keepdims=True)
    row = lax.broadcasted_iota(jnp.int32, (ROWS, HD), 0)
    lane = lax.broadcasted_iota(jnp.int32, (ROWS, HD), 1)
    both = jnp.where(lane == row, aligned, 0.0) + jnp.where(lane == row + ROWS, energy, 0.0)
    line = jnp.concatenate([jnp.sum(both, 0, keepdims=True), base[...]], 0)
    message[...] = jnp.broadcast_to(line[None], (NDOM * TP, 2, HD))


def mix(parts, act, twist, base):
    sd = jax.ShapeDtypeStruct
    return pl.pallas_call(
        mix_body,
        in_specs=[spec(VM)] * (TP + 3),
        out_specs=[spec(VM)] * 2,
        out_shape=[sd((ROWS, DB), BF), sd((NDOM * TP, 2, HD), F32)],
        compiler_params=limit(8),
        name="mix",
    )(*parts, act, twist, base)


def finish_body(me_ref, got, out, logw_s):
    total = got[:, 0]
    for t in range(1, TP):
        total = total + got[:, t]
    sums = total[:, 0, :]
    energy = pltpu.roll(sums, ROWS, 1)
    score = sums / jnp.sqrt(energy / D + 1e-06)
    logw = total[:, 1, :] + score
    for t in range(1, STEPS):
        logw = logw + pltpu.roll(score, HD - NP * t, 1)
    lane = lax.broadcasted_iota(jnp.int32, (NDOM, HD), 1)
    logw = jnp.where(lane < NP, logw, -jnp.inf)
    logw_s[...] = logw
    largest = jnp.max(logw, keepdims=True)
    mass = jnp.sum(jnp.exp(logw - largest), keepdims=True)
    mine = logw_s[pl.ds(me_ref[0], 1), :]
    out[...] = (mine - (largest + jnp.log(mass)))[:, 0:NP]


def finish(me, got):
    return pl.pallas_call(
        finish_body,
        in_specs=[spec(SM), spec(VM)],
        out_specs=spec(VM),
        out_shape=jax.ShapeDtypeStruct((1, NP), F32),
        scratch_shapes=[VM((NDOM, HD), F32)],
        compiler_params=limit(8),
        name="finish",
    )(me, got)


def plan_body(me_ref, *refs):
    out = refs[-1]
    me = me_ref[0]
    blocks = jnp.concatenate([r[...] for r in refs[:-1]], 0).astype(F32)
    rel = lax.broadcasted_iota(jnp.int32, (NDOM, NDOM), 1)
    back_y = (me // 8 - rel // 8) & 3
    back_x = (me // 2 - rel // 2) & 3
    holder = 8 * back_y + 2 * back_x + ((me + rel) & 1)
    sorted_rows = lax.broadcasted_iota(jnp.int32, (NDOM, NDOM), 0) == holder
    counts = mm(sorted_rows.astype(F32), blocks)
    r16 = lax.broadcasted_iota(jnp.int32, (NP, NP), 0)
    c16 = lax.broadcasted_iota(jnp.int32, (NP, NP), 1)
    within = mm(counts, (r16 <= c16).astype(F32))
    r32 = lax.broadcasted_iota(jnp.int32, (NDOM, NDOM), 0)
    c32 = lax.broadcasted_iota(jnp.int32, (NDOM, NDOM), 1)
    before = jnp.sum(mm((c32 < r32).astype(F32), counts), -1, keepdims=True)
    ends = (within + before).astype(jnp.int32)
    before = before.astype(jnp.int32)
    device = lax.broadcasted_iota(jnp.int32, (NDOM, 1), 0)
    chip_end = jnp.where(device % 2 == 1, ends[:, NP - 1 : NP], -1)
    chip = me // 2
    first = jnp.sum(jnp.where(device == 2 * chip, before, 0))
    lane = lax.broadcasted_iota(jnp.int32, (1, HD), 1)
    dest = 2 * (lane // 4) + me % 2
    sent = first + ((dest - first) & (NDOM - 1)) + NDOM * (lane % 4)
    kept = NDOM * (lane - 64) + me
    found = jnp.zeros((NDOM, HD), jnp.int32)
    for j in range(NP):
        found = found + (ends[:, j : j + 1] <= sent).astype(jnp.int32)
    particle = jnp.sum(found, 0, keepdims=True) - 2 * NP * chip
    particle = jnp.clip(particle, 0, 2 * NP - 1)
    passed = (chip_end >= 0) & (chip_end <= kept)
    source = jnp.sum(passed.astype(jnp.int32), 0, keepdims=True)
    base = jnp.max(jnp.where(passed, chip_end, 0), 0, keepdims=True)
    slot = jnp.clip((kept - base) // NDOM, 0, 3)
    arrived = 4 * jnp.clip(source, 0, NCHIP - 1) + slot
    owned = jnp.sum(counts, -1, keepdims=True).astype(jnp.int32)
    pair = lax.broadcasted_iota(jnp.int32, (NDOM, HD), 1)
    most = jnp.max(jnp.sum(jnp.where(pair == device // 2, owned, 0), 0, keepdims=True))
    line = jnp.where(lane < 64, particle, jnp.where(lane < 80, arrived, most))

    found = jnp.zeros((NDOM, HD), jnp.int32)
    for j in range(NP):
        found = found + (ends[:, j : j + 1] <= kept).astype(jnp.int32)
    owner = jnp.clip(jnp.sum(found, 0, keepdims=True), 0, NDOM * NP - 1)
    row = lax.broadcasted_iota(jnp.int32, (8, HD), 0)
    out[...] = jnp.where(row == 0, line, owner)


def plan(me, blocks):
    return pl.pallas_call(
        plan_body,
        in_specs=[spec(SM)] + [spec(VM)] * len(blocks),
        out_specs=spec(VM),
        out_shape=jax.ShapeDtypeStruct((8, HD), jnp.int32),
        compiler_params=limit(8),
        name="plan",
    )(me, *blocks)


def pack_body(me_ref, idx, *refs):
    half = (len(refs) - 3) // 2
    own, partner = (refs[:half], refs[half : 2 * half])
    out, rows, sems = refs[2 * half :]
    core = me_ref[0] % 2
    loads, at = ([], 0)
    for n in range(half):
        length = own[n].shape[1]
        for side, ref in ((core, own[n]), (1 - core, partner[n])):
            there = rows.at[pl.ds(side * NP, NP), pl.ds(at, length), :]
            loads.append(pltpu.make_async_copy(ref, there, sems.at[len(loads) + 1]))
        at += length
    for c in loads:
        c.start()
    for c in loads:
        c.wait()
    for q in range(NCHIP):
        for s in range(SLOTS):
            pltpu.make_async_copy(rows.at[idx[0, 4 * q + s]], out.at[q, s], sems.at[0]).start()
    pltpu.make_async_copy(out, out, sems.at[0]).wait()


def pack(me, idx, own, partner):
    length = sum(a.shape[1] for a in own)
    return pl.pallas_call(
        pack_body,
        in_specs=[spec(SM), spec(SM)] + [spec(ANY)] * (2 * len(own)),
        out_specs=spec(ANY),
        out_shape=jax.ShapeDtypeStruct((NCHIP, SLOTS, length, HD), BF),
        scratch_shapes=[
            VM((2 * NP, length, HD), BF),
            pltpu.SemaphoreType.DMA((1 + 2 * len(own),)),
        ],
        compiler_params=limit(16),
        name="pack",
    )(me, idx, *own, *partner)


def place_body(slots, idx, rows, fresh, keys, values, r_s, f_s, sems):
    copies = []
    for k in range(NP):
        code = idx[0, 64 + k]
        slot = jnp.minimum(code % 4, slots - 1)
        copies.append(
            pltpu.make_async_copy(rows.at[code // 4, slot], r_s.at[k], sems.at[0, k])
        )
        copies.append(
            pltpu.make_async_copy(fresh.at[idx[1, 64 + k]], f_s.at[k], sems.at[1, k])
        )
    for c in copies:
        c.start()
    for k in range(NP):
        copies[2 * k].wait()
        copies[2 * k + 1].wait()
        keys[k, 0:SPAN, :] = r_s[k, 0:SPAN, :]
        values[k, 0:SPAN, :] = r_s[k, SPAN : 2 * SPAN, :]
        tail = f_s[k].astype(F32)
        keys[k, SPAN : SPAN + STEPS, :] = tail[0:STEPS].astype(BF)
        values[k, SPAN : SPAN + STEPS, :] = tail[STEPS : 2 * STEPS].astype(BF)


def place(idx, rows, fresh):
    out = jax.ShapeDtypeStruct((NP, SPAN + STEPS, HD), BF)
    slots = rows.shape[1]
    return pl.pallas_call(
        lambda *refs: place_body(slots, *refs),
        in_specs=[spec(SM), spec(ANY), spec(ANY)],
        out_specs=[spec(VM)] * 2,
        out_shape=[out] * 2,
        scratch_shapes=[
            VM((NP, 2 * SPAN, HD), BF),
            VM((NP, 2 * STEPS, HD), BF),
            pltpu.SemaphoreType.DMA((2, NP)),
        ],
        compiler_params=limit(16),
        name="place",
    )(idx, rows, fresh)


def shifted(value, shift):
    return lax.ppermute(value, "tp", [(i, (i + shift) % TP) for i in range(TP)])


def swapped(value):
    return lax.ppermute(value, "dom", [(i, i ^ 1) for i in range(NDOM)])


def next_chip(value):
    return lax.ppermute(value, "dom", [(i, (i + 2) % NDOM) for i in range(NDOM)])


SAME_CORE = [list(range(c, NDOM, 2)) for c in range(2)]


def exchanged(rows):
    return lax.all_to_all(rows, "dom", 0, 0, tiled=True, axis_index_groups=SAME_CORE)


def moved(value, axis_stride, shift):
    def to(i):
        at = i // axis_stride % 4
        return i + ((at + shift) % 4 - at) * axis_stride

    return lax.ppermute(value, "dom", [(i, to(i)) for i in range(NDOM)])


def spread_counts(copy_counts):
    own = copy_counts.reshape(1, NP)
    chip = jnp.concatenate([own, swapped(own)], 0)
    row = jnp.concatenate([chip] + [moved(chip, 2, s) for s in range(1, 4)], 0)
    return [row] + [moved(row, 8, s) for s in range(1, 4)]


def rotation_table():
    frequency = np.float32(500000.0) ** (-2.0 * np.arange(HD // 2, dtype=np.float32) / HD)
    angles = (SPAN + np.arange(STEPS, dtype=np.float32))[:, None] * frequency.astype(np.float32)
    cosine = np.concatenate([np.cos(angles), np.cos(angles)], 1)
    sine = np.concatenate([-np.sin(angles), np.sin(angles)], 1)
    return np.stack([np.repeat(cosine, NP, 0), np.repeat(sine, NP, 0)]).astype(np.float32)


def local(
    activations,
    norm_gain,
    w_query,
    w_key,
    value_weight,
    w_output,
    cache_keys,
    cache_values,
    tokens,
    twisting_table,
    twist_vec,
    previous_log_weights,
    copy_counts,
):
    dom = lax.axis_index("dom")
    tp = lax.axis_index("tp")
    me = dom.reshape(1)
    blk = ((tp + np.arange(TP)) % TP).astype(jnp.int32)
    act = activations.reshape(ROWS, DB)

    gathered = lax.all_to_all(
        jnp.broadcast_to(act[None], (TP, ROWS, DB)), "tp", 0, 0, tiled=True
    )
    idx = plan(me, spread_counts(copy_counts))
    partner_keys = swapped(cache_keys)
    partner_values = swapped(cache_values)
    packed = pack(me, idx, [cache_keys, cache_values], [partner_keys, partner_values])
    rows = exchanged(packed)

    packed, gathered = lax.optimization_barrier((packed, gathered))
    qa, kf, vf, fresh = project(
        gathered, norm_gain.reshape(TP, DB), w_query, w_key, value_weight, rotation_table()
    )
    fresh = lax.all_gather(fresh, "dom", axis=0, tiled=True)
    partials = attend(blk, qa, kf, vf, cache_keys, cache_values, w_output)
    parts = [partials[0]] + [shifted(partials[s], s) for s in range(1, TP)]
    reward = jnp.sum(twisting_table[tokens].astype(F32), 0)
    base = jnp.where(tp == 0, previous_log_weights + reward, 0.0)
    base = jnp.pad(base, (0, HD - NP)).reshape(1, HD)
    attn, message = mix(parts, act, twist_vec.reshape(1, DB), base)
    message, rows = lax.optimization_barrier((message, rows))
    got = lax.all_to_all(message, ("dom", "tp"), 0, 0, tiled=True)
    out_logw = finish(me, got.reshape(NDOM, TP, 2, HD))

    def usual(rows, fresh, *_):
        return tuple(place(idx, rows, fresh))

    def crowded(rows, fresh, partner_keys, partner_values, idx):
        even = dom % 2 == 0
        mine = jnp.concatenate([cache_keys, cache_values], 1)
        other = jnp.concatenate([partner_keys, partner_values], 1)
        chip_rows = jnp.concatenate(
            [jnp.where(even, mine, other), jnp.where(even, other, mine)], 0
        )
        chosen = chip_rows[idx[0, 3:64:4]]
        chip = dom // 2

        def turn(step, state):
            passing, more = state
            passing = next_chip(passing)
            return passing, more.at[(chip - step) % NCHIP].set(passing[chip])

        start = (chosen, chosen)
        more = lax.fori_loop(1, NCHIP, turn, start)[1].at[chip].set(chosen[chip])
        return tuple(place(idx, jnp.concatenate([rows, more[:, None]], 1), fresh))

    new_keys, new_values = lax.cond(
        idx[0, 127] > SLOTS * NDOM,
        crowded,
        usual,
        rows,
        fresh,
        partner_keys,
        partner_values,
        idx,
    )
    return (attn.reshape(STEPS, NP, DB), new_keys, new_values, out_logw.reshape(NP))


def solution(mesh):
    return jax.shard_map(
        local,
        mesh=mesh,
        in_specs=(
            P(None, "dom", "tp"),
            P(),
            P(None, "tp"),
            P(None, "tp"),
            P(None, "tp"),
            P("tp", None),
            P("dom", None, "tp"),
            P("dom", None, "tp"),
            P(None, "dom"),
            P(),
            P("tp"),
            P("dom"),
            P("dom"),
        ),
        out_specs=(P(None, "dom", "tp"), P("dom", None, "tp"), P("dom", None, "tp"), P("dom")),
        check_vma=False,
    )
```

```python
import jax
import jax.numpy as jnp
import numpy as np
from jax import lax
from jax.experimental import pallas as pl
from jax.experimental.pallas import tpu as pltpu
from jax.sharding import PartitionSpec as P

D = 4096
HD = 128
STEPS = 4
NP = 16
ROWS = STEPS * NP
SPAN = 128
TP = 8
DB = D // TP
HEADS = DB // HD
GROUP = HEADS * STEPS
NDOM = 32
NCHIP = 16
SLOTS = 3
BF = jnp.bfloat16
F32 = jnp.float32
ANY = pl.ANY
VM = pltpu.VMEM
SM = pltpu.SMEM


def spec(space):
    return pl.BlockSpec(memory_space=space)


def limit(mib):
    return pltpu.CompilerParams(vmem_limit_bytes=mib * 2**20)


def nt(a, b):
    return lax.dot_general(a, b, (((1,), (1,)), ((), ())), preferred_element_type=F32)


def mm(a, b):
    return jnp.dot(a, b, preferred_element_type=F32)


def project_body(acts, gain, wq, wk, wv, table, qa, kf, vf, fresh, *scratch):
    wq_s, wk_s, wv_s, q_s, kf_s, vf_s, sems = scratch
    copies = []
    for s in range(TP):
        part = pl.ds(s * DB, DB)
        copies.append(
            [
                pltpu.make_async_copy(w.at[part, :], w_s.at[s], sems.at[n, s])
                for n, (w, w_s) in enumerate(((wq, wq_s), (wk, wk_s), (wv, wv_s)))
            ]
        )
    for group in copies:
        for c in group:
            c.start()
    square = jnp.zeros((ROWS, 1), F32)
    for s in range(TP):
        x = acts[s].astype(F32)
        square = square + jnp.sum(x * x, -1, keepdims=True)
    inv = lax.rsqrt(square / D + 1e-05)
    q = jnp.zeros((ROWS, DB), F32)
    k = jnp.zeros((ROWS, HD), F32)
    v = jnp.zeros((ROWS, HD), F32)
    for s in range(TP):
        x = acts[s].astype(F32)
        normed = (x * inv * gain[s : s + 1, :]).astype(BF)
        for c in copies[s]:
            c.wait()
        q = q + mm(normed, wq_s[s])
        k = k + mm(normed, wk_s[s])
        v = v + mm(normed, wv_s[s])
    cosine = table[0]
    sine = table[1]

    def turned(u):
        return (u * cosine + pltpu.roll(u, HD // 2, 1) * sine).astype(BF)

    for g in range(HEADS):
        q_s[g] = turned(q[:, g * HD : (g + 1) * HD]).astype(F32)
    k = turned(k)
    v = v.astype(BF)
    kf[...] = k
    vf[...] = v
    kf_s[...] = k.astype(F32)
    vf_s[...] = v.astype(F32)
    for n in range(NP):
        mine = pl.ds(n, STEPS, stride=NP)
        fresh[n] = jnp.concatenate([kf_s[mine, :], vf_s[mine, :]], 0).astype(BF)
        qa[n * GROUP : (n + 1) * GROUP, :] = jnp.concatenate(
            [q_s[g, mine, :] for g in range(HEADS)], 0
        ).astype(BF)


def project(acts, gain, wq, wk, wv, table):
    sd = jax.ShapeDtypeStruct
    return pl.pallas_call(
        project_body,
        in_specs=[spec(VM)] * 2 + [spec(ANY)] * 3 + [spec(VM)],
        out_specs=[spec(VM)] * 4,
        out_shape=[
            sd((NP * GROUP, HD), BF),
            sd((ROWS, HD), BF),
            sd((ROWS, HD), BF),
            sd((NP, 2 * STEPS, HD), BF),
        ],
        scratch_shapes=[
            VM((TP, DB, DB), BF),
            VM((TP, DB, HD), BF),
            VM((TP, DB, HD), BF),
            VM((HEADS, ROWS, HD), F32),
            VM((ROWS, HD), F32),
            VM((ROWS, HD), F32),
            pltpu.SemaphoreType.DMA((3, TP)),
        ],
        compiler_params=limit(55),
        cost_estimate=pl.CostEstimate(
            flops=2 * ROWS * D * 768, bytes_accessed=7 * 2**20, transcendentals=0
        ),
        name="project",
    )(acts, gain, wq, wk, wv, table)


def attend_body(blk, qa, kf, vf, kc, vc, wo, *refs):
    outs = refs[:TP]
    s1_s, ctx_s, wo_s, sems = refs[TP:]
    copies = []
    for s in range(TP):
        there = pl.ds(pl.multiple_of(blk[s] * DB, DB), DB)
        copies.append(pltpu.make_async_copy(wo.at[:, there], wo_s.at[s], sems.at[s]))
    for c in copies:
        c.start()
    for n in range(NP):
        span = slice(n * GROUP, (n + 1) * GROUP)
        s1_s[span, :] = nt(qa[span, :], kc[n])
    scale = 1.0 / HD**0.5
    s1 = s1_s[...] * scale
    s2 = nt(qa[...], kf[...]) * scale
    row = lax.broadcasted_iota(jnp.int32, (NP * GROUP, ROWS), 0)
    col = lax.broadcasted_iota(jnp.int32, (NP * GROUP, ROWS), 1)
    seen = ((row // GROUP) == (col % NP)) & ((col // NP) <= (row % STEPS))
    s2 = jnp.where(seen, s2, -jnp.inf)
    top = jnp.maximum(jnp.max(s1, -1, keepdims=True), jnp.max(s2, -1, keepdims=True))
    e1 = jnp.exp(s1 - top)
    e2 = jnp.exp(s2 - top)
    total = jnp.sum(e1, -1, keepdims=True) + jnp.sum(e2, -1, keepdims=True)
    w1 = (e1 / total).astype(BF)
    w2 = (e2 / total).astype(BF)
    c2 = mm(w2, vf[...])
    for n in range(NP):
        span = slice(n * GROUP, (n + 1) * GROUP)
        cn = (mm(w1[span], vc[n]) + c2[span]).astype(BF).astype(F32)
        for g in range(HEADS):
            ctx_s[g, pl.ds(n, STEPS, stride=NP), :] = cn[g * STEPS : (g + 1) * STEPS]
    ctx = jnp.concatenate([ctx_s[g] for g in range(HEADS)], 1).astype(BF)
    for s in range(TP):
        copies[s].wait()
        outs[s][...] = mm(ctx, wo_s[s]).astype(BF)


def attend(blk, qa, kf, vf, kc, vc, wo):
    return pl.pallas_call(
        attend_body,
        in_specs=[spec(SM)] + [spec(VM)] * 5 + [spec(ANY)],
        out_specs=[spec(VM)] * TP,
        out_shape=[jax.ShapeDtypeStruct((ROWS, DB), BF)] * TP,
        scratch_shapes=[
            VM((NP * GROUP, SPAN), F32),
            VM((HEADS, ROWS, HD), F32),
            VM((TP, DB, DB), BF),
            pltpu.SemaphoreType.DMA((TP,)),
        ],
        compiler_params=limit(55),
        cost_estimate=pl.CostEstimate(
            flops=2 * ROWS * D * 640, bytes_accessed=6 * 2**20, transcendentals=NP * 16 * 192
        ),
        name="attend",
    )(blk, qa, kf, vf, kc, vc, wo)


def mix_body(*refs):
    parts = refs[:TP]
    act, twist, attn, sums = refs[TP:]
    mix = parts[0][...].astype(F32)
    for s in range(1, TP):
        mix = mix + parts[s][...].astype(F32)
    attn[...] = mix.astype(BF)
    summed = act[...].astype(F32) + mix
    aligned = jnp.sum(summed * twist[...], -1, keepdims=True)
    energy = jnp.sum(summed * summed, -1, keepdims=True)
    row = lax.broadcasted_iota(jnp.int32, (ROWS, HD), 0)
    lane = lax.broadcasted_iota(jnp.int32, (ROWS, HD), 1)
    both = jnp.where(lane == row, aligned, 0.0) + jnp.where(lane == row + ROWS, energy, 0.0)
    sums[...] = jnp.broadcast_to(jnp.sum(both, 0, keepdims=True)[None], (TP, 1, HD))


def mix(parts, act, twist):
    sd = jax.ShapeDtypeStruct
    return pl.pallas_call(
        mix_body,
        in_specs=[spec(VM)] * (TP + 2),
        out_specs=[spec(VM)] * 2,
        out_shape=[sd((ROWS, DB), BF), sd((TP, 1, HD), F32)],
        compiler_params=limit(8),
        name="mix",
    )(*parts, act, twist)


def weigh_body(idx, sums, reward, previous, fresh, line, sent):
    total = sums[0]
    for t in range(1, TP):
        total = total + sums[t]
    energy = pltpu.roll(total, ROWS, 1)
    score = total / jnp.sqrt(energy / D + 1e-06) + reward[...]
    gain = score
    for t in range(1, STEPS):
        gain = gain + pltpu.roll(score, HD - NP * t, 1)
    logw = previous[...] + gain
    line[...] = logw
    high = logw.astype(BF).astype(F32)
    middle = (logw - high).astype(BF).astype(F32)
    low = logw - high - middle
    row = lax.broadcasted_iota(jnp.int32, (8, HD), 0)
    parts = jnp.where(row == 0, high, jnp.where(row == 1, middle, jnp.where(row == 2, low, 0.0)))
    parts = parts.astype(BF)
    for d in range(NDOM):
        sent[d, 0] = fresh[idx[1, 2 * d]]
        sent[d, 1] = fresh[idx[1, 2 * d + 1]]
        sent[d, 2] = parts


def weigh(idx, sums, reward, previous, fresh):
    sd = jax.ShapeDtypeStruct
    return pl.pallas_call(
        weigh_body,
        in_specs=[spec(SM)] + [spec(VM)] * 4,
        out_specs=[spec(VM)] * 2,
        out_shape=[sd((1, HD), F32), sd((NDOM, 3, 8, HD), BF)],
        compiler_params=limit(8),
        name="weigh",
    )(idx, sums, reward, previous, fresh)


def finish_body(idx, line, got, keys_in, values_in, logw, keys, values, all_s, f_s, k_s, v_s, sems):
    for k in range(NP):
        code = idx[1, 64 + k]
        f_s[pl.ds(k, 2 * STEPS, stride=NP), :] = got[code // 2, code % 2].astype(F32)
    half = STEPS * NP
    k_s[...] = f_s[0:half, :].reshape(STEPS, NP, HD).astype(BF)
    v_s[...] = f_s[half : 2 * half, :].reshape(STEPS, NP, HD).astype(BF)
    tail = pl.ds(SPAN, STEPS)
    copies = [
        pltpu.make_async_copy(k_s, keys.at[tail], sems.at[0]),
        pltpu.make_async_copy(v_s, values.at[tail], sems.at[1]),
    ]
    for c in copies:
        c.start()
    for d in range(NDOM):
        all_s[d : d + 1, :] = jnp.sum(got[d, 2].astype(F32), 0, keepdims=True)
    lane = lax.broadcasted_iota(jnp.int32, (NDOM, HD), 1)
    all_w = jnp.where(lane < NP, all_s[...], -jnp.inf)
    largest = jnp.max(all_w, keepdims=True)
    mass = jnp.sum(jnp.exp(all_w - largest), keepdims=True)
    logw[...] = (line[...] - (largest + jnp.log(mass)))[:, 0:NP]
    for c in copies:
        c.wait()


def finish(idx, line, got, keys, values):
    sd = jax.ShapeDtypeStruct
    return pl.pallas_call(
        finish_body,
        in_specs=[spec(SM)] + [spec(VM)] * 2 + [spec(ANY)] * 2,
        out_specs=[spec(VM)] + [spec(ANY)] * 2,
        out_shape=[sd((1, NP), F32), sd(keys.shape, BF), sd(values.shape, BF)],
        scratch_shapes=[
            VM((NDOM, HD), F32),
            VM((2 * STEPS * NP, HD), F32),
            VM((STEPS, NP, HD), BF),
            VM((STEPS, NP, HD), BF),
            pltpu.SemaphoreType.DMA((2,)),
        ],
        input_output_aliases={3: 1, 4: 2},
        compiler_params=limit(8),
        name="finish",
    )(idx, line, got, keys, values)


def plan_body(me_ref, counts_ref, out):
    me = me_ref[0]
    counts = counts_ref[:, 0, :].astype(F32)
    r16 = lax.broadcasted_iota(jnp.int32, (NP, NP), 0)
    c16 = lax.broadcasted_iota(jnp.int32, (NP, NP), 1)
    within = mm(counts, (r16 <= c16).astype(F32))
    r32 = lax.broadcasted_iota(jnp.int32, (NDOM, NDOM), 0)
    c32 = lax.broadcasted_iota(jnp.int32, (NDOM, NDOM), 1)
    before = jnp.sum(mm((c32 < r32).astype(F32), counts), -1, keepdims=True)
    ends = (within + before).astype(jnp.int32)
    before = before.astype(jnp.int32)
    device = lax.broadcasted_iota(jnp.int32, (NDOM, 1), 0)
    chip_end = jnp.where(device % 2 == 1, ends[:, NP - 1 : NP], -1)
    chip = me // 2
    first = jnp.sum(jnp.where(device == 2 * chip, before, 0))
    lane = lax.broadcasted_iota(jnp.int32, (1, HD), 1)
    dest = 2 * (lane // 4) + me % 2
    sent = first + ((dest - first) & (NDOM - 1)) + NDOM * (lane % 4)
    kept = NDOM * (lane - 64) + me
    found = jnp.zeros((NDOM, HD), jnp.int32)
    for j in range(NP):
        found = found + (ends[:, j : j + 1] <= sent).astype(jnp.int32)
    particle = jnp.sum(found, 0, keepdims=True) - 2 * NP * chip
    particle = jnp.clip(particle, 0, 2 * NP - 1)
    passed = (chip_end >= 0) & (chip_end <= kept)
    source = jnp.sum(passed.astype(jnp.int32), 0, keepdims=True)
    base = jnp.max(jnp.where(passed, chip_end, 0), 0, keepdims=True)
    slot = jnp.clip((kept - base) // NDOM, 0, 3)
    arrived = 4 * jnp.clip(source, 0, NCHIP - 1) + slot
    owned = jnp.sum(counts, -1, keepdims=True).astype(jnp.int32)
    pair = lax.broadcasted_iota(jnp.int32, (NDOM, HD), 1)
    most = jnp.max(jnp.sum(jnp.where(pair == device // 2, owned, 0), 0, keepdims=True))
    line = jnp.where(lane < 64, particle, jnp.where(lane < 80, arrived, most))

    own = jnp.sum(jnp.where(device == me, before, 0))
    sent = own + ((lane // 2 - own) & (NDOM - 1)) + NDOM * (lane % 2)
    found = jnp.zeros((NDOM, HD), jnp.int32)
    for j in range(NP):
        found = found + (ends[:, j : j + 1] <= sent).astype(jnp.int32)
    particle = jnp.sum(found, 0, keepdims=True) - NP * me
    particle = jnp.clip(particle, 0, NP - 1)
    passed = ends[:, NP - 1 : NP] <= kept
    source = jnp.sum(passed.astype(jnp.int32), 0, keepdims=True)
    base = jnp.max(jnp.where(passed, ends[:, NP - 1 : NP], 0), 0, keepdims=True)
    slot = jnp.clip((kept - base) // NDOM, 0, 1)
    arrived = 2 * jnp.clip(source, 0, NDOM - 1) + slot
    second = jnp.where(lane < 64, particle, arrived)
    row = lax.broadcasted_iota(jnp.int32, (8, HD), 0)
    out[...] = jnp.where(row == 0, line, second)


def plan(me, counts):
    return pl.pallas_call(
        plan_body,
        in_specs=[spec(SM), spec(VM)],
        out_specs=spec(VM),
        out_shape=jax.ShapeDtypeStruct((8, HD), jnp.int32),
        compiler_params=limit(8),
        name="plan",
    )(me, counts)


def pack_body(me_ref, idx, *refs):
    half = (len(refs) - 3) // 2
    own, partner = (refs[:half], refs[half : 2 * half])
    out, rows, sems = refs[2 * half :]
    core = me_ref[0] % 2
    loads, at = ([], 0)
    for n in range(half):
        length = own[n].shape[1]
        for side, ref in ((core, own[n]), (1 - core, partner[n])):
            there = rows.at[pl.ds(side * NP, NP), pl.ds(at, length), :]
            loads.append(pltpu.make_async_copy(ref, there, sems.at[len(loads) + 1]))
        at += length
    for c in loads:
        c.start()
    for c in loads:
        c.wait()
    for q in range(NCHIP):
        for s in range(SLOTS):
            pltpu.make_async_copy(rows.at[idx[0, 4 * q + s]], out.at[q, s], sems.at[0]).start()
    pltpu.make_async_copy(out, out, sems.at[0]).wait()


def pack(me, idx, own, partner):
    length = sum(a.shape[1] for a in own)
    return pl.pallas_call(
        pack_body,
        in_specs=[spec(SM), spec(SM)] + [spec(ANY)] * (2 * len(own)),
        out_specs=spec(ANY),
        out_shape=jax.ShapeDtypeStruct((NCHIP, SLOTS, length, HD), BF),
        scratch_shapes=[
            VM((2 * NP, length, HD), BF),
            pltpu.SemaphoreType.DMA((1 + 2 * len(own),)),
        ],
        compiler_params=limit(16),
        name="pack",
    )(me, idx, *own, *partner)


def place_body(slots, idx, rows, keys, values, sems):
    copies = []
    for k in range(NP):
        code = idx[0, 64 + k]
        slot = jnp.minimum(code % 4, slots - 1)
        for n, out in enumerate((keys, values)):
            part = rows.at[code // 4, slot, pl.ds(n * SPAN, SPAN), :]
            copies.append(pltpu.make_async_copy(part, out.at[k], sems.at[n, k]))
    for c in copies:
        c.start()
    for c in copies:
        c.wait()


def place(idx, rows):
    slots = rows.shape[1]
    return pl.pallas_call(
        lambda *refs: place_body(slots, *refs),
        in_specs=[spec(SM), spec(ANY)],
        out_specs=[spec(VM)] * 2,
        out_shape=[jax.ShapeDtypeStruct((NP, SPAN, HD), BF)] * 2,
        scratch_shapes=[pltpu.SemaphoreType.DMA((2, NP))],
        compiler_params=limit(16),
        name="place",
    )(idx, rows)


def shifted(value, shift):
    return lax.ppermute(value, "tp", [(i, (i + shift) % TP) for i in range(TP)])


def swapped(value):
    return lax.ppermute(value, "dom", [(i, i ^ 1) for i in range(NDOM)])


def next_chip(value):
    return lax.ppermute(value, "dom", [(i, (i + 2) % NDOM) for i in range(NDOM)])


SAME_CORE = [list(range(c, NDOM, 2)) for c in range(2)]


def exchanged(rows):
    return lax.all_to_all(rows, "dom", 0, 0, tiled=True, axis_index_groups=SAME_CORE)


def counts_of_all(counts):
    sent = jnp.broadcast_to(counts[None, None], (NDOM, 1, NP))
    return lax.all_to_all(sent, "dom", 0, 0, tiled=True)


def rotation_table():
    frequency = np.float32(500000.0) ** (-2.0 * np.arange(HD // 2, dtype=np.float32) / HD)
    angles = (SPAN + np.arange(STEPS, dtype=np.float32))[:, None] * frequency.astype(np.float32)
    cosine = np.concatenate([np.cos(angles), np.cos(angles)], 1)
    sine = np.concatenate([-np.sin(angles), np.sin(angles)], 1)
    return np.stack([np.repeat(cosine, NP, 0), np.repeat(sine, NP, 0)]).astype(np.float32)


def local(
    activations,
    norm_gain,
    w_query,
    w_key,
    value_weight,
    w_output,
    cache_keys,
    cache_values,
    tokens,
    twisting_table,
    twist_vec,
    previous_log_weights,
    copy_counts,
):
    dom = lax.axis_index("dom")
    tp = lax.axis_index("tp")
    me = dom.reshape(1)
    blk = ((tp + np.arange(TP)) % TP).astype(jnp.int32)
    act = activations.reshape(ROWS, DB)
    reward = twisting_table[tokens.reshape(ROWS)].astype(F32)
    reward = jnp.pad(reward, (0, HD - ROWS)).reshape(1, HD)
    previous = jnp.pad(previous_log_weights, (0, HD - NP)).reshape(1, HD)
    partner_keys = swapped(cache_keys)
    partner_values = swapped(cache_values)

    counts = counts_of_all(copy_counts)
    sent = jnp.broadcast_to(act[None], (TP, ROWS, DB))
    sent, counts, partner_keys, partner_values, reward, previous = lax.optimization_barrier(
        (sent, counts, partner_keys, partner_values, reward, previous)
    )
    gathered = lax.all_to_all(sent, "tp", 0, 0, tiled=True)
    idx = plan(me, counts)
    packed = pack(me, idx, [cache_keys, cache_values], [partner_keys, partner_values])
    packed, gathered = lax.optimization_barrier((packed, gathered))
    rows = exchanged(packed)

    qa, kf, vf, fresh = project(
        gathered, norm_gain.reshape(TP, DB), w_query, w_key, value_weight, rotation_table()
    )
    partials = attend(blk, qa, kf, vf, cache_keys, cache_values, w_output)
    parts = [partials[0]] + [shifted(partials[s], s) for s in range(1, TP)]
    attn, sums = mix(parts, act, twist_vec.reshape(1, DB))
    sums, rows = lax.optimization_barrier((sums, rows))
    sums = lax.all_to_all(sums, "tp", 0, 0, tiled=True)
    line, sent = weigh(idx, sums, reward, previous, fresh)
    got = lax.all_to_all(sent, "dom", 0, 0, tiled=True)

    def usual(rows, *_):
        return tuple(place(idx, rows))

    def crowded(rows, partner_keys, partner_values, idx):
        even = dom % 2 == 0
        mine = jnp.concatenate([cache_keys, cache_values], 1)
        other = jnp.concatenate([partner_keys, partner_values], 1)
        chip_rows = jnp.concatenate(
            [jnp.where(even, mine, other), jnp.where(even, other, mine)], 0
        )
        chosen = chip_rows[idx[0, 3:64:4]]
        chip = dom // 2

        def turn(step, state):
            passing, more = state
            passing = next_chip(passing)
            return passing, more.at[(chip - step) % NCHIP].set(passing[chip])

        start = (chosen, chosen)
        more = lax.fori_loop(1, NCHIP, turn, start)[1].at[chip].set(chosen[chip])
        return tuple(place(idx, jnp.concatenate([rows, more[:, None]], 1)))

    old_keys, old_values = lax.cond(
        idx[0, 127] > SLOTS * NDOM,
        crowded,
        usual,
        rows,
        partner_keys,
        partner_values,
        idx,
    )

    def by_position(old):
        return jnp.pad(jnp.transpose(old, (1, 0, 2)), ((0, STEPS), (0, 0), (0, 0)))

    out_logw, new_keys, new_values = finish(
        idx, line, got, by_position(old_keys), by_position(old_values)
    )
    return (
        attn.reshape(STEPS, NP, DB),
        jnp.transpose(new_keys, (1, 0, 2)),
        jnp.transpose(new_values, (1, 0, 2)),
        out_logw.reshape(NP),
    )


def solution(mesh):
    return jax.shard_map(
        local,
        mesh=mesh,
        in_specs=(
            P(None, "dom", "tp"),
            P(),
            P(None, "tp"),
            P(None, "tp"),
            P(None, "tp"),
            P("tp", None),
            P("dom", None, "tp"),
            P("dom", None, "tp"),
            P(None, "dom"),
            P(),
            P("tp"),
            P("dom"),
            P("dom"),
        ),
        out_specs=(P(None, "dom", "tp"), P("dom", None, "tp"), P("dom", None, "tp"), P("dom")),
        check_vma=False,
    )
```

```python
import jax
import jax.numpy as jnp
import numpy as np
from jax import lax
from jax.experimental import pallas as pl
from jax.experimental.pallas import tpu as pltpu
from jax.sharding import PartitionSpec as P

D = 4096
HD = 128
STEPS = 4
NP = 16
ROWS = STEPS * NP
SPAN = 128
TP = 8
PAIRS = TP // 2
DB = D // TP
HEADS = DB // HD
GROUP = HEADS * STEPS
NDOM = 32
NCHIP = 16
SLOTS = 3
BF = jnp.bfloat16
F32 = jnp.float32
ANY = pl.ANY
VM = pltpu.VMEM
SM = pltpu.SMEM


def spec(space):
    return pl.BlockSpec(memory_space=space)


def limit(mib):
    return pltpu.CompilerParams(vmem_limit_bytes=mib * 2**20)


def nt(a, b):
    return lax.dot_general(a, b, (((1,), (1,)), ((), ())), preferred_element_type=F32)


def mm(a, b):
    return jnp.dot(a, b, preferred_element_type=F32)


def project_body(acts, gain, wq, wk, wv, table, qa, kf, vf, fresh, *scratch):
    wq_s, wk_s, wv_s, q_s, kf_s, vf_s, sems = scratch
    copies = []
    for s in range(TP):
        part = pl.ds(s * DB, DB)
        copies.append(
            [
                pltpu.make_async_copy(w.at[part, :], w_s.at[s], sems.at[n, s])
                for n, (w, w_s) in enumerate(((wq, wq_s), (wk, wk_s), (wv, wv_s)))
            ]
        )
    for group in copies:
        for c in group:
            c.start()
    square = jnp.zeros((ROWS, 1), F32)
    for s in range(TP):
        x = acts[s].astype(F32)
        square = square + jnp.sum(x * x, -1, keepdims=True)
    inv = lax.rsqrt(square / D + 1e-05)
    q = jnp.zeros((ROWS, DB), F32)
    k = jnp.zeros((ROWS, HD), F32)
    v = jnp.zeros((ROWS, HD), F32)
    for s in range(TP):
        x = acts[s].astype(F32)
        normed = (x * inv * gain[s : s + 1, :]).astype(BF)
        for c in copies[s]:
            c.wait()
        q = q + mm(normed, wq_s[s])
        k = k + mm(normed, wk_s[s])
        v = v + mm(normed, wv_s[s])
    cosine = table[0]
    sine = table[1]

    def turned(u):
        return (u * cosine + pltpu.roll(u, HD // 2, 1) * sine).astype(BF)

    for g in range(HEADS):
        q_s[g] = turned(q[:, g * HD : (g + 1) * HD]).astype(F32)
    k = turned(k)
    v = v.astype(BF)
    kf[...] = k
    vf[...] = v
    kf_s[...] = k.astype(F32)
    vf_s[...] = v.astype(F32)
    for n in range(NP):
        mine = pl.ds(n, STEPS, stride=NP)
        fresh[n] = jnp.concatenate([kf_s[mine, :], vf_s[mine, :]], 0).astype(BF)
        qa[n * GROUP : (n + 1) * GROUP, :] = jnp.concatenate(
            [q_s[g, mine, :] for g in range(HEADS)], 0
        ).astype(BF)


def project(acts, gain, wq, wk, wv, table):
    sd = jax.ShapeDtypeStruct
    return pl.pallas_call(
        project_body,
        in_specs=[spec(VM)] * 2 + [spec(ANY)] * 3 + [spec(VM)],
        out_specs=[spec(VM)] * 4,
        out_shape=[
            sd((NP * GROUP, HD), BF),
            sd((ROWS, HD), BF),
            sd((ROWS, HD), BF),
            sd((NP, 2 * STEPS, HD), BF),
        ],
        scratch_shapes=[
            VM((TP, DB, DB), BF),
            VM((TP, DB, HD), BF),
            VM((TP, DB, HD), BF),
            VM((HEADS, ROWS, HD), F32),
            VM((ROWS, HD), F32),
            VM((ROWS, HD), F32),
            pltpu.SemaphoreType.DMA((3, TP)),
        ],
        compiler_params=limit(55),
        cost_estimate=pl.CostEstimate(
            flops=2 * ROWS * D * 768, bytes_accessed=7 * 2**20, transcendentals=0
        ),
        name="project",
    )(acts, gain, wq, wk, wv, table)


def attend_body(blk, qa, kf, vf, kc, vc, wo, *refs):
    outs = refs[:TP]
    s1_s, ctx_s, wo_s, sems = refs[TP:]
    copies = []
    for s in range(TP):
        there = pl.ds(pl.multiple_of(blk[s] * DB, DB), DB)
        copies.append(pltpu.make_async_copy(wo.at[:, there], wo_s.at[s], sems.at[s]))
    for c in copies:
        c.start()
    for n in range(NP):
        span = slice(n * GROUP, (n + 1) * GROUP)
        s1_s[span, :] = nt(qa[span, :], kc[n])
    scale = 1.0 / HD**0.5
    s1 = s1_s[...] * scale
    s2 = nt(qa[...], kf[...]) * scale
    row = lax.broadcasted_iota(jnp.int32, (NP * GROUP, ROWS), 0)
    col = lax.broadcasted_iota(jnp.int32, (NP * GROUP, ROWS), 1)
    seen = ((row // GROUP) == (col % NP)) & ((col // NP) <= (row % STEPS))
    s2 = jnp.where(seen, s2, -jnp.inf)
    top = jnp.maximum(jnp.max(s1, -1, keepdims=True), jnp.max(s2, -1, keepdims=True))
    e1 = jnp.exp(s1 - top)
    e2 = jnp.exp(s2 - top)
    total = jnp.sum(e1, -1, keepdims=True) + jnp.sum(e2, -1, keepdims=True)
    w1 = (e1 / total).astype(BF)
    w2 = (e2 / total).astype(BF)
    c2 = mm(w2, vf[...])
    for n in range(NP):
        span = slice(n * GROUP, (n + 1) * GROUP)
        cn = (mm(w1[span], vc[n]) + c2[span]).astype(BF).astype(F32)
        for g in range(HEADS):
            ctx_s[g, pl.ds(n, STEPS, stride=NP), :] = cn[g * STEPS : (g + 1) * STEPS]
    ctx = jnp.concatenate([ctx_s[g] for g in range(HEADS)], 1).astype(BF)
    for s in range(TP):
        copies[s].wait()
        outs[s][...] = mm(ctx, wo_s[s]).astype(BF)


def attend(blk, qa, kf, vf, kc, vc, wo):
    return pl.pallas_call(
        attend_body,
        in_specs=[spec(SM)] + [spec(VM)] * 5 + [spec(ANY)],
        out_specs=[spec(VM)] * TP,
        out_shape=[jax.ShapeDtypeStruct((ROWS, DB), BF)] * TP,
        scratch_shapes=[
            VM((NP * GROUP, SPAN), F32),
            VM((HEADS, ROWS, HD), F32),
            VM((TP, DB, DB), BF),
            pltpu.SemaphoreType.DMA((TP,)),
        ],
        compiler_params=limit(50),
        cost_estimate=pl.CostEstimate(
            flops=2 * ROWS * D * 640, bytes_accessed=6 * 2**20, transcendentals=NP * 16 * 192
        ),
        name="attend",
    )(blk, qa, kf, vf, kc, vc, wo)


def mix_body(*refs):
    parts = refs[:TP]
    act, twist, attn, sums = refs[TP:]
    mix = parts[0][...].astype(F32)
    for s in range(1, TP):
        mix = mix + parts[s][...].astype(F32)
    attn[...] = mix.astype(BF)
    summed = act[...].astype(F32) + mix
    aligned = jnp.sum(summed * twist[...], -1, keepdims=True)
    energy = jnp.sum(summed * summed, -1, keepdims=True)
    row = lax.broadcasted_iota(jnp.int32, (ROWS, HD), 0)
    lane = lax.broadcasted_iota(jnp.int32, (ROWS, HD), 1)
    both = jnp.where(lane == row, aligned, 0.0) + jnp.where(lane == row + ROWS, energy, 0.0)
    sums[...] = jnp.sum(both, 0, keepdims=True)


def mix(parts, act, twist):
    sd = jax.ShapeDtypeStruct
    return pl.pallas_call(
        mix_body,
        in_specs=[spec(VM)] * (TP + 2),
        out_specs=[spec(VM)] * 2,
        out_shape=[sd((ROWS, DB), BF), sd((1, HD), F32)],
        compiler_params=limit(8),
        name="mix",
    )(*parts, act, twist)


def weigh_body(*refs):
    parts = refs[:PAIRS]
    reward, previous, out = refs[PAIRS:]
    sums = parts[0][...]
    for s in range(1, PAIRS):
        sums = sums + parts[s][...]
    energy = pltpu.roll(sums, ROWS, 1)
    score = sums / jnp.sqrt(energy / D + 1e-06) + reward[...]
    gain = score
    for t in range(1, STEPS):
        gain = gain + pltpu.roll(score, HD - NP * t, 1)
    out[...] = jnp.broadcast_to((previous[...] + gain)[None], (NDOM, 1, HD))


def weigh(parts, reward, previous):
    return pl.pallas_call(
        weigh_body,
        in_specs=[spec(VM)] * (PAIRS + 2),
        out_specs=spec(VM),
        out_shape=jax.ShapeDtypeStruct((NDOM, 1, HD), F32),
        compiler_params=limit(8),
        name="weigh",
    )(*parts, reward, previous)


def finish_body(mine, every, out):
    lane = lax.broadcasted_iota(jnp.int32, (NDOM, HD), 1)
    all_w = jnp.where(lane < NP, every[:, 0, :], -jnp.inf)
    largest = jnp.max(all_w, keepdims=True)
    mass = jnp.sum(jnp.exp(all_w - largest), keepdims=True)
    out[...] = (mine[0] - (largest + jnp.log(mass)))[:, 0:NP]


def finish(mine, every):
    return pl.pallas_call(
        finish_body,
        in_specs=[spec(VM)] * 2,
        out_specs=spec(VM),
        out_shape=jax.ShapeDtypeStruct((1, NP), F32),
        compiler_params=limit(8),
        name="finish",
    )(mine, every)


def plan_body(me_ref, *refs):
    out = refs[-1]
    me = me_ref[0]
    blocks = jnp.concatenate([r[...] for r in refs[:-1]], 0).astype(F32)
    rel = lax.broadcasted_iota(jnp.int32, (NDOM, NDOM), 1)
    back_y = (me // 8 - rel // 8) & 3
    back_x = (me // 2 - rel // 2) & 3
    holder = 8 * back_y + 2 * back_x + ((me + rel) & 1)
    sorted_rows = lax.broadcasted_iota(jnp.int32, (NDOM, NDOM), 0) == holder
    counts = mm(sorted_rows.astype(F32), blocks)
    r16 = lax.broadcasted_iota(jnp.int32, (NP, NP), 0)
    c16 = lax.broadcasted_iota(jnp.int32, (NP, NP), 1)
    within = mm(counts, (r16 <= c16).astype(F32))
    r32 = lax.broadcasted_iota(jnp.int32, (NDOM, NDOM), 0)
    c32 = lax.broadcasted_iota(jnp.int32, (NDOM, NDOM), 1)
    before = jnp.sum(mm((c32 < r32).astype(F32), counts), -1, keepdims=True)
    ends = (within + before).astype(jnp.int32)
    before = before.astype(jnp.int32)
    device = lax.broadcasted_iota(jnp.int32, (NDOM, 1), 0)
    chip_end = jnp.where(device % 2 == 1, ends[:, NP - 1 : NP], -1)
    chip = me // 2
    first = jnp.sum(jnp.where(device == 2 * chip, before, 0))
    lane = lax.broadcasted_iota(jnp.int32, (1, HD), 1)
    dest = 2 * (lane // 4) + me % 2
    sent = first + ((dest - first) & (NDOM - 1)) + NDOM * (lane % 4)
    kept = NDOM * (lane - 64) + me
    found = jnp.zeros((NDOM, HD), jnp.int32)
    for j in range(NP):
        found = found + (ends[:, j : j + 1] <= sent).astype(jnp.int32)
    particle = jnp.sum(found, 0, keepdims=True) - 2 * NP * chip
    particle = jnp.clip(particle, 0, 2 * NP - 1)
    passed = (chip_end >= 0) & (chip_end <= kept)
    source = jnp.sum(passed.astype(jnp.int32), 0, keepdims=True)
    base = jnp.max(jnp.where(passed, chip_end, 0), 0, keepdims=True)
    slot = jnp.clip((kept - base) // NDOM, 0, 3)
    arrived = 4 * jnp.clip(source, 0, NCHIP - 1) + slot
    owned = jnp.sum(counts, -1, keepdims=True).astype(jnp.int32)
    pair = lax.broadcasted_iota(jnp.int32, (NDOM, HD), 1)
    most = jnp.max(jnp.sum(jnp.where(pair == device // 2, owned, 0), 0, keepdims=True))
    line = jnp.where(lane < 64, particle, jnp.where(lane < 80, arrived, most))
    out[...] = jnp.broadcast_to(line, (8, HD))


def plan(me, blocks):
    return pl.pallas_call(
        plan_body,
        in_specs=[spec(SM)] + [spec(VM)] * len(blocks),
        out_specs=spec(VM),
        out_shape=jax.ShapeDtypeStruct((8, HD), jnp.int32),
        compiler_params=limit(8),
        name="plan",
    )(me, *blocks)


def pack_body(me_ref, idx, *refs):
    half = (len(refs) - 3) // 2
    own, partner = (refs[:half], refs[half : 2 * half])
    out, rows, sems = refs[2 * half :]
    core = me_ref[0] % 2
    loads, at = ([], 0)
    for n in range(half):
        length = own[n].shape[1]
        for side, ref in ((core, own[n]), (1 - core, partner[n])):
            there = rows.at[pl.ds(side * NP, NP), pl.ds(at, length), :]
            loads.append(pltpu.make_async_copy(ref, there, sems.at[len(loads) + 1]))
        at += length
    for c in loads:
        c.start()
    for c in loads:
        c.wait()
    for q in range(NCHIP):
        for s in range(SLOTS):
            pltpu.make_async_copy(rows.at[idx[0, 4 * q + s]], out.at[q, s], sems.at[0]).start()
    pltpu.make_async_copy(out, out, sems.at[0]).wait()


def pack(me, idx, own, partner):
    length = sum(a.shape[1] for a in own)
    return pl.pallas_call(
        pack_body,
        in_specs=[spec(SM), spec(SM)] + [spec(ANY)] * (2 * len(own)),
        out_specs=spec(ANY),
        out_shape=jax.ShapeDtypeStruct((NCHIP, SLOTS, length, HD), BF),
        scratch_shapes=[
            VM((2 * NP, length, HD), BF),
            pltpu.SemaphoreType.DMA((1 + 2 * len(own),)),
        ],
        compiler_params=limit(16),
        name="pack",
    )(me, idx, *own, *partner)


def place_body(slots, idx, rows, keys, values, r_s, sems):
    copies = []
    for k in range(NP):
        code = idx[0, 64 + k]
        slot = jnp.minimum(code % 4, slots - 1)
        copies.append(
            pltpu.make_async_copy(rows.at[code // 4, slot], r_s.at[k], sems.at[k])
        )
    for c in copies:
        c.start()
    for k in range(NP):
        copies[k].wait()
        keys[k, 0:SPAN, :] = r_s[k, 0:SPAN, :]
        values[k, 0:SPAN, :] = r_s[k, SPAN : 2 * SPAN, :]
        tail = r_s[k, 2 * SPAN : 2 * SPAN + 2 * STEPS, :].astype(F32)
        keys[k, SPAN : SPAN + STEPS, :] = tail[0:STEPS].astype(BF)
        values[k, SPAN : SPAN + STEPS, :] = tail[STEPS : 2 * STEPS].astype(BF)


def place(idx, rows):
    out = jax.ShapeDtypeStruct((NP, SPAN + STEPS, HD), BF)
    slots = rows.shape[1]
    return pl.pallas_call(
        lambda *refs: place_body(slots, *refs),
        in_specs=[spec(SM), spec(ANY)],
        out_specs=[spec(VM)] * 2,
        out_shape=[out] * 2,
        scratch_shapes=[
            VM((NP, 2 * SPAN + 2 * STEPS, HD), BF),
            pltpu.SemaphoreType.DMA((NP,)),
        ],
        compiler_params=limit(16),
        name="place",
    )(idx, rows)


def shifted(value, shift):
    return lax.ppermute(value, "tp", [(i, (i + shift) % TP) for i in range(TP)])


def z_swapped(value):
    return lax.ppermute(value, "tp", [(i, i ^ 1) for i in range(TP)])


def swapped(value):
    return lax.ppermute(value, "dom", [(i, i ^ 1) for i in range(NDOM)])


def next_chip(value):
    return lax.ppermute(value, "dom", [(i, (i + 2) % NDOM) for i in range(NDOM)])


SAME_CORE = [list(range(c, NDOM, 2)) for c in range(2)]


def exchanged(rows):
    return lax.all_to_all(rows, "dom", 0, 0, tiled=True, axis_index_groups=SAME_CORE)


def moved(value, axis_stride, shift):
    def to(i):
        at = i // axis_stride % 4
        return i + ((at + shift) % 4 - at) * axis_stride

    return lax.ppermute(value, "dom", [(i, to(i)) for i in range(NDOM)])


def spread_counts(copy_counts):
    own = copy_counts.reshape(1, NP)
    chip = jnp.concatenate([own, swapped(own)], 0)
    row = jnp.concatenate([chip] + [moved(chip, 2, s) for s in range(1, 4)], 0)
    return [row] + [moved(row, 8, s) for s in range(1, 4)]


def rotation_table():
    frequency = np.float32(500000.0) ** (-2.0 * np.arange(HD // 2, dtype=np.float32) / HD)
    angles = (SPAN + np.arange(STEPS, dtype=np.float32))[:, None] * frequency.astype(np.float32)
    cosine = np.concatenate([np.cos(angles), np.cos(angles)], 1)
    sine = np.concatenate([-np.sin(angles), np.sin(angles)], 1)
    return np.stack([np.repeat(cosine, NP, 0), np.repeat(sine, NP, 0)]).astype(np.float32)


def local(
    activations,
    norm_gain,
    w_query,
    w_key,
    value_weight,
    w_output,
    cache_keys,
    cache_values,
    tokens,
    twisting_table,
    twist_vec,
    previous_log_weights,
    copy_counts,
):
    dom = lax.axis_index("dom")
    tp = lax.axis_index("tp")
    me = dom.reshape(1)
    blk = ((tp + np.arange(TP)) % TP).astype(jnp.int32)
    act = activations.reshape(ROWS, DB)

    gathered = lax.all_to_all(
        jnp.broadcast_to(act[None], (TP, ROWS, DB)), "tp", 0, 0, tiled=True
    )
    idx = plan(me, spread_counts(copy_counts))
    partner_keys = swapped(cache_keys)
    partner_values = swapped(cache_values)
    gathered, idx, partner_keys, partner_values = lax.optimization_barrier(
        (gathered, idx, partner_keys, partner_values)
    )
    qa, kf, vf, fresh = project(
        gathered, norm_gain.reshape(TP, DB), w_query, w_key, value_weight, rotation_table()
    )
    partner_fresh = swapped(fresh)
    packed = pack(
        me,
        idx,
        [cache_keys, cache_values, fresh],
        [partner_keys, partner_values, partner_fresh],
    )
    packed, qa = lax.optimization_barrier((packed, qa))
    rows = exchanged(packed)
    partials = attend(blk, qa, kf, vf, cache_keys, cache_values, w_output)

    tokens, *partials = lax.optimization_barrier((tokens, *partials))
    reward = twisting_table[tokens.reshape(ROWS)].astype(F32)
    reward = jnp.pad(reward, (0, HD - ROWS)).reshape(1, HD)
    previous = jnp.pad(previous_log_weights, (0, HD - NP)).reshape(1, HD)
    parts = [partials[0]] + [shifted(partials[s], s) for s in range(1, TP)]
    attn, sums = mix(parts, act, twist_vec.reshape(1, DB))
    sums = sums + z_swapped(sums)
    all_sums = [sums] + [shifted(sums, 2 * s) for s in range(1, PAIRS)]
    logw = weigh(all_sums, reward, previous)
    logw, rows = lax.optimization_barrier((logw, rows))
    every = lax.all_to_all(logw, "dom", 0, 0, tiled=True)
    out_logw = finish(logw, every).reshape(NP)

    def usual(rows, *_):
        return tuple(place(idx, rows))

    def crowded(rows, partner_keys, partner_values, partner_fresh, fresh, idx):
        even = dom % 2 == 0
        mine = jnp.concatenate([cache_keys, cache_values, fresh], 1)
        other = jnp.concatenate([partner_keys, partner_values, partner_fresh], 1)
        chip_rows = jnp.concatenate(
            [jnp.where(even, mine, other), jnp.where(even, other, mine)], 0
        )
        chosen = chip_rows[idx[0, 3:64:4]]
        chip = dom // 2

        def turn(step, state):
            passing, more = state
            passing = next_chip(passing)
            return passing, more.at[(chip - step) % NCHIP].set(passing[chip])

        start = (chosen, chosen)
        more = lax.fori_loop(1, NCHIP, turn, start)[1].at[chip].set(chosen[chip])
        return tuple(place(idx, jnp.concatenate([rows, more[:, None]], 1)))

    new_keys, new_values = lax.cond(
        idx[0, 127] > SLOTS * NDOM,
        crowded,
        usual,
        rows,
        partner_keys,
        partner_values,
        partner_fresh,
        fresh,
        idx,
    )
    return (attn.reshape(STEPS, NP, DB), new_keys, new_values, out_logw)


def solution(mesh):
    return jax.shard_map(
        local,
        mesh=mesh,
        in_specs=(
            P(None, "dom", "tp"),
            P(),
            P(None, "tp"),
            P(None, "tp"),
            P(None, "tp"),
            P("tp", None),
            P("dom", None, "tp"),
            P("dom", None, "tp"),
            P(None, "dom"),
            P(),
            P("tp"),
            P("dom"),
            P("dom"),
        ),
        out_specs=(P(None, "dom", "tp"), P("dom", None, "tp"), P("dom", None, "tp"), P("dom")),
        check_vma=False,
    )
```

```python
import jax
import jax.numpy as jnp
import numpy as np
from jax import lax
from jax.experimental import pallas as pl
from jax.experimental.pallas import tpu as pltpu
from jax.sharding import PartitionSpec as P

D = 4096
HD = 128
STEPS = 4
NP = 16
ROWS = STEPS * NP
SPAN = 128
TP = 8
PAIRS = TP // 2
DB = D // TP
HEADS = DB // HD
GROUP = HEADS * STEPS
NDOM = 32
NCHIP = 16
SLOTS = 3
BF = jnp.bfloat16
F32 = jnp.float32
ANY = pl.ANY
VM = pltpu.VMEM
SM = pltpu.SMEM


def spec(space):
    return pl.BlockSpec(memory_space=space)


def limit(mib):
    return pltpu.CompilerParams(vmem_limit_bytes=mib * 2**20)


def nt(a, b):
    return lax.dot_general(a, b, (((1,), (1,)), ((), ())), preferred_element_type=F32)


def mm(a, b):
    return jnp.dot(a, b, preferred_element_type=F32)


def project_body(acts, gain, wq, wk, wv, table, qa, kf, vf, fresh, *scratch):
    wq_s, wk_s, wv_s, q_s, kf_s, vf_s, sems = scratch
    copies = []
    for s in range(TP):
        part = pl.ds(s * DB, DB)
        copies.append(
            [
                pltpu.make_async_copy(w.at[part, :], w_s.at[s], sems.at[n, s])
                for n, (w, w_s) in enumerate(((wq, wq_s), (wk, wk_s), (wv, wv_s)))
            ]
        )
    for group in copies:
        for c in group:
            c.start()
    square = jnp.zeros((ROWS, 1), F32)
    for s in range(TP):
        x = acts[s].astype(F32)
        square = square + jnp.sum(x * x, -1, keepdims=True)
    inv = lax.rsqrt(square / D + 1e-05)
    q = jnp.zeros((ROWS, DB), F32)
    k = jnp.zeros((ROWS, HD), F32)
    v = jnp.zeros((ROWS, HD), F32)
    for s in range(TP):
        x = acts[s].astype(F32)
        normed = (x * inv * gain[s : s + 1, :]).astype(BF)
        for c in copies[s]:
            c.wait()
        q = q + mm(normed, wq_s[s])
        k = k + mm(normed, wk_s[s])
        v = v + mm(normed, wv_s[s])
    cosine = table[0]
    sine = table[1]

    def turned(u):
        return (u * cosine + pltpu.roll(u, HD // 2, 1) * sine).astype(BF)

    for g in range(HEADS):
        q_s[g] = turned(q[:, g * HD : (g + 1) * HD]).astype(F32)
    k = turned(k)
    v = v.astype(BF)
    kf[...] = k
    vf[...] = v
    kf_s[...] = k.astype(F32)
    vf_s[...] = v.astype(F32)
    for n in range(NP):
        mine = pl.ds(n, STEPS, stride=NP)
        fresh[n] = jnp.concatenate([kf_s[mine, :], vf_s[mine, :]], 0).astype(BF)
        qa[n * GROUP : (n + 1) * GROUP, :] = jnp.concatenate(
            [q_s[g, mine, :] for g in range(HEADS)], 0
        ).astype(BF)


def project(acts, gain, wq, wk, wv, table):
    sd = jax.ShapeDtypeStruct
    return pl.pallas_call(
        project_body,
        in_specs=[spec(VM)] * 2 + [spec(ANY)] * 3 + [spec(VM)],
        out_specs=[spec(VM)] * 4,
        out_shape=[
            sd((NP * GROUP, HD), BF),
            sd((ROWS, HD), BF),
            sd((ROWS, HD), BF),
            sd((NP, 2 * STEPS, HD), BF),
        ],
        scratch_shapes=[
            VM((TP, DB, DB), BF),
            VM((TP, DB, HD), BF),
            VM((TP, DB, HD), BF),
            VM((HEADS, ROWS, HD), F32),
            VM((ROWS, HD), F32),
            VM((ROWS, HD), F32),
            pltpu.SemaphoreType.DMA((3, TP)),
        ],
        compiler_params=limit(53),
        cost_estimate=pl.CostEstimate(
            flops=2 * ROWS * D * 768, bytes_accessed=7 * 2**20, transcendentals=0
        ),
        name="project",
    )(acts, gain, wq, wk, wv, table)


def attend_body(blk, qa, kf, vf, kc, vc, wo, *refs):
    outs = refs[:TP]
    s1_s, ctx_s, wo_s, sems = refs[TP:]
    copies = []
    for s in range(TP):
        there = pl.ds(pl.multiple_of(blk[s] * DB, DB), DB)
        copies.append(pltpu.make_async_copy(wo.at[:, there], wo_s.at[s], sems.at[s]))
    for c in copies:
        c.start()
    for n in range(NP):
        span = slice(n * GROUP, (n + 1) * GROUP)
        s1_s[span, :] = nt(qa[span, :], kc[n])
    scale = 1.0 / HD**0.5
    s1 = s1_s[...] * scale
    s2 = nt(qa[...], kf[...]) * scale
    row = lax.broadcasted_iota(jnp.int32, (NP * GROUP, ROWS), 0)
    col = lax.broadcasted_iota(jnp.int32, (NP * GROUP, ROWS), 1)
    seen = ((row // GROUP) == (col % NP)) & ((col // NP) <= (row % STEPS))
    s2 = jnp.where(seen, s2, -jnp.inf)
    top = jnp.maximum(jnp.max(s1, -1, keepdims=True), jnp.max(s2, -1, keepdims=True))
    e1 = jnp.exp(s1 - top)
    e2 = jnp.exp(s2 - top)
    total = jnp.sum(e1, -1, keepdims=True) + jnp.sum(e2, -1, keepdims=True)
    w1 = (e1 / total).astype(BF)
    w2 = (e2 / total).astype(BF)
    c2 = mm(w2, vf[...])
    for n in range(NP):
        span = slice(n * GROUP, (n + 1) * GROUP)
        cn = (mm(w1[span], vc[n]) + c2[span]).astype(BF).astype(F32)
        for g in range(HEADS):
            ctx_s[g, pl.ds(n, STEPS, stride=NP), :] = cn[g * STEPS : (g + 1) * STEPS]
    ctx = jnp.concatenate([ctx_s[g] for g in range(HEADS)], 1).astype(BF)
    for s in range(TP):
        copies[s].wait()
        outs[s][...] = mm(ctx, wo_s[s]).astype(BF)


def attend(blk, qa, kf, vf, kc, vc, wo):
    return pl.pallas_call(
        attend_body,
        in_specs=[spec(SM)] + [spec(VM)] * 5 + [spec(ANY)],
        out_specs=[spec(VM)] * TP,
        out_shape=[jax.ShapeDtypeStruct((ROWS, DB), BF)] * TP,
        scratch_shapes=[
            VM((NP * GROUP, SPAN), F32),
            VM((HEADS, ROWS, HD), F32),
            VM((TP, DB, DB), BF),
            pltpu.SemaphoreType.DMA((TP,)),
        ],
        compiler_params=limit(53),
        cost_estimate=pl.CostEstimate(
            flops=2 * ROWS * D * 640, bytes_accessed=6 * 2**20, transcendentals=NP * 16 * 192
        ),
        name="attend",
    )(blk, qa, kf, vf, kc, vc, wo)


def mix_body(*refs):
    parts = refs[:TP]
    act, twist, attn, sums = refs[TP:]
    mix = parts[0][...].astype(F32)
    for s in range(1, TP):
        mix = mix + parts[s][...].astype(F32)
    attn[...] = mix.astype(BF)
    summed = act[...].astype(F32) + mix
    aligned = jnp.sum(summed * twist[...], -1, keepdims=True)
    energy = jnp.sum(summed * summed, -1, keepdims=True)
    row = lax.broadcasted_iota(jnp.int32, (ROWS, HD), 0)
    lane = lax.broadcasted_iota(jnp.int32, (ROWS, HD), 1)
    both = jnp.where(lane == row, aligned, 0.0) + jnp.where(lane == row + ROWS, energy, 0.0)
    sums[...] = jnp.sum(both, 0, keepdims=True)


def mix(parts, act, twist):
    sd = jax.ShapeDtypeStruct
    return pl.pallas_call(
        mix_body,
        in_specs=[spec(VM)] * (TP + 2),
        out_specs=[spec(VM)] * 2,
        out_shape=[sd((ROWS, DB), BF), sd((1, HD), F32)],
        compiler_params=limit(8),
        name="mix",
    )(*parts, act, twist)


def weigh_body(idx, *refs):
    parts = refs[:PAIRS]
    reward, previous, fresh, line, sent = refs[PAIRS:]
    total = parts[0][...]
    for s in range(1, PAIRS):
        total = total + parts[s][...]
    energy = pltpu.roll(total, ROWS, 1)
    score = total / jnp.sqrt(energy / D + 1e-06) + reward[...]
    gain = score
    for t in range(1, STEPS):
        gain = gain + pltpu.roll(score, HD - NP * t, 1)
    logw = previous[...] + gain
    line[...] = logw
    high = logw.astype(BF).astype(F32)
    middle = (logw - high).astype(BF).astype(F32)
    low = logw - high - middle
    row = lax.broadcasted_iota(jnp.int32, (8, HD), 0)
    parts = jnp.where(row == 0, high, jnp.where(row == 1, middle, jnp.where(row == 2, low, 0.0)))
    parts = parts.astype(BF)
    for d in range(NDOM):
        sent[d, 0] = fresh[idx[1, 2 * d]]
        sent[d, 1] = fresh[idx[1, 2 * d + 1]]
        sent[d, 2] = parts


def weigh(idx, parts, reward, previous, fresh):
    sd = jax.ShapeDtypeStruct
    return pl.pallas_call(
        weigh_body,
        in_specs=[spec(SM)] + [spec(VM)] * (PAIRS + 3),
        out_specs=[spec(VM)] * 2,
        out_shape=[sd((1, HD), F32), sd((NDOM, 3, 8, HD), BF)],
        compiler_params=limit(8),
        name="weigh",
    )(idx, *parts, reward, previous, fresh)


def finish_body(idx, line, got, keys_in, values_in, logw, keys, values, all_s, f_s, k_s, v_s, sems):
    for k in range(NP):
        code = idx[1, 64 + k]
        f_s[pl.ds(k, 2 * STEPS, stride=NP), :] = got[code // 2, code % 2].astype(F32)
    half = STEPS * NP
    k_s[...] = f_s[0:half, :].reshape(STEPS, NP, HD).astype(BF)
    v_s[...] = f_s[half : 2 * half, :].reshape(STEPS, NP, HD).astype(BF)
    tail = pl.ds(SPAN, STEPS)
    copies = [
        pltpu.make_async_copy(k_s, keys.at[tail], sems.at[0]),
        pltpu.make_async_copy(v_s, values.at[tail], sems.at[1]),
    ]
    for c in copies:
        c.start()
    for d in range(NDOM):
        all_s[d : d + 1, :] = jnp.sum(got[d, 2].astype(F32), 0, keepdims=True)
    lane = lax.broadcasted_iota(jnp.int32, (NDOM, HD), 1)
    all_w = jnp.where(lane < NP, all_s[...], -jnp.inf)
    largest = jnp.max(all_w, keepdims=True)
    mass = jnp.sum(jnp.exp(all_w - largest), keepdims=True)
    logw[...] = (line[...] - (largest + jnp.log(mass)))[:, 0:NP]
    for c in copies:
        c.wait()


def finish(idx, line, got, keys, values):
    sd = jax.ShapeDtypeStruct
    return pl.pallas_call(
        finish_body,
        in_specs=[spec(SM)] + [spec(VM)] * 2 + [spec(ANY)] * 2,
        out_specs=[spec(VM)] + [spec(ANY)] * 2,
        out_shape=[sd((1, NP), F32), sd(keys.shape, BF), sd(values.shape, BF)],
        scratch_shapes=[
            VM((NDOM, HD), F32),
            VM((2 * STEPS * NP, HD), F32),
            VM((STEPS, NP, HD), BF),
            VM((STEPS, NP, HD), BF),
            pltpu.SemaphoreType.DMA((2,)),
        ],
        input_output_aliases={3: 1, 4: 2},
        compiler_params=limit(8),
        name="finish",
    )(idx, line, got, keys, values)


def plan_body(me_ref, *refs):
    out = refs[-1]
    me = me_ref[0]
    blocks = jnp.concatenate([r[...] for r in refs[:-1]], 0).astype(F32)
    rel = lax.broadcasted_iota(jnp.int32, (NDOM, NDOM), 1)
    back_y = (me // 8 - rel // 8) & 3
    back_x = (me // 2 - rel // 2) & 3
    holder = 8 * back_y + 2 * back_x + ((me + rel) & 1)
    sorted_rows = lax.broadcasted_iota(jnp.int32, (NDOM, NDOM), 0) == holder
    counts = mm(sorted_rows.astype(F32), blocks)
    r16 = lax.broadcasted_iota(jnp.int32, (NP, NP), 0)
    c16 = lax.broadcasted_iota(jnp.int32, (NP, NP), 1)
    within = mm(counts, (r16 <= c16).astype(F32))
    r32 = lax.broadcasted_iota(jnp.int32, (NDOM, NDOM), 0)
    c32 = lax.broadcasted_iota(jnp.int32, (NDOM, NDOM), 1)
    before = jnp.sum(mm((c32 < r32).astype(F32), counts), -1, keepdims=True)
    ends = (within + before).astype(jnp.int32)
    before = before.astype(jnp.int32)
    device = lax.broadcasted_iota(jnp.int32, (NDOM, 1), 0)
    chip_end = jnp.where(device % 2 == 1, ends[:, NP - 1 : NP], -1)
    chip = me // 2
    first = jnp.sum(jnp.where(device == 2 * chip, before, 0))
    lane = lax.broadcasted_iota(jnp.int32, (1, HD), 1)
    dest = 2 * (lane // 4) + me % 2
    sent = first + ((dest - first) & (NDOM - 1)) + NDOM * (lane % 4)
    kept = NDOM * (lane - 64) + me
    found = jnp.zeros((NDOM, HD), jnp.int32)
    for j in range(NP):
        found = found + (ends[:, j : j + 1] <= sent).astype(jnp.int32)
    particle = jnp.sum(found, 0, keepdims=True) - 2 * NP * chip
    particle = jnp.clip(particle, 0, 2 * NP - 1)
    passed = (chip_end >= 0) & (chip_end <= kept)
    source = jnp.sum(passed.astype(jnp.int32), 0, keepdims=True)
    base = jnp.max(jnp.where(passed, chip_end, 0), 0, keepdims=True)
    slot = jnp.clip((kept - base) // NDOM, 0, 3)
    arrived = 4 * jnp.clip(source, 0, NCHIP - 1) + slot
    owned = jnp.sum(counts, -1, keepdims=True).astype(jnp.int32)
    pair = lax.broadcasted_iota(jnp.int32, (NDOM, HD), 1)
    most = jnp.max(jnp.sum(jnp.where(pair == device // 2, owned, 0), 0, keepdims=True))
    line = jnp.where(lane < 64, particle, jnp.where(lane < 80, arrived, most))

    own = jnp.sum(jnp.where(device == me, before, 0))
    sent = own + ((lane // 2 - own) & (NDOM - 1)) + NDOM * (lane % 2)
    found = jnp.zeros((NDOM, HD), jnp.int32)
    for j in range(NP):
        found = found + (ends[:, j : j + 1] <= sent).astype(jnp.int32)
    particle = jnp.sum(found, 0, keepdims=True) - NP * me
    particle = jnp.clip(particle, 0, NP - 1)
    passed = ends[:, NP - 1 : NP] <= kept
    source = jnp.sum(passed.astype(jnp.int32), 0, keepdims=True)
    base = jnp.max(jnp.where(passed, ends[:, NP - 1 : NP], 0), 0, keepdims=True)
    slot = jnp.clip((kept - base) // NDOM, 0, 1)
    arrived = 2 * jnp.clip(source, 0, NDOM - 1) + slot
    second = jnp.where(lane < 64, particle, arrived)
    row = lax.broadcasted_iota(jnp.int32, (8, HD), 0)
    out[...] = jnp.where(row == 0, line, second)


def plan(me, blocks):
    return pl.pallas_call(
        plan_body,
        in_specs=[spec(SM)] + [spec(VM)] * len(blocks),
        out_specs=spec(VM),
        out_shape=jax.ShapeDtypeStruct((8, HD), jnp.int32),
        compiler_params=limit(8),
        name="plan",
    )(me, *blocks)


def pack_body(me_ref, idx, *refs):
    half = (len(refs) - 3) // 2
    own, partner = (refs[:half], refs[half : 2 * half])
    out, rows, sems = refs[2 * half :]
    core = me_ref[0] % 2
    loads, at = ([], 0)
    for n in range(half):
        length = own[n].shape[1]
        for side, ref in ((core, own[n]), (1 - core, partner[n])):
            there = rows.at[pl.ds(side * NP, NP), pl.ds(at, length), :]
            loads.append(pltpu.make_async_copy(ref, there, sems.at[len(loads) + 1]))
        at += length
    for c in loads:
        c.start()
    for c in loads:
        c.wait()
    for q in range(NCHIP):
        for s in range(SLOTS):
            pltpu.make_async_copy(rows.at[idx[0, 4 * q + s]], out.at[q, s], sems.at[0]).start()
    pltpu.make_async_copy(out, out, sems.at[0]).wait()


def pack(me, idx, own, partner):
    length = sum(a.shape[1] for a in own)
    return pl.pallas_call(
        pack_body,
        in_specs=[spec(SM), spec(SM)] + [spec(ANY)] * (2 * len(own)),
        out_specs=spec(ANY),
        out_shape=jax.ShapeDtypeStruct((NCHIP, SLOTS, length, HD), BF),
        scratch_shapes=[
            VM((2 * NP, length, HD), BF),
            pltpu.SemaphoreType.DMA((1 + 2 * len(own),)),
        ],
        compiler_params=limit(16),
        name="pack",
    )(me, idx, *own, *partner)


def place_body(slots, idx, rows, keys, values, sems):
    copies = []
    for k in range(NP):
        code = idx[0, 64 + k]
        slot = jnp.minimum(code % 4, slots - 1)
        for n, out in enumerate((keys, values)):
            part = rows.at[code // 4, slot, pl.ds(n * SPAN, SPAN), :]
            copies.append(pltpu.make_async_copy(part, out.at[k], sems.at[n, k]))
    for c in copies:
        c.start()
    for c in copies:
        c.wait()


def place(idx, rows):
    slots = rows.shape[1]
    return pl.pallas_call(
        lambda *refs: place_body(slots, *refs),
        in_specs=[spec(SM), spec(ANY)],
        out_specs=[spec(VM)] * 2,
        out_shape=[jax.ShapeDtypeStruct((NP, SPAN, HD), BF)] * 2,
        scratch_shapes=[pltpu.SemaphoreType.DMA((2, NP))],
        compiler_params=limit(16),
        name="place",
    )(idx, rows)


def shifted(value, shift):
    return lax.ppermute(value, "tp", [(i, (i + shift) % TP) for i in range(TP)])


def z_swapped(value):
    return lax.ppermute(value, "tp", [(i, i ^ 1) for i in range(TP)])


def swapped(value):
    return lax.ppermute(value, "dom", [(i, i ^ 1) for i in range(NDOM)])


def next_chip(value):
    return lax.ppermute(value, "dom", [(i, (i + 2) % NDOM) for i in range(NDOM)])


SAME_CORE = [list(range(c, NDOM, 2)) for c in range(2)]


def exchanged(rows):
    return lax.all_to_all(rows, "dom", 0, 0, tiled=True, axis_index_groups=SAME_CORE)


def moved(value, axis_stride, shift):
    def to(i):
        at = i // axis_stride % 4
        return i + ((at + shift) % 4 - at) * axis_stride

    return lax.ppermute(value, "dom", [(i, to(i)) for i in range(NDOM)])


def spread_counts(copy_counts):
    own = copy_counts.reshape(1, NP)
    chip = jnp.concatenate([own, swapped(own)], 0)
    row = jnp.concatenate([chip] + [moved(chip, 2, s) for s in range(1, 4)], 0)
    return [row] + [moved(row, 8, s) for s in range(1, 4)]


def rotation_table():
    frequency = np.float32(500000.0) ** (-2.0 * np.arange(HD // 2, dtype=np.float32) / HD)
    angles = (SPAN + np.arange(STEPS, dtype=np.float32))[:, None] * frequency.astype(np.float32)
    cosine = np.concatenate([np.cos(angles), np.cos(angles)], 1)
    sine = np.concatenate([-np.sin(angles), np.sin(angles)], 1)
    return np.stack([np.repeat(cosine, NP, 0), np.repeat(sine, NP, 0)]).astype(np.float32)


def local(
    activations,
    norm_gain,
    w_query,
    w_key,
    value_weight,
    w_output,
    cache_keys,
    cache_values,
    tokens,
    twisting_table,
    twist_vec,
    previous_log_weights,
    copy_counts,
):
    dom = lax.axis_index("dom")
    tp = lax.axis_index("tp")
    me = dom.reshape(1)
    blk = ((tp + np.arange(TP)) % TP).astype(jnp.int32)
    act = activations.reshape(ROWS, DB)

    gathered = lax.all_to_all(
        jnp.broadcast_to(act[None], (TP, ROWS, DB)), "tp", 0, 0, tiled=True
    )
    idx = plan(me, spread_counts(copy_counts))
    partner_keys = swapped(cache_keys)
    partner_values = swapped(cache_values)
    packed = pack(me, idx, [cache_keys, cache_values], [partner_keys, partner_values])
    rows = exchanged(packed)

    packed, gathered = lax.optimization_barrier((packed, gathered))
    qa, kf, vf, fresh = project(
        gathered, norm_gain.reshape(TP, DB), w_query, w_key, value_weight, rotation_table()
    )
    partials = attend(blk, qa, kf, vf, cache_keys, cache_values, w_output)
    tokens, *partials = lax.optimization_barrier((tokens, *partials))
    reward = twisting_table[tokens.reshape(ROWS)].astype(F32)
    reward = jnp.pad(reward, (0, HD - ROWS)).reshape(1, HD)
    previous = jnp.pad(previous_log_weights, (0, HD - NP)).reshape(1, HD)
    parts = [partials[0]] + [shifted(partials[s], s) for s in range(1, TP)]
    attn, sums = mix(parts, act, twist_vec.reshape(1, DB))
    sums = sums + z_swapped(sums)
    all_sums = [sums] + [shifted(sums, 2 * s) for s in range(1, PAIRS)]
    line, sent = weigh(idx, all_sums, reward, previous, fresh)
    sent, rows = lax.optimization_barrier((sent, rows))
    got = lax.all_to_all(sent, "dom", 0, 0, tiled=True)

    def usual(rows, *_):
        return tuple(place(idx, rows))

    def crowded(rows, partner_keys, partner_values, idx):
        even = dom % 2 == 0
        mine = jnp.concatenate([cache_keys, cache_values], 1)
        other = jnp.concatenate([partner_keys, partner_values], 1)
        chip_rows = jnp.concatenate(
            [jnp.where(even, mine, other), jnp.where(even, other, mine)], 0
        )
        chosen = chip_rows[idx[0, 3:64:4]]
        chip = dom // 2

        def turn(step, state):
            passing, more = state
            passing = next_chip(passing)
            return passing, more.at[(chip - step) % NCHIP].set(passing[chip])

        start = (chosen, chosen)
        more = lax.fori_loop(1, NCHIP, turn, start)[1].at[chip].set(chosen[chip])
        return tuple(place(idx, jnp.concatenate([rows, more[:, None]], 1)))

    old_keys, old_values = lax.cond(
        idx[0, 127] > SLOTS * NDOM,
        crowded,
        usual,
        rows,
        partner_keys,
        partner_values,
        idx,
    )

    def by_position(old):
        return jnp.pad(jnp.transpose(old, (1, 0, 2)), ((0, STEPS), (0, 0), (0, 0)))

    out_logw, new_keys, new_values = finish(
        idx, line, got, by_position(old_keys), by_position(old_values)
    )
    return (
        attn.reshape(STEPS, NP, DB),
        jnp.transpose(new_keys, (1, 0, 2)),
        jnp.transpose(new_values, (1, 0, 2)),
        out_logw.reshape(NP),
    )


def solution(mesh):
    return jax.shard_map(
        local,
        mesh=mesh,
        in_specs=(
            P(None, "dom", "tp"),
            P(),
            P(None, "tp"),
            P(None, "tp"),
            P(None, "tp"),
            P("tp", None),
            P("dom", None, "tp"),
            P("dom", None, "tp"),
            P(None, "dom"),
            P(),
            P("tp"),
            P("dom"),
            P("dom"),
        ),
        out_specs=(P(None, "dom", "tp"), P("dom", None, "tp"), P("dom", None, "tp"), P("dom")),
        check_vma=False,
    )
```

```python
import jax
import jax.numpy as jnp
import numpy as np
from jax import lax
from jax.experimental import pallas as pl
from jax.experimental.pallas import tpu as pltpu
from jax.sharding import PartitionSpec as P

D = 4096
HD = 128
STEPS = 4
NP = 16
ROWS = STEPS * NP
SPAN = 128
TP = 8
PAIRS = TP // 2
DB = D // TP
HEADS = DB // HD
GROUP = HEADS * STEPS
NDOM = 32
NCHIP = 16
SLOTS = 3
BF = jnp.bfloat16
F32 = jnp.float32
ANY = pl.ANY
VM = pltpu.VMEM
SM = pltpu.SMEM


def spec(space):
    return pl.BlockSpec(memory_space=space)


def limit(mib):
    return pltpu.CompilerParams(vmem_limit_bytes=mib * 2**20)


def nt(a, b):
    return lax.dot_general(a, b, (((1,), (1,)), ((), ())), preferred_element_type=F32)


def mm(a, b):
    return jnp.dot(a, b, preferred_element_type=F32)


def project_body(acts, gain, wq, wk, wv, table, qa, kf, vf, fresh, *scratch):
    wq_s, wk_s, wv_s, q_s, kf_s, vf_s, sems = scratch
    copies = []
    for s in range(TP):
        part = pl.ds(s * DB, DB)
        copies.append(
            [
                pltpu.make_async_copy(w.at[part, :], w_s.at[s], sems.at[n, s])
                for n, (w, w_s) in enumerate(((wq, wq_s), (wk, wk_s), (wv, wv_s)))
            ]
        )
    for group in copies:
        for c in group:
            c.start()
    square = jnp.zeros((ROWS, 1), F32)
    for s in range(TP):
        x = acts[s].astype(F32)
        square = square + jnp.sum(x * x, -1, keepdims=True)
    inv = lax.rsqrt(square / D + 1e-05)
    q = jnp.zeros((ROWS, DB), F32)
    k = jnp.zeros((ROWS, HD), F32)
    v = jnp.zeros((ROWS, HD), F32)
    for s in range(TP):
        x = acts[s].astype(F32)
        normed = (x * inv * gain[s : s + 1, :]).astype(BF)
        for c in copies[s]:
            c.wait()
        q = q + mm(normed, wq_s[s])
        k = k + mm(normed, wk_s[s])
        v = v + mm(normed, wv_s[s])
    cosine = table[0]
    sine = table[1]

    def turned(u):
        return (u * cosine + pltpu.roll(u, HD // 2, 1) * sine).astype(BF)

    for g in range(HEADS):
        q_s[g] = turned(q[:, g * HD : (g + 1) * HD]).astype(F32)
    k = turned(k)
    v = v.astype(BF)
    kf[...] = k
    vf[...] = v
    kf_s[...] = k.astype(F32)
    vf_s[...] = v.astype(F32)
    for n in range(NP):
        mine = pl.ds(n, STEPS, stride=NP)
        fresh[n] = jnp.concatenate([kf_s[mine, :], vf_s[mine, :]], 0).astype(BF)
        qa[n * GROUP : (n + 1) * GROUP, :] = jnp.concatenate(
            [q_s[g, mine, :] for g in range(HEADS)], 0
        ).astype(BF)


def project(acts, gain, wq, wk, wv, table):
    sd = jax.ShapeDtypeStruct
    return pl.pallas_call(
        project_body,
        in_specs=[spec(VM)] * 2 + [spec(ANY)] * 3 + [spec(VM)],
        out_specs=[spec(VM)] * 4,
        out_shape=[
            sd((NP * GROUP, HD), BF),
            sd((ROWS, HD), BF),
            sd((ROWS, HD), BF),
            sd((NP, 2 * STEPS, HD), BF),
        ],
        scratch_shapes=[
            VM((TP, DB, DB), BF),
            VM((TP, DB, HD), BF),
            VM((TP, DB, HD), BF),
            VM((HEADS, ROWS, HD), F32),
            VM((ROWS, HD), F32),
            VM((ROWS, HD), F32),
            pltpu.SemaphoreType.DMA((3, TP)),
        ],
        compiler_params=limit(53),
        cost_estimate=pl.CostEstimate(
            flops=2 * ROWS * D * 768, bytes_accessed=7 * 2**20, transcendentals=0
        ),
        name="project",
    )(acts, gain, wq, wk, wv, table)


def attend_body(blk, qa, kf, vf, kc, vc, wo, *refs):
    outs = refs[:TP]
    s1_s, ctx_s, wo_s, sems = refs[TP:]
    copies = []
    for s in range(TP):
        there = pl.ds(pl.multiple_of(blk[s] * DB, DB), DB)
        copies.append(pltpu.make_async_copy(wo.at[:, there], wo_s.at[s], sems.at[s]))
    for c in copies:
        c.start()
    for n in range(NP):
        span = slice(n * GROUP, (n + 1) * GROUP)
        s1_s[span, :] = nt(qa[span, :], kc[n])
    scale = 1.0 / HD**0.5
    s1 = s1_s[...] * scale
    s2 = nt(qa[...], kf[...]) * scale
    row = lax.broadcasted_iota(jnp.int32, (NP * GROUP, ROWS), 0)
    col = lax.broadcasted_iota(jnp.int32, (NP * GROUP, ROWS), 1)
    seen = ((row // GROUP) == (col % NP)) & ((col // NP) <= (row % STEPS))
    s2 = jnp.where(seen, s2, -jnp.inf)
    top = jnp.maximum(jnp.max(s1, -1, keepdims=True), jnp.max(s2, -1, keepdims=True))
    e1 = jnp.exp(s1 - top)
    e2 = jnp.exp(s2 - top)
    total = jnp.sum(e1, -1, keepdims=True) + jnp.sum(e2, -1, keepdims=True)
    w1 = (e1 / total).astype(BF)
    w2 = (e2 / total).astype(BF)
    c2 = mm(w2, vf[...])
    for n in range(NP):
        span = slice(n * GROUP, (n + 1) * GROUP)
        cn = (mm(w1[span], vc[n]) + c2[span]).astype(BF).astype(F32)
        for g in range(HEADS):
            ctx_s[g, pl.ds(n, STEPS, stride=NP), :] = cn[g * STEPS : (g + 1) * STEPS]
    ctx = jnp.concatenate([ctx_s[g] for g in range(HEADS)], 1).astype(BF)
    for s in range(TP):
        copies[s].wait()
        outs[s][...] = mm(ctx, wo_s[s]).astype(BF)


def attend(blk, qa, kf, vf, kc, vc, wo):
    return pl.pallas_call(
        attend_body,
        in_specs=[spec(SM)] + [spec(VM)] * 5 + [spec(ANY)],
        out_specs=[spec(VM)] * TP,
        out_shape=[jax.ShapeDtypeStruct((ROWS, DB), BF)] * TP,
        scratch_shapes=[
            VM((NP * GROUP, SPAN), F32),
            VM((HEADS, ROWS, HD), F32),
            VM((TP, DB, DB), BF),
            pltpu.SemaphoreType.DMA((TP,)),
        ],
        compiler_params=limit(53),
        cost_estimate=pl.CostEstimate(
            flops=2 * ROWS * D * 640, bytes_accessed=6 * 2**20, transcendentals=NP * 16 * 192
        ),
        name="attend",
    )(blk, qa, kf, vf, kc, vc, wo)


def mix_body(*refs):
    parts = refs[:TP]
    act, twist, attn, sums = refs[TP:]
    mix = parts[0][...].astype(F32)
    for s in range(1, TP):
        mix = mix + parts[s][...].astype(F32)
    attn[...] = mix.astype(BF)
    summed = act[...].astype(F32) + mix
    aligned = jnp.sum(summed * twist[...], -1, keepdims=True)
    energy = jnp.sum(summed * summed, -1, keepdims=True)
    row = lax.broadcasted_iota(jnp.int32, (ROWS, HD), 0)
    lane = lax.broadcasted_iota(jnp.int32, (ROWS, HD), 1)
    both = jnp.where(lane == row, aligned, 0.0) + jnp.where(lane == row + ROWS, energy, 0.0)
    sums[...] = jnp.sum(both, 0, keepdims=True)


def mix(parts, act, twist):
    sd = jax.ShapeDtypeStruct
    return pl.pallas_call(
        mix_body,
        in_specs=[spec(VM)] * (TP + 2),
        out_specs=[spec(VM)] * 2,
        out_shape=[sd((ROWS, DB), BF), sd((1, HD), F32)],
        compiler_params=limit(8),
        name="mix",
    )(*parts, act, twist)


def weigh_body(idx, *refs):
    parts = refs[:PAIRS]
    reward, previous, fresh, line, sent = refs[PAIRS:]
    total = parts[0][...]
    for s in range(1, PAIRS):
        total = total + parts[s][...]
    energy = pltpu.roll(total, ROWS, 1)
    score = total / jnp.sqrt(energy / D + 1e-06) + reward[...]
    gain = score
    for t in range(1, STEPS):
        gain = gain + pltpu.roll(score, HD - NP * t, 1)
    logw = previous[...] + gain
    line[...] = logw
    high = logw.astype(BF).astype(F32)
    middle = (logw - high).astype(BF).astype(F32)
    low = logw - high - middle
    row = lax.broadcasted_iota(jnp.int32, (8, HD), 0)
    parts = jnp.where(row == 0, high, jnp.where(row == 1, middle, jnp.where(row == 2, low, 0.0)))
    parts = parts.astype(BF)
    for d in range(NDOM):
        sent[d, 0] = fresh[idx[1, 2 * d]]
        sent[d, 1] = fresh[idx[1, 2 * d + 1]]
        sent[d, 2] = parts


def weigh(idx, parts, reward, previous, fresh):
    sd = jax.ShapeDtypeStruct
    return pl.pallas_call(
        weigh_body,
        in_specs=[spec(SM)] + [spec(VM)] * (PAIRS + 3),
        out_specs=[spec(VM)] * 2,
        out_shape=[sd((1, HD), F32), sd((NDOM, 3, 8, HD), BF)],
        compiler_params=limit(8),
        name="weigh",
    )(idx, *parts, reward, previous, fresh)


def finish_body(idx, line, got, keys_in, values_in, logw, keys, values, all_s, f_s, k_s, v_s, sems):
    for k in range(NP):
        code = idx[1, 64 + k]
        f_s[pl.ds(k, 2 * STEPS, stride=NP), :] = got[code // 2, code % 2].astype(F32)
    half = STEPS * NP
    k_s[...] = f_s[0:half, :].reshape(STEPS, NP, HD).astype(BF)
    v_s[...] = f_s[half : 2 * half, :].reshape(STEPS, NP, HD).astype(BF)
    tail = pl.ds(SPAN, STEPS)
    copies = [
        pltpu.make_async_copy(k_s, keys.at[tail], sems.at[0]),
        pltpu.make_async_copy(v_s, values.at[tail], sems.at[1]),
    ]
    for c in copies:
        c.start()
    for d in range(NDOM):
        all_s[d : d + 1, :] = jnp.sum(got[d, 2].astype(F32), 0, keepdims=True)
    lane = lax.broadcasted_iota(jnp.int32, (NDOM, HD), 1)
    all_w = jnp.where(lane < NP, all_s[...], -jnp.inf)
    largest = jnp.max(all_w, keepdims=True)
    mass = jnp.sum(jnp.exp(all_w - largest), keepdims=True)
    logw[...] = (line[...] - (largest + jnp.log(mass)))[:, 0:NP]
    for c in copies:
        c.wait()


def finish(idx, line, got, keys, values):
    sd = jax.ShapeDtypeStruct
    return pl.pallas_call(
        finish_body,
        in_specs=[spec(SM)] + [spec(VM)] * 2 + [spec(ANY)] * 2,
        out_specs=[spec(VM)] + [spec(ANY)] * 2,
        out_shape=[sd((1, NP), F32), sd(keys.shape, BF), sd(values.shape, BF)],
        scratch_shapes=[
            VM((NDOM, HD), F32),
            VM((2 * STEPS * NP, HD), F32),
            VM((STEPS, NP, HD), BF),
            VM((STEPS, NP, HD), BF),
            pltpu.SemaphoreType.DMA((2,)),
        ],
        input_output_aliases={3: 1, 4: 2},
        compiler_params=limit(8),
        name="finish",
    )(idx, line, got, keys, values)


def plan_body(me_ref, *refs):
    out = refs[-1]
    me = me_ref[0]
    blocks = jnp.concatenate([r[...] for r in refs[:-1]], 0).astype(F32)
    rel = lax.broadcasted_iota(jnp.int32, (NDOM, NDOM), 1)
    holder = me ^ rel
    sorted_rows = lax.broadcasted_iota(jnp.int32, (NDOM, NDOM), 0) == holder
    counts = mm(sorted_rows.astype(F32), blocks)
    r16 = lax.broadcasted_iota(jnp.int32, (NP, NP), 0)
    c16 = lax.broadcasted_iota(jnp.int32, (NP, NP), 1)
    within = mm(counts, (r16 <= c16).astype(F32))
    r32 = lax.broadcasted_iota(jnp.int32, (NDOM, NDOM), 0)
    c32 = lax.broadcasted_iota(jnp.int32, (NDOM, NDOM), 1)
    before = jnp.sum(mm((c32 < r32).astype(F32), counts), -1, keepdims=True)
    ends = (within + before).astype(jnp.int32)
    before = before.astype(jnp.int32)
    device = lax.broadcasted_iota(jnp.int32, (NDOM, 1), 0)
    chip_end = jnp.where(device % 2 == 1, ends[:, NP - 1 : NP], -1)
    chip = me // 2
    first = jnp.sum(jnp.where(device == 2 * chip, before, 0))
    lane = lax.broadcasted_iota(jnp.int32, (1, HD), 1)
    dest = 2 * (lane // 4) + me % 2
    sent = first + ((dest - first) & (NDOM - 1)) + NDOM * (lane % 4)
    kept = NDOM * (lane - 64) + me
    found = jnp.zeros((NDOM, HD), jnp.int32)
    for j in range(NP):
        found = found + (ends[:, j : j + 1] <= sent).astype(jnp.int32)
    particle = jnp.sum(found, 0, keepdims=True) - 2 * NP * chip
    particle = jnp.clip(particle, 0, 2 * NP - 1)
    passed = (chip_end >= 0) & (chip_end <= kept)
    source = jnp.sum(passed.astype(jnp.int32), 0, keepdims=True)
    base = jnp.max(jnp.where(passed, chip_end, 0), 0, keepdims=True)
    slot = jnp.clip((kept - base) // NDOM, 0, 3)
    arrived = 4 * jnp.clip(source, 0, NCHIP - 1) + slot
    owned = jnp.sum(counts, -1, keepdims=True).astype(jnp.int32)
    pair = lax.broadcasted_iota(jnp.int32, (NDOM, HD), 1)
    most = jnp.max(jnp.sum(jnp.where(pair == device // 2, owned, 0), 0, keepdims=True))
    line = jnp.where(lane < 64, particle, jnp.where(lane < 80, arrived, most))

    own = jnp.sum(jnp.where(device == me, before, 0))
    sent = own + ((lane // 2 - own) & (NDOM - 1)) + NDOM * (lane % 2)
    found = jnp.zeros((NDOM, HD), jnp.int32)
    for j in range(NP):
        found = found + (ends[:, j : j + 1] <= sent).astype(jnp.int32)
    particle = jnp.sum(found, 0, keepdims=True) - NP * me
    particle = jnp.clip(particle, 0, NP - 1)
    passed = ends[:, NP - 1 : NP] <= kept
    source = jnp.sum(passed.astype(jnp.int32), 0, keepdims=True)
    base = jnp.max(jnp.where(passed, ends[:, NP - 1 : NP], 0), 0, keepdims=True)
    slot = jnp.clip((kept - base) // NDOM, 0, 1)
    arrived = 2 * jnp.clip(source, 0, NDOM - 1) + slot
    second = jnp.where(lane < 64, particle, arrived)
    row = lax.broadcasted_iota(jnp.int32, (8, HD), 0)
    out[...] = jnp.where(row == 0, line, second)


def plan(me, blocks):
    return pl.pallas_call(
        plan_body,
        in_specs=[spec(SM)] + [spec(VM)] * len(blocks),
        out_specs=spec(VM),
        out_shape=jax.ShapeDtypeStruct((8, HD), jnp.int32),
        compiler_params=limit(8),
        name="plan",
    )(me, *blocks)


def pack_body(me_ref, idx, *refs):
    half = (len(refs) - 3) // 2
    own, partner = (refs[:half], refs[half : 2 * half])
    out, rows, sems = refs[2 * half :]
    core = me_ref[0] % 2
    loads, at = ([], 0)
    for n in range(half):
        length = own[n].shape[1]
        for side, ref in ((core, own[n]), (1 - core, partner[n])):
            there = rows.at[pl.ds(side * NP, NP), pl.ds(at, length), :]
            loads.append(pltpu.make_async_copy(ref, there, sems.at[len(loads) + 1]))
        at += length
    for c in loads:
        c.start()
    for c in loads:
        c.wait()
    for q in range(NCHIP):
        for s in range(SLOTS):
            pltpu.make_async_copy(rows.at[idx[0, 4 * q + s]], out.at[q, s], sems.at[0]).start()
    pltpu.make_async_copy(out, out, sems.at[0]).wait()


def pack(me, idx, own, partner):
    length = sum(a.shape[1] for a in own)
    return pl.pallas_call(
        pack_body,
        in_specs=[spec(SM), spec(SM)] + [spec(ANY)] * (2 * len(own)),
        out_specs=spec(ANY),
        out_shape=jax.ShapeDtypeStruct((NCHIP, SLOTS, length, HD), BF),
        scratch_shapes=[
            VM((2 * NP, length, HD), BF),
            pltpu.SemaphoreType.DMA((1 + 2 * len(own),)),
        ],
        compiler_params=limit(16),
        name="pack",
    )(me, idx, *own, *partner)


def place_body(slots, idx, rows, keys, values, sems):
    copies = []
    for k in range(NP):
        code = idx[0, 64 + k]
        slot = jnp.minimum(code % 4, slots - 1)
        for n, out in enumerate((keys, values)):
            part = rows.at[code // 4, slot, pl.ds(n * SPAN, SPAN), :]
            copies.append(pltpu.make_async_copy(part, out.at[k], sems.at[n, k]))
    for c in copies:
        c.start()
    for c in copies:
        c.wait()


def place(idx, rows):
    slots = rows.shape[1]
    return pl.pallas_call(
        lambda *refs: place_body(slots, *refs),
        in_specs=[spec(SM), spec(ANY)],
        out_specs=[spec(VM)] * 2,
        out_shape=[jax.ShapeDtypeStruct((NP, SPAN, HD), BF)] * 2,
        scratch_shapes=[pltpu.SemaphoreType.DMA((2, NP))],
        compiler_params=limit(16),
        name="place",
    )(idx, rows)


def met(value, axis, step):
    length = lax.axis_size(axis)
    return lax.ppermute(value, axis, [(i, i ^ step) for i in range(length)])


def swapped(value):
    return met(value, "dom", 1)


def next_chip(value):
    return lax.ppermute(value, "dom", [(i, (i + 2) % NDOM) for i in range(NDOM)])


SAME_CORE = [list(range(c, NDOM, 2)) for c in range(2)]


def exchanged(rows):
    return lax.all_to_all(rows, "dom", 0, 0, tiled=True, axis_index_groups=SAME_CORE)


def spread_counts(copy_counts):
    own = copy_counts.reshape(1, NP)
    chip = jnp.concatenate([own, swapped(own)], 0)
    row = jnp.concatenate([chip] + [met(chip, "dom", 2 * s) for s in range(1, 4)], 0)
    return [row] + [met(row, "dom", 8 * s) for s in range(1, 4)]


def rotation_table():
    frequency = np.float32(500000.0) ** (-2.0 * np.arange(HD // 2, dtype=np.float32) / HD)
    angles = (SPAN + np.arange(STEPS, dtype=np.float32))[:, None] * frequency.astype(np.float32)
    cosine = np.concatenate([np.cos(angles), np.cos(angles)], 1)
    sine = np.concatenate([-np.sin(angles), np.sin(angles)], 1)
    return np.stack([np.repeat(cosine, NP, 0), np.repeat(sine, NP, 0)]).astype(np.float32)


def local(
    activations,
    norm_gain,
    w_query,
    w_key,
    value_weight,
    w_output,
    cache_keys,
    cache_values,
    tokens,
    twisting_table,
    twist_vec,
    previous_log_weights,
    copy_counts,
):
    dom = lax.axis_index("dom")
    tp = lax.axis_index("tp")
    me = dom.reshape(1)
    blk = (tp ^ np.arange(TP)).astype(jnp.int32)
    act = activations.reshape(ROWS, DB)

    gathered = lax.all_to_all(
        jnp.broadcast_to(act[None], (TP, ROWS, DB)), "tp", 0, 0, tiled=True
    )
    idx = plan(me, spread_counts(copy_counts))
    partner_keys = swapped(cache_keys)
    partner_values = swapped(cache_values)
    packed = pack(me, idx, [cache_keys, cache_values], [partner_keys, partner_values])
    rows = exchanged(packed)

    packed, gathered = lax.optimization_barrier((packed, gathered))
    qa, kf, vf, fresh = project(
        gathered, norm_gain.reshape(TP, DB), w_query, w_key, value_weight, rotation_table()
    )
    partials = attend(blk, qa, kf, vf, cache_keys, cache_values, w_output)
    tokens, *partials = lax.optimization_barrier((tokens, *partials))
    reward = twisting_table[tokens.reshape(ROWS)].astype(F32)
    reward = jnp.pad(reward, (0, HD - ROWS)).reshape(1, HD)
    previous = jnp.pad(previous_log_weights, (0, HD - NP)).reshape(1, HD)
    parts = [partials[0]] + [met(partials[s], "tp", s) for s in range(1, TP)]
    attn, sums = mix(parts, act, twist_vec.reshape(1, DB))
    sums = sums + met(sums, "tp", 1)
    all_sums = [sums] + [met(sums, "tp", 2 * s) for s in range(1, PAIRS)]
    line, sent = weigh(idx, all_sums, reward, previous, fresh)
    sent, rows = lax.optimization_barrier((sent, rows))
    got = lax.all_to_all(sent, "dom", 0, 0, tiled=True)

    def usual(rows, *_):
        return tuple(place(idx, rows))

    def crowded(rows, partner_keys, partner_values, idx):
        even = dom % 2 == 0
        mine = jnp.concatenate([cache_keys, cache_values], 1)
        other = jnp.concatenate([partner_keys, partner_values], 1)
        chip_rows = jnp.concatenate(
            [jnp.where(even, mine, other), jnp.where(even, other, mine)], 0
        )
        chosen = chip_rows[idx[0, 3:64:4]]
        chip = dom // 2

        def turn(step, state):
            passing, more = state
            passing = next_chip(passing)
            return passing, more.at[(chip - step) % NCHIP].set(passing[chip])

        start = (chosen, chosen)
        more = lax.fori_loop(1, NCHIP, turn, start)[1].at[chip].set(chosen[chip])
        return tuple(place(idx, jnp.concatenate([rows, more[:, None]], 1)))

    old_keys, old_values = lax.cond(
        idx[0, 127] > SLOTS * NDOM,
        crowded,
        usual,
        rows,
        partner_keys,
        partner_values,
        idx,
    )

    def by_position(old):
        return jnp.pad(jnp.transpose(old, (1, 0, 2)), ((0, STEPS), (0, 0), (0, 0)))

    out_logw, new_keys, new_values = finish(
        idx, line, got, by_position(old_keys), by_position(old_values)
    )
    return (
        attn.reshape(STEPS, NP, DB),
        jnp.transpose(new_keys, (1, 0, 2)),
        jnp.transpose(new_values, (1, 0, 2)),
        out_logw.reshape(NP),
    )


def solution(mesh):
    return jax.shard_map(
        local,
        mesh=mesh,
        in_specs=(
            P(None, "dom", "tp"),
            P(),
            P(None, "tp"),
            P(None, "tp"),
            P(None, "tp"),
            P("tp", None),
            P("dom", None, "tp"),
            P("dom", None, "tp"),
            P(None, "dom"),
            P(),
            P("tp"),
            P("dom"),
            P("dom"),
        ),
        out_specs=(P(None, "dom", "tp"), P("dom", None, "tp"), P("dom", None, "tp"), P("dom")),
        check_vma=False,
    )
```

```python
import jax
import jax.numpy as jnp
import numpy as np
from jax import lax
from jax.experimental import pallas as pl
from jax.experimental.pallas import tpu as pltpu
from jax.sharding import PartitionSpec as P

D = 4096
HD = 128
STEPS = 4
NP = 16
ROWS = STEPS * NP
SPAN = 128
TP = 8
PAIRS = TP // 2
DB = D // TP
HEADS = DB // HD
GROUP = HEADS * STEPS
NDOM = 32
NCHIP = 16
SLOTS = 3
BF = jnp.bfloat16
F32 = jnp.float32
ANY = pl.ANY
VM = pltpu.VMEM
SM = pltpu.SMEM


def spec(space):
    return pl.BlockSpec(memory_space=space)


def limit(mib):
    return pltpu.CompilerParams(vmem_limit_bytes=mib * 2**20)


def nt(a, b):
    return lax.dot_general(a, b, (((1,), (1,)), ((), ())), preferred_element_type=F32)


def mm(a, b):
    return jnp.dot(a, b, preferred_element_type=F32)


def project_body(acts, gain, wq, wk, wv, table, qa, kf, vf, fresh, *scratch):
    wq_s, wk_s, wv_s, q_s, kf_s, vf_s, sems = scratch
    copies = []
    for s in range(TP):
        part = pl.ds(s * DB, DB)
        copies.append(
            [
                pltpu.make_async_copy(w.at[part, :], w_s.at[s], sems.at[n, s])
                for n, (w, w_s) in enumerate(((wq, wq_s), (wk, wk_s), (wv, wv_s)))
            ]
        )
    for group in copies:
        for c in group:
            c.start()
    square = jnp.zeros((ROWS, 1), F32)
    for s in range(TP):
        x = acts[s].astype(F32)
        square = square + jnp.sum(x * x, -1, keepdims=True)
    inv = lax.rsqrt(square / D + 1e-05)
    q = jnp.zeros((ROWS, DB), F32)
    k = jnp.zeros((ROWS, HD), F32)
    v = jnp.zeros((ROWS, HD), F32)
    for s in range(TP):
        x = acts[s].astype(F32)
        normed = (x * inv * gain[s : s + 1, :]).astype(BF)
        for c in copies[s]:
            c.wait()
        q = q + mm(normed, wq_s[s])
        k = k + mm(normed, wk_s[s])
        v = v + mm(normed, wv_s[s])
    cosine = table[0]
    sine = table[1]

    def turned(u):
        return (u * cosine + pltpu.roll(u, HD // 2, 1) * sine).astype(BF)

    for g in range(HEADS):
        q_s[g] = turned(q[:, g * HD : (g + 1) * HD]).astype(F32)
    k = turned(k)
    v = v.astype(BF)
    kf[...] = k
    vf[...] = v
    kf_s[...] = k.astype(F32)
    vf_s[...] = v.astype(F32)
    for n in range(NP):
        mine = pl.ds(n, STEPS, stride=NP)
        fresh[n] = jnp.concatenate([kf_s[mine, :], vf_s[mine, :]], 0).astype(BF)
        qa[n * GROUP : (n + 1) * GROUP, :] = jnp.concatenate(
            [q_s[g, mine, :] for g in range(HEADS)], 0
        ).astype(BF)


def project(acts, gain, wq, wk, wv, table):
    sd = jax.ShapeDtypeStruct
    return pl.pallas_call(
        project_body,
        in_specs=[spec(VM)] * 2 + [spec(ANY)] * 3 + [spec(VM)],
        out_specs=[spec(VM)] * 4,
        out_shape=[
            sd((NP * GROUP, HD), BF),
            sd((ROWS, HD), BF),
            sd((ROWS, HD), BF),
            sd((NP, 2 * STEPS, HD), BF),
        ],
        scratch_shapes=[
            VM((TP, DB, DB), BF),
            VM((TP, DB, HD), BF),
            VM((TP, DB, HD), BF),
            VM((HEADS, ROWS, HD), F32),
            VM((ROWS, HD), F32),
            VM((ROWS, HD), F32),
            pltpu.SemaphoreType.DMA((3, TP)),
        ],
        compiler_params=limit(53),
        cost_estimate=pl.CostEstimate(
            flops=2 * ROWS * D * 768, bytes_accessed=7 * 2**20, transcendentals=0
        ),
        name="project",
    )(acts, gain, wq, wk, wv, table)


def attend_body(blk, qa, kf, vf, kc, vc, wo, *refs):
    outs = refs[:TP]
    s1_s, ctx_s, wo_s, sems = refs[TP:]
    copies = []
    for s in range(TP):
        there = pl.ds(pl.multiple_of(blk[s] * DB, DB), DB)
        copies.append(pltpu.make_async_copy(wo.at[:, there], wo_s.at[s], sems.at[s]))
    for c in copies:
        c.start()
    for n in range(NP):
        span = slice(n * GROUP, (n + 1) * GROUP)
        s1_s[span, :] = nt(qa[span, :], kc[n])
    scale = 1.0 / HD**0.5
    s1 = s1_s[...] * scale
    s2 = nt(qa[...], kf[...]) * scale
    row = lax.broadcasted_iota(jnp.int32, (NP * GROUP, ROWS), 0)
    col = lax.broadcasted_iota(jnp.int32, (NP * GROUP, ROWS), 1)
    seen = ((row // GROUP) == (col % NP)) & ((col // NP) <= (row % STEPS))
    s2 = jnp.where(seen, s2, -jnp.inf)
    top = jnp.maximum(jnp.max(s1, -1, keepdims=True), jnp.max(s2, -1, keepdims=True))
    e1 = jnp.exp(s1 - top)
    e2 = jnp.exp(s2 - top)
    total = jnp.sum(e1, -1, keepdims=True) + jnp.sum(e2, -1, keepdims=True)
    w1 = (e1 / total).astype(BF)
    w2 = (e2 / total).astype(BF)
    c2 = mm(w2, vf[...])
    for n in range(NP):
        span = slice(n * GROUP, (n + 1) * GROUP)
        cn = (mm(w1[span], vc[n]) + c2[span]).astype(BF).astype(F32)
        for g in range(HEADS):
            ctx_s[g, pl.ds(n, STEPS, stride=NP), :] = cn[g * STEPS : (g + 1) * STEPS]
    ctx = jnp.concatenate([ctx_s[g] for g in range(HEADS)], 1).astype(BF)
    for s in range(TP):
        copies[s].wait()
        outs[s][...] = mm(ctx, wo_s[s]).astype(BF)


def attend(blk, qa, kf, vf, kc, vc, wo):
    return pl.pallas_call(
        attend_body,
        in_specs=[spec(SM)] + [spec(VM)] * 5 + [spec(ANY)],
        out_specs=[spec(VM)] * TP,
        out_shape=[jax.ShapeDtypeStruct((ROWS, DB), BF)] * TP,
        scratch_shapes=[
            VM((NP * GROUP, SPAN), F32),
            VM((HEADS, ROWS, HD), F32),
            VM((TP, DB, DB), BF),
            pltpu.SemaphoreType.DMA((TP,)),
        ],
        compiler_params=limit(53),
        cost_estimate=pl.CostEstimate(
            flops=2 * ROWS * D * 640, bytes_accessed=6 * 2**20, transcendentals=NP * 16 * 192
        ),
        name="attend",
    )(blk, qa, kf, vf, kc, vc, wo)


def mix_body(*refs):
    parts = refs[:TP]
    act, twist, attn, sums = refs[TP:]
    mix = parts[0][...].astype(F32)
    for s in range(1, TP):
        mix = mix + parts[s][...].astype(F32)
    attn[...] = mix.astype(BF)
    summed = act[...].astype(F32) + mix
    aligned = jnp.sum(summed * twist[...], -1, keepdims=True)
    energy = jnp.sum(summed * summed, -1, keepdims=True)
    row = lax.broadcasted_iota(jnp.int32, (ROWS, HD), 0)
    lane = lax.broadcasted_iota(jnp.int32, (ROWS, HD), 1)
    both = jnp.where(lane == row, aligned, 0.0) + jnp.where(lane == row + ROWS, energy, 0.0)
    sums[...] = jnp.sum(both, 0, keepdims=True)


def mix(parts, act, twist):
    sd = jax.ShapeDtypeStruct
    return pl.pallas_call(
        mix_body,
        in_specs=[spec(VM)] * (TP + 2),
        out_specs=[spec(VM)] * 2,
        out_shape=[sd((ROWS, DB), BF), sd((1, HD), F32)],
        compiler_params=limit(8),
        name="mix",
    )(*parts, act, twist)


def weigh_body(idx, *refs):
    parts = refs[:PAIRS]
    reward, previous, fresh, line, sent = refs[PAIRS:]
    total = parts[0][...]
    for s in range(1, PAIRS):
        total = total + parts[s][...]
    energy = pltpu.roll(total, ROWS, 1)
    score = total / jnp.sqrt(energy / D + 1e-06) + reward[...]
    gain = score
    for t in range(1, STEPS):
        gain = gain + pltpu.roll(score, HD - NP * t, 1)
    logw = previous[...] + gain
    line[...] = logw
    high = logw.astype(BF).astype(F32)
    middle = (logw - high).astype(BF).astype(F32)
    low = logw - high - middle
    row = lax.broadcasted_iota(jnp.int32, (8, HD), 0)
    parts = jnp.where(row == 0, high, jnp.where(row == 1, middle, jnp.where(row == 2, low, 0.0)))
    parts = parts.astype(BF)
    for d in range(NDOM):
        sent[d, 0] = fresh[idx[1, 2 * d]]
        sent[d, 1] = fresh[idx[1, 2 * d + 1]]
        sent[d, 2] = parts


def weigh(idx, parts, reward, previous, fresh):
    sd = jax.ShapeDtypeStruct
    return pl.pallas_call(
        weigh_body,
        in_specs=[spec(SM)] + [spec(VM)] * (PAIRS + 3),
        out_specs=[spec(VM)] * 2,
        out_shape=[sd((1, HD), F32), sd((NDOM, 3, 8, HD), BF)],
        compiler_params=limit(8),
        name="weigh",
    )(idx, *parts, reward, previous, fresh)


def finish_body(idx, line, got, keys_in, values_in, logw, keys, values, all_s, f_s, k_s, v_s, sems):
    for k in range(NP):
        code = idx[1, 64 + k]
        f_s[pl.ds(k, 2 * STEPS, stride=NP), :] = got[code // 2, code % 2].astype(F32)
    half = STEPS * NP
    k_s[...] = f_s[0:half, :].reshape(STEPS, NP, HD).astype(BF)
    v_s[...] = f_s[half : 2 * half, :].reshape(STEPS, NP, HD).astype(BF)
    tail = pl.ds(SPAN, STEPS)
    copies = [
        pltpu.make_async_copy(k_s, keys.at[tail], sems.at[0]),
        pltpu.make_async_copy(v_s, values.at[tail], sems.at[1]),
    ]
    for c in copies:
        c.start()
    for d in range(NDOM):
        all_s[d : d + 1, :] = jnp.sum(got[d, 2].astype(F32), 0, keepdims=True)
    lane = lax.broadcasted_iota(jnp.int32, (NDOM, HD), 1)
    all_w = jnp.where(lane < NP, all_s[...], -jnp.inf)
    largest = jnp.max(all_w, keepdims=True)
    mass = jnp.sum(jnp.exp(all_w - largest), keepdims=True)
    logw[...] = (line[...] - (largest + jnp.log(mass)))[:, 0:NP]
    for c in copies:
        c.wait()


def finish(idx, line, got, keys, values):
    sd = jax.ShapeDtypeStruct
    return pl.pallas_call(
        finish_body,
        in_specs=[spec(SM)] + [spec(VM)] * 2 + [spec(ANY)] * 2,
        out_specs=[spec(VM)] + [spec(ANY)] * 2,
        out_shape=[sd((1, NP), F32), sd(keys.shape, BF), sd(values.shape, BF)],
        scratch_shapes=[
            VM((NDOM, HD), F32),
            VM((2 * STEPS * NP, HD), F32),
            VM((STEPS, NP, HD), BF),
            VM((STEPS, NP, HD), BF),
            pltpu.SemaphoreType.DMA((2,)),
        ],
        input_output_aliases={3: 1, 4: 2},
        compiler_params=limit(8),
        name="finish",
    )(idx, line, got, keys, values)


def plan_body(me_ref, *refs):
    out, crowd = refs[-2:]
    me = me_ref[0]
    blocks = jnp.concatenate([r[...] for r in refs[:-2]], 0).astype(F32)
    rel = lax.broadcasted_iota(jnp.int32, (NDOM, NDOM), 1)
    back_y = (me // 8 - rel // 8) & 3
    back_x = (me // 2 - rel // 2) & 3
    holder = 8 * back_y + 2 * back_x + ((me + rel) & 1)
    sorted_rows = lax.broadcasted_iota(jnp.int32, (NDOM, NDOM), 0) == holder
    counts = mm(sorted_rows.astype(F32), blocks)
    r16 = lax.broadcasted_iota(jnp.int32, (NP, NP), 0)
    c16 = lax.broadcasted_iota(jnp.int32, (NP, NP), 1)
    within = mm(counts, (r16 <= c16).astype(F32))
    r32 = lax.broadcasted_iota(jnp.int32, (NDOM, NDOM), 0)
    c32 = lax.broadcasted_iota(jnp.int32, (NDOM, NDOM), 1)
    before = jnp.sum(mm((c32 < r32).astype(F32), counts), -1, keepdims=True)
    ends = (within + before).astype(jnp.int32)
    before = before.astype(jnp.int32)
    device = lax.broadcasted_iota(jnp.int32, (NDOM, 1), 0)
    chip_end = jnp.where(device % 2 == 1, ends[:, NP - 1 : NP], -1)
    chip = me // 2
    first = jnp.sum(jnp.where(device == 2 * chip, before, 0))
    lane = lax.broadcasted_iota(jnp.int32, (1, HD), 1)
    dest = 2 * (lane // 4) + me % 2
    sent = first + ((dest - first) & (NDOM - 1)) + NDOM * (lane % 4)
    kept = NDOM * (lane - 64) + me
    found = jnp.zeros((NDOM, HD), jnp.int32)
    for j in range(NP):
        found = found + (ends[:, j : j + 1] <= sent).astype(jnp.int32)
    particle = jnp.sum(found, 0, keepdims=True) - 2 * NP * chip
    particle = jnp.clip(particle, 0, 2 * NP - 1)
    passed = (chip_end >= 0) & (chip_end <= kept)
    source = jnp.sum(passed.astype(jnp.int32), 0, keepdims=True)
    base = jnp.max(jnp.where(passed, chip_end, 0), 0, keepdims=True)
    slot = jnp.clip((kept - base) // NDOM, 0, 3)
    arrived = 4 * jnp.clip(source, 0, NCHIP - 1) + slot
    owned = jnp.sum(counts, -1, keepdims=True).astype(jnp.int32)
    pair = lax.broadcasted_iota(jnp.int32, (NDOM, HD), 1)
    most = jnp.max(jnp.sum(jnp.where(pair == device // 2, owned, 0), 0, keepdims=True))
    line = jnp.where(lane < 64, particle, jnp.where(lane < 80, arrived, most))

    own = jnp.sum(jnp.where(device == me, before, 0))
    sent = own + ((lane // 2 - own) & (NDOM - 1)) + NDOM * (lane % 2)
    found = jnp.zeros((NDOM, HD), jnp.int32)
    for j in range(NP):
        found = found + (ends[:, j : j + 1] <= sent).astype(jnp.int32)
    particle = jnp.sum(found, 0, keepdims=True) - NP * me
    particle = jnp.clip(particle, 0, NP - 1)
    passed = ends[:, NP - 1 : NP] <= kept
    source = jnp.sum(passed.astype(jnp.int32), 0, keepdims=True)
    base = jnp.max(jnp.where(passed, ends[:, NP - 1 : NP], 0), 0, keepdims=True)
    slot = jnp.clip((kept - base) // NDOM, 0, 1)
    arrived = 2 * jnp.clip(source, 0, NDOM - 1) + slot
    second = jnp.where(lane < 64, particle, arrived)
    row = lax.broadcasted_iota(jnp.int32, (8, HD), 0)
    out[...] = jnp.where(row == 0, line, second)
    crowd[0] = most


def plan(me, blocks):
    return pl.pallas_call(
        plan_body,
        in_specs=[spec(SM)] + [spec(VM)] * len(blocks),
        out_specs=[spec(VM), spec(SM)],
        out_shape=[
            jax.ShapeDtypeStruct((8, HD), jnp.int32),
            jax.ShapeDtypeStruct((1,), jnp.int32),
        ],
        compiler_params=limit(8),
        name="plan",
    )(me, *blocks)


def pack_body(me_ref, idx, *refs):
    half = (len(refs) - 3) // 2
    own, partner = (refs[:half], refs[half : 2 * half])
    out, rows, sems = refs[2 * half :]
    core = me_ref[0] % 2
    loads, at = ([], 0)
    for n in range(half):
        length = own[n].shape[1]
        for side, ref in ((core, own[n]), (1 - core, partner[n])):
            there = rows.at[pl.ds(side * NP, NP), pl.ds(at, length), :]
            loads.append(pltpu.make_async_copy(ref, there, sems.at[len(loads) + 1]))
        at += length
    for c in loads:
        c.start()
    for c in loads:
        c.wait()
    for q in range(NCHIP):
        for s in range(SLOTS):
            pltpu.make_async_copy(rows.at[idx[0, 4 * q + s]], out.at[q, s], sems.at[0]).start()
    pltpu.make_async_copy(out, out, sems.at[0]).wait()


def pack(me, idx, own, partner):
    length = sum(a.shape[1] for a in own)
    return pl.pallas_call(
        pack_body,
        in_specs=[spec(SM), spec(SM)] + [spec(ANY)] * (2 * len(own)),
        out_specs=spec(ANY),
        out_shape=jax.ShapeDtypeStruct((NCHIP, SLOTS, length, HD), BF),
        scratch_shapes=[
            VM((2 * NP, length, HD), BF),
            pltpu.SemaphoreType.DMA((1 + 2 * len(own),)),
        ],
        compiler_params=limit(16),
        name="pack",
    )(me, idx, *own, *partner)


def place_body(slots, idx, rows, keys, values, sems):
    copies = []
    for k in range(NP):
        code = idx[0, 64 + k]
        slot = jnp.minimum(code % 4, slots - 1)
        for n, out in enumerate((keys, values)):
            part = rows.at[code // 4, slot, pl.ds(n * SPAN, SPAN), :]
            there = out.at[k, pl.ds(0, SPAN), :]
            copies.append(pltpu.make_async_copy(part, there, sems.at[n, k]))
    for c in copies:
        c.start()
    blank = jnp.zeros((NP, STEPS, HD), BF)
    for out in (keys, values):
        out[:, SPAN : SPAN + STEPS, :] = blank
    for c in copies:
        c.wait()


def place(idx, rows):
    slots = rows.shape[1]
    return pl.pallas_call(
        lambda *refs: place_body(slots, *refs),
        in_specs=[spec(SM), spec(ANY)],
        out_specs=[spec(VM)] * 2,
        out_shape=[jax.ShapeDtypeStruct((NP, SPAN + STEPS, HD), BF)] * 2,
        scratch_shapes=[pltpu.SemaphoreType.DMA((2, NP))],
        compiler_params=limit(16),
        name="place",
    )(idx, rows)


def shifted(value, shift):
    return lax.ppermute(value, "tp", [(i, (i + shift) % TP) for i in range(TP)])


def z_swapped(value):
    return lax.ppermute(value, "tp", [(i, i ^ 1) for i in range(TP)])


def swapped(value):
    return lax.ppermute(value, "dom", [(i, i ^ 1) for i in range(NDOM)])


def next_chip(value):
    return lax.ppermute(value, "dom", [(i, (i + 2) % NDOM) for i in range(NDOM)])


SAME_CORE = [list(range(c, NDOM, 2)) for c in range(2)]


def exchanged(rows):
    return lax.all_to_all(rows, "dom", 0, 0, tiled=True, axis_index_groups=SAME_CORE)


def moved(value, axis_stride, shift):
    def to(i):
        at = i // axis_stride % 4
        return i + ((at + shift) % 4 - at) * axis_stride

    return lax.ppermute(value, "dom", [(i, to(i)) for i in range(NDOM)])


def spread_counts(copy_counts):
    own = copy_counts.reshape(1, NP)
    chip = jnp.concatenate([own, swapped(own)], 0)
    row = jnp.concatenate([chip] + [moved(chip, 2, s) for s in range(1, 4)], 0)
    return [row] + [moved(row, 8, s) for s in range(1, 4)]


def rotation_table():
    frequency = np.float32(500000.0) ** (-2.0 * np.arange(HD // 2, dtype=np.float32) / HD)
    angles = (SPAN + np.arange(STEPS, dtype=np.float32))[:, None] * frequency.astype(np.float32)
    cosine = np.concatenate([np.cos(angles), np.cos(angles)], 1)
    sine = np.concatenate([-np.sin(angles), np.sin(angles)], 1)
    return np.stack([np.repeat(cosine, NP, 0), np.repeat(sine, NP, 0)]).astype(np.float32)


def local(
    activations,
    norm_gain,
    w_query,
    w_key,
    value_weight,
    w_output,
    cache_keys,
    cache_values,
    tokens,
    twisting_table,
    twist_vec,
    previous_log_weights,
    copy_counts,
):
    dom = lax.axis_index("dom")
    tp = lax.axis_index("tp")
    me = dom.reshape(1)
    blk = ((tp + np.arange(TP)) % TP).astype(jnp.int32)
    act = activations.reshape(ROWS, DB)

    gathered = lax.all_to_all(
        jnp.broadcast_to(act[None], (TP, ROWS, DB)), "tp", 0, 0, tiled=True
    )
    idx, crowd = plan(me, spread_counts(copy_counts))
    partner_keys = swapped(cache_keys)
    partner_values = swapped(cache_values)
    packed = pack(me, idx, [cache_keys, cache_values], [partner_keys, partner_values])
    rows = exchanged(packed)

    packed, gathered = lax.optimization_barrier((packed, gathered))
    qa, kf, vf, fresh = project(
        gathered, norm_gain.reshape(TP, DB), w_query, w_key, value_weight, rotation_table()
    )
    partials = attend(blk, qa, kf, vf, cache_keys, cache_values, w_output)
    tokens, *partials = lax.optimization_barrier((tokens, *partials))
    reward = twisting_table[tokens.reshape(ROWS)].astype(F32)
    reward = jnp.pad(reward, (0, HD - ROWS)).reshape(1, HD)
    previous = jnp.pad(previous_log_weights, (0, HD - NP)).reshape(1, HD)
    parts = [partials[0]] + [shifted(partials[s], s) for s in range(1, TP)]
    attn, sums = mix(parts, act, twist_vec.reshape(1, DB))
    sums = sums + z_swapped(sums)
    all_sums = [sums] + [shifted(sums, 2 * s) for s in range(1, PAIRS)]
    line, sent = weigh(idx, all_sums, reward, previous, fresh)
    sent, rows = lax.optimization_barrier((sent, rows))
    got = lax.all_to_all(sent, "dom", 0, 0, tiled=True)

    def usual(rows, *_):
        return tuple(place(idx, rows))

    def crowded(rows, partner_keys, partner_values, idx):
        even = dom % 2 == 0
        mine = jnp.concatenate([cache_keys, cache_values], 1)
        other = jnp.concatenate([partner_keys, partner_values], 1)
        chip_rows = jnp.concatenate(
            [jnp.where(even, mine, other), jnp.where(even, other, mine)], 0
        )
        chosen = chip_rows[idx[0, 3:64:4]]
        chip = dom // 2

        def turn(step, state):
            passing, more = state
            passing = next_chip(passing)
            return passing, more.at[(chip - step) % NCHIP].set(passing[chip])

        start = (chosen, chosen)
        more = lax.fori_loop(1, NCHIP, turn, start)[1].at[chip].set(chosen[chip])
        return tuple(place(idx, jnp.concatenate([rows, more[:, None]], 1)))

    old_keys, old_values = lax.cond(
        crowd[0] > SLOTS * NDOM,
        crowded,
        usual,
        rows,
        partner_keys,
        partner_values,
        idx,
    )

    def by_position(old):
        return jnp.transpose(old, (1, 0, 2))

    out_logw, new_keys, new_values = finish(
        idx, line, got, by_position(old_keys), by_position(old_values)
    )
    return (
        attn.reshape(STEPS, NP, DB),
        jnp.transpose(new_keys, (1, 0, 2)),
        jnp.transpose(new_values, (1, 0, 2)),
        out_logw.reshape(NP),
    )


def solution(mesh):
    return jax.shard_map(
        local,
        mesh=mesh,
        in_specs=(
            P(None, "dom", "tp"),
            P(),
            P(None, "tp"),
            P(None, "tp"),
            P(None, "tp"),
            P("tp", None),
            P("dom", None, "tp"),
            P("dom", None, "tp"),
            P(None, "dom"),
            P(),
            P("tp"),
            P("dom"),
            P("dom"),
        ),
        out_specs=(P(None, "dom", "tp"), P("dom", None, "tp"), P("dom", None, "tp"), P("dom")),
        check_vma=False,
    )
```

```python
import jax
import jax.numpy as jnp
import numpy as np
from jax import lax
from jax.experimental import pallas as pl
from jax.experimental.pallas import tpu as pltpu
from jax.sharding import PartitionSpec as P

D = 4096
HD = 128
STEPS = 4
NP = 16
ROWS = STEPS * NP
SPAN = 128
TP = 8
PAIRS = TP // 2
FAR_FIRST = (4, 3, 5, 2, 6, 1, 7)
DB = D // TP
HEADS = DB // HD
GROUP = HEADS * STEPS
NDOM = 32
NCHIP = 16
SLOTS = 3
BF = jnp.bfloat16
F32 = jnp.float32
ANY = pl.ANY
VM = pltpu.VMEM
SM = pltpu.SMEM


def spec(space):
    return pl.BlockSpec(memory_space=space)


def limit(mib):
    return pltpu.CompilerParams(vmem_limit_bytes=mib * 2**20)


def nt(a, b):
    return lax.dot_general(a, b, (((1,), (1,)), ((), ())), preferred_element_type=F32)


def mm(a, b):
    return jnp.dot(a, b, preferred_element_type=F32)


def project_body(acts, gain, wq, wk, wv, table, qa, kf, vf, fresh, *scratch):
    wq_s, wk_s, wv_s, q_s, kf_s, vf_s, sems = scratch
    copies = []
    for s in range(TP):
        part = pl.ds(s * DB, DB)
        copies.append(
            [
                pltpu.make_async_copy(w.at[part, :], w_s.at[s], sems.at[n, s])
                for n, (w, w_s) in enumerate(((wq, wq_s), (wk, wk_s), (wv, wv_s)))
            ]
        )
    for group in copies:
        for c in group:
            c.start()
    square = jnp.zeros((ROWS, 1), F32)
    for s in range(TP):
        x = acts[s].astype(F32)
        square = square + jnp.sum(x * x, -1, keepdims=True)
    inv = lax.rsqrt(square / D + 1e-05)
    q = jnp.zeros((ROWS, DB), F32)
    k = jnp.zeros((ROWS, HD), F32)
    v = jnp.zeros((ROWS, HD), F32)
    for s in range(TP):
        x = acts[s].astype(F32)
        normed = (x * inv * gain[s : s + 1, :]).astype(BF)
        for c in copies[s]:
            c.wait()
        q = q + mm(normed, wq_s[s])
        k = k + mm(normed, wk_s[s])
        v = v + mm(normed, wv_s[s])
    cosine = table[0]
    sine = table[1]

    def turned(u):
        return (u * cosine + pltpu.roll(u, HD // 2, 1) * sine).astype(BF)

    for g in range(HEADS):
        q_s[g] = turned(q[:, g * HD : (g + 1) * HD]).astype(F32)
    k = turned(k)
    v = v.astype(BF)
    kf[...] = k
    vf[...] = v
    kf_s[...] = k.astype(F32)
    vf_s[...] = v.astype(F32)
    for n in range(NP):
        mine = pl.ds(n, STEPS, stride=NP)
        fresh[n] = jnp.concatenate([kf_s[mine, :], vf_s[mine, :]], 0).astype(BF)
        qa[n * GROUP : (n + 1) * GROUP, :] = jnp.concatenate(
            [q_s[g, mine, :] for g in range(HEADS)], 0
        ).astype(BF)


def project(acts, gain, wq, wk, wv, table):
    sd = jax.ShapeDtypeStruct
    return pl.pallas_call(
        project_body,
        in_specs=[spec(VM)] * 2 + [spec(ANY)] * 3 + [spec(VM)],
        out_specs=[spec(VM)] * 4,
        out_shape=[
            sd((NP * GROUP, HD), BF),
            sd((ROWS, HD), BF),
            sd((ROWS, HD), BF),
            sd((NP, 2 * STEPS, HD), BF),
        ],
        scratch_shapes=[
            VM((TP, DB, DB), BF),
            VM((TP, DB, HD), BF),
            VM((TP, DB, HD), BF),
            VM((HEADS, ROWS, HD), F32),
            VM((ROWS, HD), F32),
            VM((ROWS, HD), F32),
            pltpu.SemaphoreType.DMA((3, TP)),
        ],
        compiler_params=limit(53),
        cost_estimate=pl.CostEstimate(
            flops=2 * ROWS * D * 768, bytes_accessed=7 * 2**20, transcendentals=0
        ),
        name="project",
    )(acts, gain, wq, wk, wv, table)


def attend_body(blk, qa, kf, vf, kc, vc, wo, *refs):
    outs = refs[:TP]
    s1_s, ctx_s, wo_s, sems = refs[TP:]
    copies = []
    for s in range(TP):
        there = pl.ds(pl.multiple_of(blk[s] * DB, DB), DB)
        copies.append(pltpu.make_async_copy(wo.at[:, there], wo_s.at[s], sems.at[s]))
    for c in copies:
        c.start()
    for n in range(NP):
        span = slice(n * GROUP, (n + 1) * GROUP)
        s1_s[span, :] = nt(qa[span, :], kc[n])
    scale = 1.0 / HD**0.5
    s1 = s1_s[...] * scale
    s2 = nt(qa[...], kf[...]) * scale
    row = lax.broadcasted_iota(jnp.int32, (NP * GROUP, ROWS), 0)
    col = lax.broadcasted_iota(jnp.int32, (NP * GROUP, ROWS), 1)
    seen = ((row // GROUP) == (col % NP)) & ((col // NP) <= (row % STEPS))
    s2 = jnp.where(seen, s2, -jnp.inf)
    top = jnp.maximum(jnp.max(s1, -1, keepdims=True), jnp.max(s2, -1, keepdims=True))
    e1 = jnp.exp(s1 - top)
    e2 = jnp.exp(s2 - top)
    total = jnp.sum(e1, -1, keepdims=True) + jnp.sum(e2, -1, keepdims=True)
    w1 = (e1 / total).astype(BF)
    w2 = (e2 / total).astype(BF)
    c2 = mm(w2, vf[...])
    for n in range(NP):
        span = slice(n * GROUP, (n + 1) * GROUP)
        cn = (mm(w1[span], vc[n]) + c2[span]).astype(BF).astype(F32)
        for g in range(HEADS):
            ctx_s[g, pl.ds(n, STEPS, stride=NP), :] = cn[g * STEPS : (g + 1) * STEPS]
    ctx = jnp.concatenate([ctx_s[g] for g in range(HEADS)], 1).astype(BF)
    for s in range(TP):
        copies[s].wait()
        outs[s][...] = mm(ctx, wo_s[s]).astype(BF)


def attend(blk, qa, kf, vf, kc, vc, wo):
    return pl.pallas_call(
        attend_body,
        in_specs=[spec(SM)] + [spec(VM)] * 5 + [spec(ANY)],
        out_specs=[spec(VM)] * TP,
        out_shape=[jax.ShapeDtypeStruct((ROWS, DB), BF)] * TP,
        scratch_shapes=[
            VM((NP * GROUP, SPAN), F32),
            VM((HEADS, ROWS, HD), F32),
            VM((TP, DB, DB), BF),
            pltpu.SemaphoreType.DMA((TP,)),
        ],
        compiler_params=limit(53),
        cost_estimate=pl.CostEstimate(
            flops=2 * ROWS * D * 640, bytes_accessed=6 * 2**20, transcendentals=NP * 16 * 192
        ),
        name="attend",
    )(blk, qa, kf, vf, kc, vc, wo)


def mix_body(*refs):
    parts = refs[:TP]
    act, twist, attn, sums = refs[TP:]
    mix = parts[0][...].astype(F32)
    for s in range(1, TP):
        mix = mix + parts[s][...].astype(F32)
    attn[...] = mix.astype(BF)
    summed = act[...].astype(F32) + mix
    aligned = jnp.sum(summed * twist[...], -1, keepdims=True)
    energy = jnp.sum(summed * summed, -1, keepdims=True)
    row = lax.broadcasted_iota(jnp.int32, (ROWS, HD), 0)
    lane = lax.broadcasted_iota(jnp.int32, (ROWS, HD), 1)
    both = jnp.where(lane == row, aligned, 0.0) + jnp.where(lane == row + ROWS, energy, 0.0)
    sums[...] = jnp.sum(both, 0, keepdims=True)


def mix(parts, act, twist):
    sd = jax.ShapeDtypeStruct
    return pl.pallas_call(
        mix_body,
        in_specs=[spec(VM)] * (TP + 2),
        out_specs=[spec(VM)] * 2,
        out_shape=[sd((ROWS, DB), BF), sd((1, HD), F32)],
        compiler_params=limit(8),
        name="mix",
    )(*parts, act, twist)


def weigh_body(idx, *refs):
    parts = refs[:PAIRS]
    reward, previous, fresh, line, sent = refs[PAIRS:]
    total = parts[0][...]
    for s in range(1, PAIRS):
        total = total + parts[s][...]
    energy = pltpu.roll(total, ROWS, 1)
    score = total / jnp.sqrt(energy / D + 1e-06) + reward[...]
    gain = score
    for t in range(1, STEPS):
        gain = gain + pltpu.roll(score, HD - NP * t, 1)
    logw = previous[...] + gain
    line[...] = logw
    high = logw.astype(BF).astype(F32)
    middle = (logw - high).astype(BF).astype(F32)
    low = logw - high - middle
    row = lax.broadcasted_iota(jnp.int32, (8, HD), 0)
    parts = jnp.where(row == 0, high, jnp.where(row == 1, middle, jnp.where(row == 2, low, 0.0)))
    parts = parts.astype(BF)
    for d in range(NDOM):
        sent[d, 0] = fresh[idx[1, 2 * d]]
        sent[d, 1] = fresh[idx[1, 2 * d + 1]]
        sent[d, 2] = parts


def weigh(idx, parts, reward, previous, fresh):
    sd = jax.ShapeDtypeStruct
    return pl.pallas_call(
        weigh_body,
        in_specs=[spec(SM)] + [spec(VM)] * (PAIRS + 3),
        out_specs=[spec(VM)] * 2,
        out_shape=[sd((1, HD), F32), sd((NDOM, 3, 8, HD), BF)],
        compiler_params=limit(8),
        name="weigh",
    )(idx, *parts, reward, previous, fresh)


def finish_body(idx, line, got, keys_in, values_in, logw, keys, values, all_s, f_s, k_s, v_s, sems):
    for k in range(NP):
        code = idx[1, 64 + k]
        f_s[pl.ds(k, 2 * STEPS, stride=NP), :] = got[code // 2, code % 2].astype(F32)
    half = STEPS * NP
    k_s[...] = f_s[0:half, :].reshape(STEPS, NP, HD).astype(BF)
    v_s[...] = f_s[half : 2 * half, :].reshape(STEPS, NP, HD).astype(BF)
    tail = pl.ds(SPAN, STEPS)
    copies = [
        pltpu.make_async_copy(k_s, keys.at[tail], sems.at[0]),
        pltpu.make_async_copy(v_s, values.at[tail], sems.at[1]),
    ]
    for c in copies:
        c.start()
    for d in range(NDOM):
        all_s[d : d + 1, :] = jnp.sum(got[d, 2].astype(F32), 0, keepdims=True)
    lane = lax.broadcasted_iota(jnp.int32, (NDOM, HD), 1)
    all_w = jnp.where(lane < NP, all_s[...], -jnp.inf)
    largest = jnp.max(all_w, keepdims=True)
    mass = jnp.sum(jnp.exp(all_w - largest), keepdims=True)
    logw[...] = (line[...] - (largest + jnp.log(mass)))[:, 0:NP]
    for c in copies:
        c.wait()


def finish(idx, line, got, keys, values):
    sd = jax.ShapeDtypeStruct
    return pl.pallas_call(
        finish_body,
        in_specs=[spec(SM)] + [spec(VM)] * 2 + [spec(ANY)] * 2,
        out_specs=[spec(VM)] + [spec(ANY)] * 2,
        out_shape=[sd((1, NP), F32), sd(keys.shape, BF), sd(values.shape, BF)],
        scratch_shapes=[
            VM((NDOM, HD), F32),
            VM((2 * STEPS * NP, HD), F32),
            VM((STEPS, NP, HD), BF),
            VM((STEPS, NP, HD), BF),
            pltpu.SemaphoreType.DMA((2,)),
        ],
        input_output_aliases={3: 1, 4: 2},
        compiler_params=limit(8),
        name="finish",
    )(idx, line, got, keys, values)


def plan_body(me_ref, *refs):
    out, crowd = refs[-2:]
    me = me_ref[0]
    blocks = jnp.concatenate([r[...] for r in refs[:-2]], 0).astype(F32)
    rel = lax.broadcasted_iota(jnp.int32, (NDOM, NDOM), 1)
    back_y = (me // 8 - rel // 8) & 3
    back_x = (me // 2 - rel // 2) & 3
    holder = 8 * back_y + 2 * back_x + ((me + rel) & 1)
    sorted_rows = lax.broadcasted_iota(jnp.int32, (NDOM, NDOM), 0) == holder
    counts = mm(sorted_rows.astype(F32), blocks)
    r16 = lax.broadcasted_iota(jnp.int32, (NP, NP), 0)
    c16 = lax.broadcasted_iota(jnp.int32, (NP, NP), 1)
    within = mm(counts, (r16 <= c16).astype(F32))
    r32 = lax.broadcasted_iota(jnp.int32, (NDOM, NDOM), 0)
    c32 = lax.broadcasted_iota(jnp.int32, (NDOM, NDOM), 1)
    before = jnp.sum(mm((c32 < r32).astype(F32), counts), -1, keepdims=True)
    ends = (within + before).astype(jnp.int32)
    before = before.astype(jnp.int32)
    device = lax.broadcasted_iota(jnp.int32, (NDOM, 1), 0)
    chip_end = jnp.where(device % 2 == 1, ends[:, NP - 1 : NP], -1)
    chip = me // 2
    first = jnp.sum(jnp.where(device == 2 * chip, before, 0))
    lane = lax.broadcasted_iota(jnp.int32, (1, HD), 1)
    dest = 2 * (lane // 4) + me % 2
    sent = first + ((dest - first) & (NDOM - 1)) + NDOM * (lane % 4)
    kept = NDOM * (lane - 64) + me
    found = jnp.zeros((NDOM, HD), jnp.int32)
    for j in range(NP):
        found = found + (ends[:, j : j + 1] <= sent).astype(jnp.int32)
    particle = jnp.sum(found, 0, keepdims=True) - 2 * NP * chip
    particle = jnp.clip(particle, 0, 2 * NP - 1)
    passed = (chip_end >= 0) & (chip_end <= kept)
    source = jnp.sum(passed.astype(jnp.int32), 0, keepdims=True)
    base = jnp.max(jnp.where(passed, chip_end, 0), 0, keepdims=True)
    slot = jnp.clip((kept - base) // NDOM, 0, 3)
    arrived = 4 * jnp.clip(source, 0, NCHIP - 1) + slot
    owned = jnp.sum(counts, -1, keepdims=True).astype(jnp.int32)
    pair = lax.broadcasted_iota(jnp.int32, (NDOM, HD), 1)
    most = jnp.max(jnp.sum(jnp.where(pair == device // 2, owned, 0), 0, keepdims=True))
    line = jnp.where(lane < 64, particle, jnp.where(lane < 80, arrived, most))

    own = jnp.sum(jnp.where(device == me, before, 0))
    sent = own + ((lane // 2 - own) & (NDOM - 1)) + NDOM * (lane % 2)
    found = jnp.zeros((NDOM, HD), jnp.int32)
    for j in range(NP):
        found = found + (ends[:, j : j + 1] <= sent).astype(jnp.int32)
    particle = jnp.sum(found, 0, keepdims=True) - NP * me
    particle = jnp.clip(particle, 0, NP - 1)
    passed = ends[:, NP - 1 : NP] <= kept
    source = jnp.sum(passed.astype(jnp.int32), 0, keepdims=True)
    base = jnp.max(jnp.where(passed, ends[:, NP - 1 : NP], 0), 0, keepdims=True)
    slot = jnp.clip((kept - base) // NDOM, 0, 1)
    arrived = 2 * jnp.clip(source, 0, NDOM - 1) + slot
    second = jnp.where(lane < 64, particle, arrived)
    row = lax.broadcasted_iota(jnp.int32, (8, HD), 0)
    out[...] = jnp.where(row == 0, line, second)
    crowd[0] = most


def plan(me, blocks):
    return pl.pallas_call(
        plan_body,
        in_specs=[spec(SM)] + [spec(VM)] * len(blocks),
        out_specs=[spec(VM), spec(SM)],
        out_shape=[
            jax.ShapeDtypeStruct((8, HD), jnp.int32),
            jax.ShapeDtypeStruct((1,), jnp.int32),
        ],
        compiler_params=limit(8),
        name="plan",
    )(me, *blocks)


def pack_body(me_ref, idx, *refs):
    half = (len(refs) - 3) // 2
    own, partner = (refs[:half], refs[half : 2 * half])
    out, rows, sems = refs[2 * half :]
    core = me_ref[0] % 2
    loads, at = ([], 0)
    for n in range(half):
        length = own[n].shape[1]
        for side, ref in ((core, own[n]), (1 - core, partner[n])):
            there = rows.at[pl.ds(side * NP, NP), pl.ds(at, length), :]
            loads.append(pltpu.make_async_copy(ref, there, sems.at[len(loads) + 1]))
        at += length
    for c in loads:
        c.start()
    for c in loads:
        c.wait()
    for q in range(NCHIP):
        for s in range(SLOTS):
            pltpu.make_async_copy(rows.at[idx[0, 4 * q + s]], out.at[q, s], sems.at[0]).start()
    pltpu.make_async_copy(out, out, sems.at[0]).wait()


def pack(me, idx, own, partner):
    length = sum(a.shape[1] for a in own)
    return pl.pallas_call(
        pack_body,
        in_specs=[spec(SM), spec(SM)] + [spec(ANY)] * (2 * len(own)),
        out_specs=spec(ANY),
        out_shape=jax.ShapeDtypeStruct((NCHIP, SLOTS, length, HD), BF),
        scratch_shapes=[
            VM((2 * NP, length, HD), BF),
            pltpu.SemaphoreType.DMA((1 + 2 * len(own),)),
        ],
        compiler_params=limit(16),
        name="pack",
    )(me, idx, *own, *partner)


def place_body(slots, idx, rows, keys, values, sems):
    copies = []
    for k in range(NP):
        code = idx[0, 64 + k]
        slot = jnp.minimum(code % 4, slots - 1)
        for n, out in enumerate((keys, values)):
            part = rows.at[code // 4, slot, pl.ds(n * SPAN, SPAN), :]
            there = out.at[k, pl.ds(0, SPAN), :]
            copies.append(pltpu.make_async_copy(part, there, sems.at[n, k]))
    for c in copies:
        c.start()
    blank = jnp.zeros((NP, STEPS, HD), BF)
    for out in (keys, values):
        out[:, SPAN : SPAN + STEPS, :] = blank
    for c in copies:
        c.wait()


def place(idx, rows):
    slots = rows.shape[1]
    return pl.pallas_call(
        lambda *refs: place_body(slots, *refs),
        in_specs=[spec(SM), spec(ANY)],
        out_specs=[spec(VM)] * 2,
        out_shape=[jax.ShapeDtypeStruct((NP, SPAN + STEPS, HD), BF)] * 2,
        scratch_shapes=[pltpu.SemaphoreType.DMA((2, NP))],
        compiler_params=limit(16),
        name="place",
    )(idx, rows)


def shifted(value, shift):
    return lax.ppermute(value, "tp", [(i, (i + shift) % TP) for i in range(TP)])


def z_swapped(value):
    return lax.ppermute(value, "tp", [(i, i ^ 1) for i in range(TP)])


def swapped(value):
    return lax.ppermute(value, "dom", [(i, i ^ 1) for i in range(NDOM)])


def next_chip(value):
    return lax.ppermute(value, "dom", [(i, (i + 2) % NDOM) for i in range(NDOM)])


SAME_CORE = [list(range(c, NDOM, 2)) for c in range(2)]


def exchanged(rows):
    return lax.all_to_all(rows, "dom", 0, 0, tiled=True, axis_index_groups=SAME_CORE)


def moved(value, axis_stride, shift):
    def to(i):
        at = i // axis_stride % 4
        return i + ((at + shift) % 4 - at) * axis_stride

    return lax.ppermute(value, "dom", [(i, to(i)) for i in range(NDOM)])


def spread_counts(copy_counts):
    own = copy_counts.reshape(1, NP)
    chip = jnp.concatenate([own, swapped(own)], 0)
    far, near, back = [moved(chip, 2, s) for s in (2, 1, 3)]
    row = jnp.concatenate([chip, near, far, back], 0)
    far, near, back = [moved(row, 8, s) for s in (2, 1, 3)]
    return [row, near, far, back]


def rotation_table():
    frequency = np.float32(500000.0) ** (-2.0 * np.arange(HD // 2, dtype=np.float32) / HD)
    angles = (SPAN + np.arange(STEPS, dtype=np.float32))[:, None] * frequency.astype(np.float32)
    cosine = np.concatenate([np.cos(angles), np.cos(angles)], 1)
    sine = np.concatenate([-np.sin(angles), np.sin(angles)], 1)
    return np.stack([np.repeat(cosine, NP, 0), np.repeat(sine, NP, 0)]).astype(np.float32)


def local(
    activations,
    norm_gain,
    w_query,
    w_key,
    value_weight,
    w_output,
    cache_keys,
    cache_values,
    tokens,
    twisting_table,
    twist_vec,
    previous_log_weights,
    copy_counts,
):
    dom = lax.axis_index("dom")
    tp = lax.axis_index("tp")
    me = dom.reshape(1)
    blk = ((tp + np.arange(TP)) % TP).astype(jnp.int32)
    act = activations.reshape(ROWS, DB)

    gathered = lax.all_to_all(
        jnp.broadcast_to(act[None], (TP, ROWS, DB)), "tp", 0, 0, tiled=True
    )
    idx, crowd = plan(me, spread_counts(copy_counts))
    partner_keys = swapped(cache_keys)
    partner_values = swapped(cache_values)
    packed = pack(me, idx, [cache_keys, cache_values], [partner_keys, partner_values])
    rows = exchanged(packed)

    packed, gathered = lax.optimization_barrier((packed, gathered))
    qa, kf, vf, fresh = project(
        gathered, norm_gain.reshape(TP, DB), w_query, w_key, value_weight, rotation_table()
    )
    partials = attend(blk, qa, kf, vf, cache_keys, cache_values, w_output)
    tokens, *partials = lax.optimization_barrier((tokens, *partials))
    reward = twisting_table[tokens.reshape(ROWS)].astype(F32)
    reward = jnp.pad(reward, (0, HD - ROWS)).reshape(1, HD)
    previous = jnp.pad(previous_log_weights, (0, HD - NP)).reshape(1, HD)
    parts = [partials[0]] + [shifted(partials[s], s) for s in FAR_FIRST]
    attn, sums = mix(parts, act, twist_vec.reshape(1, DB))
    sums = sums + z_swapped(sums)
    all_sums = [sums] + [shifted(sums, s) for s in (4, 2, 6)]
    line, sent = weigh(idx, all_sums, reward, previous, fresh)
    sent, rows = lax.optimization_barrier((sent, rows))
    got = lax.all_to_all(sent, "dom", 0, 0, tiled=True)

    def usual(rows, *_):
        return tuple(place(idx, rows))

    def crowded(rows, partner_keys, partner_values, idx):
        even = dom % 2 == 0
        mine = jnp.concatenate([cache_keys, cache_values], 1)
        other = jnp.concatenate([partner_keys, partner_values], 1)
        chip_rows = jnp.concatenate(
            [jnp.where(even, mine, other), jnp.where(even, other, mine)], 0
        )
        chosen = chip_rows[idx[0, 3:64:4]]
        chip = dom // 2

        def turn(step, state):
            passing, more = state
            passing = next_chip(passing)
            return passing, more.at[(chip - step) % NCHIP].set(passing[chip])

        start = (chosen, chosen)
        more = lax.fori_loop(1, NCHIP, turn, start)[1].at[chip].set(chosen[chip])
        return tuple(place(idx, jnp.concatenate([rows, more[:, None]], 1)))

    old_keys, old_values = lax.cond(
        crowd[0] > SLOTS * NDOM,
        crowded,
        usual,
        rows,
        partner_keys,
        partner_values,
        idx,
    )

    def by_position(old):
        return jnp.transpose(old, (1, 0, 2))

    out_logw, new_keys, new_values = finish(
        idx, line, got, by_position(old_keys), by_position(old_values)
    )
    return (
        attn.reshape(STEPS, NP, DB),
        jnp.transpose(new_keys, (1, 0, 2)),
        jnp.transpose(new_values, (1, 0, 2)),
        out_logw.reshape(NP),
    )


def solution(mesh):
    return jax.shard_map(
        local,
        mesh=mesh,
        in_specs=(
            P(None, "dom", "tp"),
            P(),
            P(None, "tp"),
            P(None, "tp"),
            P(None, "tp"),
            P("tp", None),
            P("dom", None, "tp"),
            P("dom", None, "tp"),
            P(None, "dom"),
            P(),
            P("tp"),
            P("dom"),
            P("dom"),
        ),
        out_specs=(P(None, "dom", "tp"), P("dom", None, "tp"), P("dom", None, "tp"), P("dom")),
        check_vma=False,
    )
```
